32 devices in a mesh: dp: 8 (over z, x), tensor: 4 (over y, core).
Axes of the slice: x: 2, y: 2, z: 4, core: 2. Of those that a mesh axis runs over, the one named last changes fastest.
Arguments:
- tokens: bfloat16 [16384, 1024], P(('dp', 'tensor')), may hold values from -6 to 6
- first_gain: float32 [1024], replicated, may hold values from 0.5 to 1.5
- first_shift: float32 [1024], replicated, may hold values from -2 to 2
- triple_weight: bfloat16 [1024, 3, 1024], P(None, None, 'tensor'), may hold values from -0.1875 to 0.1875
- triple_bias: float32 [3, 1024], P(None, 'tensor'), may hold values from -2 to 2
- merge_weight: bfloat16 [1024, 1024], P('tensor'), may hold values from -6 to 6
- merge_bias: float32 [1024], replicated, may hold values from -2 to 2
- second_gain: float32 [1024], replicated, may hold values from 0.5 to 1.5
- second_shift: float32 [1024], replicated, may hold values from -2 to 2
- up_weight: bfloat16 [1024, 4096], P(None, 'tensor'), may hold values from -0.1875 to 0.1875
- up_bias: float32 [4096], P('tensor'), may hold values from -2 to 2
- down_weight: bfloat16 [4096, 1024], P('tensor'), may hold values from -0.1875 to 0.1875
- down_bias: float32 [1024], replicated, may hold values from -2 to 2
- lengths: int32 [8], P('dp'), may hold values from 1024 to 2048, as said below
- cotangent: bfloat16 [16384, 1024], P(('dp', 'tensor')), may hold values from -8 to 8
Outputs:
- output: bfloat16 [16384, 1024], P(('dp', 'tensor'))
- grad_tokens: float32 [16384, 1024], P(('dp', 'tensor'))
- grad_first_gain: float32 [1024], replicated
- grad_first_shift: float32 [1024], replicated
- grad_triple_weight: float32 [1024, 3, 1024], P(None, None, 'tensor')
- grad_triple_bias: float32 [3, 1024], P(None, 'tensor')
- grad_merge_weight: float32 [1024, 1024], P('tensor')
- grad_merge_bias: float32 [1024], replicated
- grad_second_gain: float32 [1024], replicated
- grad_second_shift: float32 [1024], replicated
- grad_up_weight: float32 [1024, 4096], P(None, 'tensor')
- grad_up_bias: float32 [4096], P('tensor')
- grad_down_weight: float32 [4096, 1024], P('tensor')
- grad_down_bias: float32 [1024], replicated
The draws below stay inside these ranges and needn't reach their ends.
Inputs may be any that keep to these rules, and one draw needn't show every extreme that they name: lengths[s] is the number of real tokens of sequence slot s; the largest entry equals 2048 in every draw.
All inputs are finite; a program needn't handle non-finite values.
Results may differ from the reference program's by a relative error of at most 0.0095.
The reference program's roundings to bfloat16 on the way count: a program that leaves them out, or rounds other values in their place, can miss the bound.
Values may be sent and summed in bfloat16 or wider, within the bound.
A program may use at most 192 MiB of HBM per device.

```python
import jax
import jax.numpy as jnp
from jax import lax

D = 1024
H = 16
HD = 64
FF = 4096
LEN = 2048
SLOTS = 1
NSEQ = 8
TOKENS = 16384


def draw_lengths(key, part):
    base = jax.random.randint(key, (NSEQ,), LEN // 2, LEN + 1)
    chosen = jax.random.randint(jax.random.fold_in(key, 7), (), 0, NSEQ)
    return jnp.where(jnp.arange(NSEQ) == chosen, LEN, base).astype(jnp.int32)


def draw_cotangent(key, part):
    group_rows = SLOTS * LEN
    group_count = TOKENS // group_rows
    row_group = (jnp.arange(TOKENS) // group_rows).astype(jnp.float32)
    ramp = 0.6 + 1.2 * row_group / max(group_count - 1, 1)
    base = jnp.clip(jax.random.normal(key, (TOKENS, D), jnp.float32), -4.0, 4.0)
    return (base * ramp[:, None]).astype(jnp.bfloat16)


def levels(stream_key, extent, shards, low, top_value):
    def one(dim, blocks):
        heights = jax.random.uniform(jax.random.fold_in(jax.random.fold_in(stream_key, 6), dim), (blocks,), jnp.float32, low / len(shards), top_value / len(shards))
        return jnp.repeat(jnp.exp(heights), extent[dim] // blocks).reshape((-1,) + (1,) * (len(extent) - dim - 1))

    gain = one(*shards[0])
    for cut in shards[1:]:
        gain = gain * one(*cut)
    return gain


def bell_draw(stream_key, shape, deviation, limit, shards=(), kind=jnp.bfloat16):
    factor_of = levels(stream_key, shape, shards, -0.22, 0.18) if shards else 1.0
    array = jax.random.normal(stream_key, shape, jnp.float32) * deviation * factor_of
    return jnp.minimum(jnp.maximum(array, -limit), limit).astype(kind)


def setup_inputs(seed: int = 0) -> dict:
    keys = jax.random.split(jax.random.key(seed), 16)
    tokens = bell_draw(keys[0], (TOKENS, D), 1.0, 6.0, ((0, 32),))
    first_gain = jnp.clip(1.0 + 0.1 * jax.random.normal(keys[1], (D,), jnp.float32), 0.5, 1.5)
    first_shift = bell_draw(keys[2], (D,), 0.3, 2.0, (), jnp.float32)
    triple_weight = bell_draw(keys[3], (D, 3, D), D ** -0.5, 0.1875, ((2, 4),))
    triple_bias = bell_draw(keys[4], (3, D), 0.3, 2.0, ((1, 4),), jnp.float32)
    merge_weight = bell_draw(keys[5], (D, D), (max(D // LEN, 1)) ** -0.5, 6.0, ((0, 4),))
    merge_bias = bell_draw(keys[6], (D,), 0.3, 2.0, (), jnp.float32)
    second_gain = jnp.clip(1.0 + 0.1 * jax.random.normal(keys[7], (D,), jnp.float32), 0.5, 1.5)
    second_shift = bell_draw(keys[8], (D,), 0.3, 2.0, (), jnp.float32)
    up_weight = bell_draw(keys[9], (D, FF), D ** -0.5, 0.1875, ((1, 4),))
    up_bias = bell_draw(keys[10], (FF,), 0.3, 2.0, ((0, 4),), jnp.float32)
    down_weight = bell_draw(keys[11], (FF, D), (FF // 4) ** -0.5, 0.1875, ((0, 4),))
    down_bias = bell_draw(keys[12], (D,), 0.3, 2.0, (), jnp.float32)
    lengths = draw_lengths(jax.random.fold_in(keys[15], 71), 0)
    cotangent = draw_cotangent(jax.random.fold_in(keys[15], 71), 0)
    return dict(tokens=tokens, first_gain=first_gain, first_shift=first_shift, triple_weight=triple_weight, triple_bias=triple_bias, merge_weight=merge_weight, merge_bias=merge_bias, second_gain=second_gain, second_shift=second_shift, up_weight=up_weight, up_bias=up_bias, down_weight=down_weight, down_bias=down_bias, lengths=lengths, cotangent=cotangent)


@jax.custom_vjp
def low(v):
    return lax.optimization_barrier(v.astype(jnp.bfloat16)).astype(jnp.float32)

@jax.custom_vjp
def low_back(v):
    return v

def low_keep(v):
    return (low(v), None)

def low_pass(kept, grad):
    return (grad,)

def back_keep(v):
    return (v, None)

def back_low(kept, grad):
    return (low(grad),)
low.defvjp(low_keep, low_pass)
low_back.defvjp(back_keep, back_low)
EPS = 1e-05
MASKED = -1e+30
HIGH = lax.Precision.HIGHEST

def norm_apply(values, scale_vec, shift_vec):
    centred = values - lax.optimization_barrier(jnp.mean(values, axis=-1, keepdims=True))
    inverse = lax.rsqrt(lax.optimization_barrier(jnp.mean(centred * centred, axis=-1, keepdims=True)) + EPS)
    return centred * inverse * scale_vec + shift_vec

def attend_block(query_block, start_row, key_block, value_block, length):
    scores = low_back(jnp.einsum('qhd,khd->hqk', query_block, key_block, precision=HIGH) * HD ** (-0.5))
    query_index = start_row + jnp.arange(query_block.shape[0], dtype=jnp.int32)
    key_index = jnp.arange(LEN, dtype=jnp.int32)
    key_mask = (key_index[None, :] <= query_index[:, None]) & (key_index[None, :] < length)
    query_live = jnp.where(query_index < length, 1.0, 0.0).astype(jnp.float32)
    magnitude = jnp.where(key_mask[None], jnp.abs(scores), MASKED)
    row_max = lax.optimization_barrier(jnp.max(magnitude, axis=-1, keepdims=True))
    exponent = jnp.exp(magnitude - row_max)
    probability = exponent / lax.optimization_barrier(jnp.sum(exponent, axis=-1, keepdims=True))
    weights = low(jnp.sign(scores) * probability * query_live[None, :, None])
    return jnp.einsum('hqk,khd->qhd', weights, value_block, precision=HIGH)

def attend_slot(slot_pack):
    query_slot, key_slot, value_slot, length = slot_pack
    block_rows = min(512, LEN)
    block_count = LEN // block_rows
    query_blocks = query_slot.reshape(block_count, block_rows, H, HD)
    start_rows = jnp.arange(block_count, dtype=jnp.int32) * block_rows

    def block_step(block_item):
        return attend_block(block_item[0], block_item[1], key_slot, value_slot, length)
    result = lax.map(jax.checkpoint(block_step), (query_blocks, start_rows))
    return result.reshape(LEN, H, HD)

def forward(tokens, first_gain, first_shift, triple_weight, triple_bias, merge_weight, merge_bias, second_gain, second_shift, up_weight, up_bias, down_weight, down_bias, lengths):
    first_normed = low(norm_apply(tokens, first_gain, first_shift))
    mixed = jnp.dot(first_normed, triple_weight.reshape(D, 3 * D), precision=HIGH).reshape(TOKENS, 3, D)
    mixed = low(low_back(mixed + triple_bias))
    queries = mixed[:, 0].reshape(NSEQ, LEN, H, HD)
    key_rows = mixed[:, 1].reshape(NSEQ, LEN, H, HD)
    value_rows = mixed[:, 2].reshape(NSEQ, LEN, H, HD)
    attended = lax.map(attend_slot, (queries, key_rows, value_rows, lengths)).reshape(TOKENS, D)
    attended = low(low_back(attended))
    residual = tokens + low_back(jnp.dot(attended, merge_weight, precision=HIGH)) + merge_bias
    second_normed = low(norm_apply(residual, second_gain, second_shift))
    before = low_back(jnp.dot(second_normed, up_weight, precision=HIGH) + up_bias)
    hidden = low(jax.nn.gelu(before, approximate=True))
    return residual + low_back(jnp.dot(hidden, down_weight, precision=HIGH)) + down_bias

def reference(tokens, first_gain, first_shift, triple_weight, triple_bias, merge_weight, merge_bias, second_gain, second_shift, up_weight, up_bias, down_weight, down_bias, lengths, cotangent):
    position = jnp.arange(LEN, dtype=jnp.int32)
    real_mask = jnp.where(position[None, :] < lengths[:, None], 1.0, 0.0).astype(jnp.float32).reshape(TOKENS, 1)
    params = (tokens.astype(jnp.float32), first_gain, first_shift, triple_weight.astype(jnp.float32), triple_bias, merge_weight.astype(jnp.float32), merge_bias, second_gain, second_shift, up_weight.astype(jnp.float32), up_bias, down_weight.astype(jnp.float32), down_bias)

    def run_block(*values):
        return forward(*values, lengths)
    top, pull_back = jax.vjp(run_block, *params)
    grads = pull_back(cotangent.astype(jnp.float32) * real_mask)
    return (top.astype(jnp.bfloat16), grads[0], grads[1], grads[2], grads[3], grads[4], grads[5], grads[6], grads[7], grads[8], grads[9], grads[10], grads[11], grads[12])
```

```python
import functools

import jax
import jax.numpy as jnp
from jax import lax
from jax.experimental import pallas as pl
from jax.experimental.pallas import tpu as pltpu
from jax.sharding import PartitionSpec as P

EPS = 1e-05
HD = 64
LOG2E = 1.4426950408889634
SC = HD ** (-0.5) * LOG2E
BIG = 1e30
NT = (((1,), (1,)), ((), ()))
TN = (((0,), (0,)), ((), ()))
NN = (((1,), (0,)), ((), ()))


def mm(a, b, dims):
    return lax.dot_general(a, b, dims, preferred_element_type=jnp.float32)


def sgn_of(s):
    return jnp.minimum(jnp.maximum(s * BIG, -1.0), 1.0)


def fwd_kernel(bq, bk, len_ref, q_ref, k_ref, v_ref, o_ref, lse_ref, s_sc, v0_sc, v1_sc):
    n = q_ref.shape[0]
    lane = lax.broadcasted_iota(jnp.int32, (1, 128), 1)
    hm = [lane < HD, lane >= HD]
    v_sc = [v0_sc, v1_sc]
    for h in range(2):
        v_sc[h][...] = jnp.where(hm[h], v_ref[...], jnp.zeros_like(v_ref))
    length = len_ref[0]
    row = lax.broadcasted_iota(jnp.int32, (bq, bk), 0)
    col = lax.broadcasted_iota(jnp.int32, (bq, bk), 1)

    def fold(x, op):
        r = x[:, :128]
        for c in range(1, bk // 128):
            r = op(r, x[:, c * 128:(c + 1) * 128])
        return r

    def qblock(i, _):
        q0 = pl.multiple_of(i * bq, bq)
        qb = q_ref[pl.ds(q0, bq), :]
        qh = [jnp.where(hm[h], qb, jnp.zeros_like(qb)) for h in range(2)]
        nfull = q0 // bk

        def p1(j, mx):
            kb = k_ref[pl.ds(pl.multiple_of(j * bk, bk), bk), :]
            out = []
            for h in range(2):
                s = mm(qh[h], kb, NT)
                s_sc[h, j] = s
                out.append(jnp.maximum(mx[h], fold(jnp.abs(s), jnp.maximum)))
            return tuple(out)

        zero = jnp.zeros((bq, 128), jnp.float32)
        mx = lax.fori_loop(0, nfull, p1, (zero, zero))
        kb = k_ref[pl.ds(pl.multiple_of(nfull * bk, bk), bk), :]
        mask = (col + nfull * bk) <= (row + q0)
        mrow = []
        for h in range(2):
            s = mm(qh[h], kb, NT)
            s_sc[h, nfull] = jnp.where(mask, s, 0.0)
            m = jnp.maximum(mx[h], fold(jnp.where(mask, jnp.abs(s), 0.0), jnp.maximum))
            mrow.append(jnp.max(m, axis=1, keepdims=True) * SC)

        def p2(j, carry):
            new = []
            for h in range(2):
                acc, ls = carry[h]
                s = s_sc[h, j]
                p = jnp.exp2(jnp.abs(s) * SC - mrow[h])
                ls = ls + fold(p, jnp.add)
                w = (sgn_of(s) * p).astype(jnp.bfloat16)
                acc = acc + mm(w, v_sc[h][pl.ds(pl.multiple_of(j * bk, bk), bk), :], NN)
                new.append((acc, ls))
            return tuple(new)

        carry = lax.fori_loop(0, nfull, p2, ((zero, zero), (zero, zero)))
        outs = []
        for h in range(2):
            acc, ls = carry[h]
            s = s_sc[h, nfull]
            p = jnp.where(mask, jnp.exp2(jnp.abs(s) * SC - mrow[h]), 0.0)
            ls = ls + fold(p, jnp.add)
            w = (sgn_of(s) * p).astype(jnp.bfloat16)
            acc = acc + mm(w, v_sc[h][pl.ds(pl.multiple_of(nfull * bk, bk), bk), :], NN)
            tot = jnp.sum(ls, axis=1, keepdims=True)
            outs.append(acc / tot)
            lse = jnp.broadcast_to(mrow[h] + jnp.log(tot) * LOG2E, (bq, 128))
            lse_ref[0, h:h + 1, pl.ds(q0, bq)] = jnp.transpose(lse)[0:1, :]
        live = (lax.broadcasted_iota(jnp.int32, (bq, 1), 0) + q0) < length
        o_ref[pl.ds(q0, bq), :] = jnp.where(live, outs[0] + outs[1], 0.0).astype(jnp.bfloat16)
        return 0

    lax.fori_loop(0, n // bq, qblock, 0)


def attend_fwd(mixed, lengths, bq=512, bk=512):
    n = mixed.shape[0]
    width = mixed.shape[1] // 3
    pairs = width // 128
    spec = lambda off: pl.BlockSpec((n, 128), lambda p, off=off: (0, off + p))
    return pl.pallas_call(
        functools.partial(fwd_kernel, bq, bk),
        grid=(pairs,),
        out_shape=(jax.ShapeDtypeStruct((n, width), jnp.bfloat16), jax.ShapeDtypeStruct((pairs, 8, n), jnp.float32)),
        in_specs=[pl.BlockSpec(memory_space=pltpu.SMEM), spec(0), spec(pairs), spec(2 * pairs)],
        out_specs=(pl.BlockSpec((n, 128), lambda p: (0, p)), pl.BlockSpec((1, 8, n), lambda p: (p, 0, 0))),
        scratch_shapes=[pltpu.VMEM((2, n // bk, bq, bk), jnp.float32)] + [pltpu.VMEM((n, 128), jnp.bfloat16)] * 2,
        compiler_params=pltpu.CompilerParams(vmem_limit_bytes=48 << 20),
        cost_estimate=pl.CostEstimate(flops=4 * n * n * width, bytes_accessed=8 * n * width, transcendentals=n * n * width // 128),
        name="attend_fwd",
    )(lengths, mixed, mixed, mixed)


def bwd_kernel(bq, bk, q_ref, k_ref, v_ref, do_ref, o_ref, lse_ref, dq_ref, dk_ref, dv_ref,
               qm, km, dom, dsc, dq_acc):
    n = q_ref.shape[0]
    lane = lax.broadcasted_iota(jnp.int32, (1, 128), 1)
    hm = [lane < HD, lane >= HD]
    for h in range(2):
        for r in range(0, n, 512):
            sl = pl.ds(r, 512)
            z = jnp.zeros((512, 128), jnp.bfloat16)
            qm[h, sl, :] = jnp.where(hm[h], q_ref[sl, :], z)
            km[h, sl, :] = jnp.where(hm[h], k_ref[sl, :], z)
            d = jnp.where(hm[h], do_ref[sl, :], z)
            dom[h, sl, :] = d
            prod = d.astype(jnp.float32) * o_ref[sl, :].astype(jnp.float32)
            dd = jnp.broadcast_to(jnp.sum(prod, axis=1, keepdims=True), (512, 128))
            dsc[h:h + 1, sl] = jnp.transpose(dd)[0:1, :]
    dq_acc[...] = jnp.zeros_like(dq_acc)
    row = lax.broadcasted_iota(jnp.int32, (bk, bq), 0)
    col = lax.broadcasted_iota(jnp.int32, (bk, bq), 1)

    def tile(j, i, dk, dv, diag):
        k0 = pl.multiple_of(j * bk, bk)
        q0 = pl.multiple_of(i * bq, bq)
        ks, qs = pl.ds(k0, bk), pl.ds(q0, bq)
        kb, vb = k_ref[ks, :], v_ref[ks, :]
        dq = None
        for h in range(2):
            qh = qm[h, qs, :]
            doh = dom[h, qs, :]
            s = mm(kb, qh, NT)
            dp = mm(vb, doh, NT)
            p = jnp.exp2(jnp.abs(s) * SC - lse_ref[0, h:h + 1, qs])
            if diag:
                p = jnp.where((row + k0) <= (col + q0), p, 0.0)
            sg = sgn_of(s)
            w = sg * p
            ds = (w * (sg * dp - dsc[h:h + 1, qs])).astype(jnp.bfloat16)
            dv = dv + mm(w.astype(jnp.bfloat16), doh, NN)
            dk = dk + mm(ds, qh, NN)
            t = mm(ds, km[h, ks, :], TN)
            dq = t if dq is None else dq + t
        dq_acc[qs, :] += dq
        return dk, dv

    r = bk // bq
    def kvblock(j, _):
        z = jnp.zeros((bk, 128), jnp.float32)
        dk, dv = z, z
        for a in range(r):
            dk, dv = tile(j, j * r + a, dk, dv, True)
        dk, dv = lax.fori_loop((j + 1) * r, n // bq, lambda i, c: tile(j, i, c[0], c[1], False), (dk, dv))
        ks = pl.ds(pl.multiple_of(j * bk, bk), bk)
        dk_ref[ks, :] = (dk * HD ** (-0.5)).astype(jnp.bfloat16)
        dv_ref[ks, :] = dv.astype(jnp.bfloat16)
        return 0

    lax.fori_loop(0, n // bk, kvblock, 0)
    dq_ref[...] = (dq_acc[...] * HD ** (-0.5)).astype(jnp.bfloat16)


def attend_bwd(mixed, attended, lse, grad, bq=512, bk=512):
    n = mixed.shape[0]
    width = mixed.shape[1] // 3
    pairs = width // 128
    spec = lambda off: pl.BlockSpec((n, 128), lambda p, off=off: (0, off + p))
    o = jax.ShapeDtypeStruct((n, width), jnp.bfloat16)
    return pl.pallas_call(
        functools.partial(bwd_kernel, bq, bk),
        grid=(pairs,),
        out_shape=(o, o, o),
        in_specs=[spec(0), spec(pairs), spec(2 * pairs), spec(0), spec(0), pl.BlockSpec((1, 8, n), lambda p: (p, 0, 0))],
        out_specs=(spec(0),) * 3,
        scratch_shapes=[pltpu.VMEM((2, n, 128), jnp.bfloat16)] * 3 + [pltpu.VMEM((8, n), jnp.float32), pltpu.VMEM((n, 128), jnp.float32)],
        compiler_params=pltpu.CompilerParams(vmem_limit_bytes=48 << 20),
        cost_estimate=pl.CostEstimate(flops=10 * n * n * width, bytes_accessed=16 * n * width, transcendentals=n * n * width // 128),
        name="attend_bwd",
    )(mixed, mixed, mixed, grad, attended, lse)


BF = jnp.bfloat16
F32 = jnp.float32
CHUNKS = 4
VMEM_SPEC = pl.BlockSpec(memory_space=pltpu.VMEM)
SMEM_SPEC = pl.BlockSpec(memory_space=pltpu.SMEM)


def remote(src, dst, send_sem, recv_sem, axis, index):
    return pltpu.make_async_remote_copy(
        src_ref=src,
        dst_ref=dst,
        send_sem=send_sem,
        recv_sem=recv_sem,
        device_id={axis: index},
        device_id_type=pl.DeviceIdType.MESH,
    )


class Group:
    def __init__(self, size):
        self.size = size
        self.chips = size // 2
        self.me = lax.axis_index("tensor")
        self.chip = self.me // 2
        self.core = self.me % 2
        self.sibling = self.chip * 2 + 1 - self.core

    def same(self, off):
        return (self.chip + off) % self.chips * 2 + self.core

    def other(self, off):
        return (self.chip + off) % self.chips * 2 + 1 - self.core

    def greet(self, barrier):
        peers = [self.sibling] + [self.same(off) for off in range(1, self.chips)]
        for peer in peers:
            pl.semaphore_signal(
                barrier, inc=1, device_id={"tensor": peer}, device_id_type=pl.DeviceIdType.MESH
            )
        return len(peers)


def loop(count, body):
    def step(k, carry):
        body(k)
        return carry

    lax.fori_loop(0, count, step, 0)


def loop_range(low, high, body):
    def step(k, carry):
        body(k)
        return carry

    lax.fori_loop(low, high, step, 0)


class Gather:
    def __init__(self, group, buf, sem):
        self.g, self.buf, self.sem = group, buf, sem

    def own(self, off, k):
        g, sem = self.g, self.sem
        here = self.buf.at[g.me, k]
        if off == 0:
            return remote(here, here, sem.at[0, 0, k], sem.at[3, 0, k], "tensor", g.sibling)
        return remote(
            here, here, sem.at[0, off, k], sem.at[2, g.chips - off, k], "tensor", g.same(off)
        )

    def passed(self, off, k):
        here = self.buf.at[self.g.same(off), k]
        sem = self.sem
        return remote(here, here, sem.at[1, off, k], sem.at[3, off, k], "tensor", self.g.sibling)

    def send(self, k):
        for off in list(range(1, self.g.chips)) + [0]:
            self.own(off, k).start()

    def forward(self, k):
        g, sem = self.g, self.sem
        for off in range(1, g.chips):
            here = self.buf.at[g.same(off), k]
            remote(
                here, here, sem.at[0, off, k], sem.at[2, off, k], "tensor", g.same(off)
            ).wait_recv()
            self.passed(off, k).start()

    def wait(self, k):
        g, sem = self.g, self.sem
        for off in range(g.chips):
            here = self.buf.at[g.other(off), k]
            remote(
                here, here, sem.at[0, 0, k], sem.at[3, off, k], "tensor", g.sibling
            ).wait_recv()

    def drain(self, k):
        for off in range(self.g.chips):
            self.own(off, k).wait_send()
            if off:
                self.passed(off, k).wait_send()


class Scatter:
    def __init__(self, group, part, in_near, out_far, in_far, sem):
        self.g, self.part, self.sem = group, part, sem
        self.in_near, self.out_far, self.in_far = in_near, out_far, in_far

    def near(self, off, k):
        sem = self.sem
        return remote(
            self.part.at[self.g.other(off), k], self.in_near.at[off, k], sem.at[0, off, k],
            sem.at[1, off, k], "tensor", self.g.sibling,
        )

    def far(self, off, k):
        g, sem = self.g, self.sem
        back = g.chips - off
        return remote(
            self.out_far.at[off - 1, k], self.in_far.at[back - 1, k], sem.at[2, off, k],
            sem.at[3, back, k], "tensor", g.same(off),
        )

    def send(self, k):
        for off in list(range(1, self.g.chips)) + [0]:
            self.near(off, k).start()

    def combine(self, k):
        g = self.g
        for off in range(1, g.chips):
            self.near(off, k).wait_recv()
            total = self.part[g.same(off), k].astype(F32) + self.in_near[off, k].astype(F32)
            self.out_far[off - 1, k] = total.astype(BF)
            self.far(off, k).start()

    def final(self, k):
        g, sem = self.g, self.sem
        self.near(0, k).wait_recv()
        total = self.part[g.me, k].astype(F32) + self.in_near[0, k].astype(F32)
        for off in range(1, g.chips):
            remote(
                self.out_far.at[off - 1, k], self.in_far.at[off - 1, k], sem.at[2, off, k],
                sem.at[3, off, k], "tensor", g.same(off),
            ).wait_recv()
            total = total + self.in_far[off - 1, k].astype(F32)
        return total

    def drain(self, k):
        for off in range(self.g.chips):
            self.near(off, k).wait_send()
            if off:
                self.far(off, k).wait_send()


def scatter_scratch(size, rows, d):
    chips = size // 2
    block = lambda c: pltpu.VMEM((c, CHUNKS, rows, d), BF)
    return [pltpu.VMEM((size, CHUNKS, rows, d), BF), block(chips), block(chips - 1), block(chips - 1)]


def sems(group):
    return pltpu.SemaphoreType.DMA((4, group // 2, CHUNKS))


class Place:
    def __init__(self, count):
        self.count = count
        self.line = count // 2
        self.me = lax.axis_index("dp")
        self.row = self.me // 2
        self.side = self.me % 2
        self.partner = self.row * 2 + 1 - self.side

    def step(self, off):
        return (self.row + off) % self.line

    def peer(self, off):
        return self.step(off) * 2 + self.side

    def greet(self, barrier):
        peers = [self.partner] + [self.peer(off) for off in range(1, self.line)]
        for peer in peers:
            pl.semaphore_signal(
                barrier, inc=1, device_id={"dp": peer}, device_id_type=pl.DeviceIdType.MESH
            )
        return len(peers)


class Total:
    def __init__(self, place, src, near, half, far, out, sem):
        self.p, self.src, self.near = place, src, near
        self.half, self.far, self.out, self.sem = half, far, out, sem

    def pair(self):
        p, sem = self.p, self.sem
        return remote(
            self.src.at[1 - p.side], self.near, sem.at[0, 0], sem.at[1, 0], "dp", p.partner
        )

    def piece(self, off):
        p, sem = self.p, self.sem
        back = p.line - off
        return remote(
            self.half.at[p.step(off)], self.far.at[back - 1], sem.at[0, off], sem.at[1, back],
            "dp", p.peer(off),
        )

    def start(self):
        self.pair().start()

    def halve(self):
        self.pair().wait_recv()
        for j in range(self.p.line):
            total = self.src[self.p.side, j].astype(F32) + self.near[j].astype(F32)
            self.half[j] = total.astype(BF)
        for off in range(1, self.p.line):
            self.piece(off).start()

    def settle(self):
        p, sem = self.p, self.sem
        total = self.src[p.side, p.row].astype(F32) + self.near[p.row].astype(F32)
        for off in range(1, p.line):
            remote(
                self.half.at[p.row], self.far.at[off - 1], sem.at[0, off], sem.at[1, off],
                "dp", p.peer(off),
            ).wait_recv()
            total = total + self.far[off - 1].astype(F32)
        return total.astype(BF)

    def drain(self):
        self.pair().wait_send()
        for off in range(1, self.p.line):
            self.piece(off).wait_send()


class Share:
    def __init__(self, place, out, sem):
        self.p, self.out, self.sem = place, out, sem

    def piece(self, off):
        p, sem = self.p, self.sem
        here = self.out.at[p.side, p.row]
        return remote(here, here, sem.at[0, off], sem.at[1, p.line - off], "dp", p.peer(off))

    def half(self):
        p, sem = self.p, self.sem
        here = self.out.at[p.side]
        return remote(here, here, sem.at[0, 0], sem.at[1, 0], "dp", p.partner)

    def start(self, piece):
        self.out[self.p.side, self.p.row] = piece
        for off in range(1, self.p.line):
            self.piece(off).start()

    def spread(self):
        p, sem = self.p, self.sem
        for off in range(1, p.line):
            here = self.out.at[p.side, p.step(off)]
            remote(here, here, sem.at[0, off], sem.at[1, off], "dp", p.peer(off)).wait_recv()
        self.half().start()

    def finish(self):
        p, sem = self.p, self.sem
        there = self.out.at[1 - p.side]
        remote(there, there, sem.at[0, 0], sem.at[1, 0], "dp", p.partner).wait_recv()
        for off in range(1, p.line):
            self.piece(off).wait_send()
        self.half().wait_send()


def total_scratch(line, block):
    return [pltpu.VMEM((line,) + block, BF)] * 2 + [
        pltpu.VMEM((line - 1,) + block, BF),
        pltpu.SemaphoreType.DMA((2, line)),
    ]


def norm_stats(x):
    centred = x - jnp.mean(x, axis=-1, keepdims=True)
    inverse = lax.rsqrt(jnp.mean(centred * centred, axis=-1, keepdims=True) + EPS)
    return centred * inverse, inverse


def norm_pull(grad, unit, inverse, gain):
    g = grad * gain
    g = g - jnp.mean(g, axis=-1, keepdims=True) - unit * jnp.mean(g * unit, axis=-1, keepdims=True)
    return g * inverse


def rows_of(ref, k, cols=slice(None)):
    x = ref[:, k, :, cols]
    return x.reshape(x.shape[0] * x.shape[1], x.shape[2])


def col_sum(x):
    return jnp.sum(x, axis=0, keepdims=True)


def enter_kernel(group):
    barrier = pltpu.get_barrier_semaphore()
    pl.semaphore_wait(barrier, group.greet(barrier))


def project_kernel(size, length, tok, cot, gain, shift, w, b, full, mixed, top, sem):
    g = Group(size)
    rows = tok.shape[0] // CHUNKS
    width = w.shape[2]
    enter_kernel(g)
    gather = Gather(g, full, sem)

    def norm(k):
        unit, _ = norm_stats(tok[pl.ds(pl.multiple_of(k * rows, rows), rows), :].astype(F32))
        full[g.me, k] = (unit * gain[...] + shift[...]).astype(BF)
        gather.send(k)

    loop(CHUNKS, norm)

    def mask(k):
        span = pl.ds(pl.multiple_of(k * rows, rows), rows)
        row = lax.broadcasted_iota(jnp.int32, (rows, 1), 0) + (g.me * CHUNKS + k) * rows
        top[span, :] = jnp.where(row < length[0], cot[span, :].astype(F32), 0.0).astype(BF)

    loop(CHUNKS, mask)

    def multiply(k):
        gather.wait(k)
        x = rows_of(full, k)
        for c in range(3):
            cols = slice(c * width, (c + 1) * width)
            y = (mm(x, w[c], NN) + b[:, cols]).astype(BF)
            for s in range(size):
                mixed[s, k, :, cols] = y[s * rows:(s + 1) * rows]

    def body(k):
        gather.forward(k)

        @pl.when(k > 0)
        def _():
            multiply(k - 1)

    loop(CHUNKS, body)
    multiply(CHUNKS - 1)
    loop(CHUNKS, gather.drain)


def project(size, lengths, tokens, cotangent, gain, shift, w, b):
    rows, d = tokens.shape
    r = rows // CHUNKS
    return pl.pallas_call(
        functools.partial(project_kernel, size),
        out_shape=(
            jax.ShapeDtypeStruct((size, CHUNKS, r, d), BF),
            jax.ShapeDtypeStruct((size, CHUNKS, r, 3 * w.shape[2]), BF),
            jax.ShapeDtypeStruct((rows, d), BF),
        ),
        in_specs=[SMEM_SPEC] + [VMEM_SPEC] * 6,
        out_specs=(VMEM_SPEC,) * 3,
        scratch_shapes=[sems(size)],
        compiler_params=pltpu.CompilerParams(
            collective_id=0, has_side_effects=True, vmem_limit_bytes=40 << 20
        ),
        name="project",
    )(lengths, tokens, cotangent, gain, shift, w, b)


def middle_kernel(
    size, count, length, att, tok, cot, mw, mb, gain, shift, up, ub, down,
    gatt, gres, resid, pout, g_up, g_down, g_merge, small, bias, *rest,
):
    pieces, rest = (rest[:2], rest[2:]) if count else ((), rest)
    part, in_near, out_far, in_far, full, gfull, hid, gb, sem1, sem2, sem3, sem4 = rest[:12]
    rest = rest[12:]
    g = Group(size)
    rows, d = tok.shape[0] // CHUNKS, tok.shape[1]
    units = up.shape[1]
    step = min(256, units)
    p = Place(count) if count else None
    barrier = pltpu.get_barrier_semaphore()
    pl.semaphore_wait(barrier, g.greet(barrier) + (p.greet(barrier) if count else 0))
    first = Scatter(g, part, in_near, out_far, in_far, sem1)
    spread = Gather(g, full, sem2)
    second = Scatter(g, part, in_near, out_far, in_far, sem3)
    back = Gather(g, gfull, sem4)
    span = lambda k: pl.ds(pl.multiple_of(k * rows, rows), rows)
    sums = []
    for ref in (g_down, g_up) if count else ():
        for h in range(2):
            near, half, far, sem = rest[:4]
            rest = rest[4:]
            sums.append(Total(p, ref.at[h], near, half, far, None, sem))

    def merge(k):
        y = mm(rows_of(att, k), mw[...], NN).astype(BF)
        for s in range(size):
            part[s, k] = y[s * rows:(s + 1) * rows]
        first.send(k)

    loop(CHUNKS, merge)
    loop(CHUNKS, first.combine)

    def norm(k):
        x = tok[span(k), :].astype(F32) + first.final(k) + mb[...]
        resid[span(k), :] = x
        unit, _ = norm_stats(x)
        full[g.me, k] = (unit * gain[...] + shift[...]).astype(BF)
        spread.send(k)

    loop(CHUNKS, norm)
    loop(CHUNKS, first.drain)
    bias[...] = jnp.zeros_like(bias)

    def enter(k):
        spread.forward(k)
        spread.wait(k)
        x = rows_of(full, k)
        top = rows_of(cot, k)

        def inner(j):
            cols = pl.ds(pl.multiple_of(j * step, step), step)
            v = mm(x, up[:, cols], NN) + ub[:, cols]
            gh = mm(top, down[cols, :], NT)
            c0, c1 = 0.7978845608, 0.044715
            v2 = v * v
            th = jnp.tanh(c0 * (v + c1 * v2 * v))
            half = 0.5 * (1.0 + th)
            h = (v * half).astype(BF)
            slope = half + 0.5 * v * (1.0 - th * th) * (c0 * (1.0 + 3.0 * c1 * v2))
            gv = (gh * slope).astype(BF)
            bias[0:1, cols] += col_sum(gv.astype(F32))
            for s in range(size):
                hid[s, k, :, cols] = h[s * rows:(s + 1) * rows]
                gb[s, k, :, cols] = gv[s * rows:(s + 1) * rows]

        loop(units // step, inner)

    loop(CHUNKS, enter)

    def flat(ref, cols):
        x = ref[:, :, :, cols]
        return x.reshape(size * CHUNKS * rows, x.shape[3])

    def products(ref, left, right, extent):
        tall = min(256, extent)

        def block(i):
            cols = pl.ds(pl.multiple_of(i * tall, tall), tall)
            y = mm(flat(left, cols), flat(right, slice(None)), TN).astype(BF)
            if not count:
                ref[cols, :] = y
            else:
                deep = ref.shape[3]
                for e in range(tall // deep):
                    f = i * (tall // deep) + e
                    ref[f // (2 * p.line), f // p.line % 2, f % p.line] = y[e * deep:(e + 1) * deep]

        return block, extent // tall

    block, blocks = products(g_down, hid, cot, units)
    if count:
        for h in range(2):
            loop_range(h * blocks // 2, (h + 1) * blocks // 2, block)
            sums[h].start()
    else:
        loop(blocks, block)

    def leave(k):
        h, gv = rows_of(hid, k), rows_of(gb, k)

        def outer(j):
            cols = pl.ds(pl.multiple_of(j * 256, 256), 256)
            y = mm(h, down[:, cols], NN).astype(BF)
            z = mm(gv, up[cols, :], NT).astype(BF)
            for s in range(size):
                pout[s, k, :, cols] = y[s * rows:(s + 1) * rows]
                part[s, k, :, cols] = z[s * rows:(s + 1) * rows]

        loop(d // 256, outer)
        second.send(k)

        @pl.when(k > 0)
        def _():
            second.combine(k - 1)

    if count:
        loop_range(0, 3, leave)
        sums[0].halve()
        loop_range(3, CHUNKS, leave)
    else:
        loop(CHUNKS, leave)
    second.combine(CHUNKS - 1)
    block, blocks = products(g_up, full, gb, d)
    if count:
        for h in range(2):
            loop_range(h * blocks // 2, (h + 1) * blocks // 2, block)
            sums[2 + h].start()
        sums[1].halve()
    else:
        loop(blocks, block)
    loop(CHUNKS, spread.drain)
    small[...] = jnp.zeros_like(small)

    def pull(k):
        gs = second.final(k)
        unit, inverse = norm_stats(resid[span(k), :])
        top = cot[g.me, k].astype(F32)
        gr = top + norm_pull(gs, unit, inverse, gain[...])
        gres[span(k), :] = gr
        gfull[g.me, k] = gr.astype(BF)
        back.send(k)
        small[2:3, :] += col_sum(gr)
        small[3:4, :] += col_sum(gs * unit)
        small[4:5, :] += col_sum(gs)
        small[5:6, :] += col_sum(top)

    loop(CHUNKS, pull)
    loop(CHUNKS, second.drain)
    if count:
        sums[2].halve()

    def last(k):
        back.forward(k)
        back.wait(k)
        y = mm(rows_of(gfull, k), mw[...], NT)
        for s in range(size):
            row = lax.broadcasted_iota(jnp.int32, (rows, 1), 0) + (s * CHUNKS + k) * rows
            gatt[s, k] = jnp.where(row < length[0], y[s * rows:(s + 1) * rows], 0.0).astype(BF)

    loop(CHUNKS // 2, last)
    if count:
        sums[3].halve()
    loop_range(CHUNKS // 2, CHUNKS, last)
    block, blocks = products(g_merge, att, gfull, mw.shape[0])
    if count:
        deep = g_merge.shape[2]
        y = mm(flat(att, slice(None)), flat(gfull, slice(None)), TN).astype(BF)
        for f in range(2 * p.line):
            g_merge[f // p.line, f % p.line] = y[f * deep:(f + 1) * deep]
        for h in range(4):
            pieces[h // 2][h % 2] = sums[h].settle()
        for h in range(4):
            sums[h].drain()
    else:
        loop(blocks, block)
    loop(CHUNKS, back.drain)


def middle(size, count, lengths, att, tokens, cot, mw, mb, gain, shift, up, ub, down):
    rows, d = tokens.shape
    r = rows // CHUNKS
    width, units = mw.shape[0], up.shape[1]
    shape = jax.ShapeDtypeStruct
    wide = lambda c: pltpu.VMEM((size, CHUNKS, r, c), BF)
    line = count // 2
    if count:
        grads = (
            shape((2, 2, line, d // (4 * line), units), BF),
            shape((2, 2, line, units // (4 * line), d), BF),
            shape((2, line, width // (2 * line), d), BF),
        )
        extra = (
            shape((2, units // (4 * line), d), BF),
            shape((2, d // (4 * line), units), BF),
        )
        scratch = total_scratch(line, (units // (4 * line), d)) * 2
        scratch += total_scratch(line, (d // (4 * line), units)) * 2
    else:
        grads = (shape((d, units), BF), shape((units, d), BF), shape((width, d), BF))
        extra, scratch = (), []
    outs = (
        shape((size, CHUNKS, r, width), BF),
        shape((rows, d), F32),
        shape((rows, d), F32),
        shape((size, CHUNKS, r, d), BF),
        *grads,
        shape((8, d), F32),
        shape((8, units), F32),
        *extra,
    )
    return pl.pallas_call(
        functools.partial(middle_kernel, size, count),
        out_shape=outs,
        in_specs=[SMEM_SPEC] + [VMEM_SPEC] * 10,
        out_specs=(VMEM_SPEC,) * len(outs),
        scratch_shapes=scatter_scratch(size, r, d)
        + [wide(d), wide(d), wide(units), wide(units)]
        + [sems(size)] * 4
        + scratch,
        compiler_params=pltpu.CompilerParams(
            collective_id=1, has_side_effects=True, vmem_limit_bytes=63 << 20
        ),
        name="middle",
    )(lengths, att, tokens, cot, mw, mb, gain, shift, up, ub, down)


def tail_kernel(
    size, dq, dk, dv, full, w, tok, gres, gain,
    gtok, g_triple, small, bias,
    part, in_near, out_far, in_far, sem,
):
    g = Group(size)
    rows, d = tok.shape[0] // CHUNKS, tok.shape[1]
    width = dq.shape[3]
    enter_kernel(g)
    scatter = Scatter(g, part, in_near, out_far, in_far, sem)
    span = lambda k: pl.ds(pl.multiple_of(k * rows, rows), rows)
    grads = (dq, dk, dv)

    def back(k):
        def tile(j):
            cols = pl.ds(pl.multiple_of(j * 256, 256), 256)
            z = sum(
                mm(rows_of(x, k), w[c, cols, :], NT)
                for c, x in enumerate(grads)
            )
            for s in range(size):
                part[s, k, :, cols] = z[s * rows:(s + 1) * rows].astype(BF)

        loop(d // 256, tile)
        scatter.send(k)

    loop(CHUNKS, back)
    loop(CHUNKS, scatter.combine)

    def flat(ref, cols):
        x = ref[:, :, :, cols]
        return x.reshape(size * CHUNKS * rows, x.shape[3])

    bias[...] = jnp.zeros_like(bias)
    for c, x in enumerate(grads):
        y = flat(x, slice(None))
        bias[0:1, c * width:(c + 1) * width] = col_sum(y.astype(F32))

        def tile(i):
            more = pl.ds(pl.multiple_of(i * 256, 256), 256)
            g_triple[c, more, :] = mm(flat(full, more), y, TN).astype(BF)

        loop(d // 256, tile)
    small[...] = jnp.zeros_like(small)

    def pull(k):
        gf = scatter.final(k)
        unit, inverse = norm_stats(tok[span(k), :].astype(F32))
        gtok[span(k), :] = gres[span(k), :] + norm_pull(gf, unit, inverse, gain[...])
        small[0:1, :] += col_sum(gf * unit)
        small[1:2, :] += col_sum(gf)

    loop(CHUNKS, pull)
    loop(CHUNKS, scatter.drain)


def tail(size, dq, dk, dv, full, w, tokens, gres, gain):
    rows, d = tokens.shape
    r = rows // CHUNKS
    width = dq.shape[-1]
    shape = jax.ShapeDtypeStruct
    return pl.pallas_call(
        functools.partial(tail_kernel, size),
        out_shape=(
            shape((rows, d), F32),
            shape((3, d, width), BF),
            shape((8, d), F32),
            shape((8, 3 * width), F32),
        ),
        in_specs=[VMEM_SPEC] * 8,
        out_specs=(VMEM_SPEC,) * 4,
        scratch_shapes=scatter_scratch(size, r, d) + [sems(size)],
        compiler_params=pltpu.CompilerParams(
            collective_id=2, has_side_effects=True, vmem_limit_bytes=56 << 20
        ),
        name="tail",
    )(dq, dk, dv, full, w, tokens, gres, gain)


class Everyone:
    def __init__(self, axis, count, buf, sem):
        self.axis, self.count, self.buf, self.sem = axis, count, buf, sem
        self.me = lax.axis_index(axis)

    def copy(self, owner, off, back):
        here = self.buf.at[owner]
        return remote(
            here, here, self.sem.at[0, off], self.sem.at[1, back], self.axis,
            (self.me + off) % self.count,
        )

    def start(self, value):
        self.buf[self.me] = value
        for off in range(1, self.count):
            self.copy(self.me, off, self.count - off).start()

    def finish(self):
        for off in range(1, self.count):
            self.copy((self.me + off) % self.count, off, off).wait_recv()
        total = self.buf[0]
        for j in range(1, self.count):
            total = total + self.buf[j]
        for off in range(1, self.count):
            self.copy(self.me, off, self.count - off).wait_send()
        return total


def late_kernel(
    size, count, bk, mixed, att, gatt, lse, full, w, tok, gres, gain, p_down, p_up, g_merge,
    small_in, bias_in,
    gtok, o_down, o_up, o_merge, o_triple, small,
    qm, km, dom, dsc, dq_acc, gm, g_triple, part, in_near, out_far, in_far, sem,
    m_near, m_half, m_far, m_sem, t_near, t_half, t_far, t_sem, s_sem, t_buf, t_sems, d_buf, d_sems,
):
    g, p = Group(size), Place(count)
    n = mixed.shape[0]
    rows, d = tok.shape[0] // CHUNKS, tok.shape[1]
    width = att.shape[1]
    pairs = width // 128
    barrier = pltpu.get_barrier_semaphore()
    for axis, extent in (("tensor", size), ("dp", count)):
        for off in range(1, extent):
            pl.semaphore_signal(
                barrier,
                inc=1,
                device_id={axis: (lax.axis_index(axis) + off) % extent},
                device_id_type=pl.DeviceIdType.MESH,
            )
    pl.semaphore_wait(barrier, size + count - 2)

    shares = [Share(p, ref.at[h], s_sem.at[2 * a + h]) for a, ref in enumerate((o_down, o_up)) for h in range(2)]
    merge_total = Total(p, g_merge, m_near, m_half, m_far, None, m_sem)
    merge_share = Share(p, o_merge, s_sem.at[4])
    totals = [
        Total(p, g_triple.at[x], t_near.at[x], t_half.at[x], t_far.at[x], None, t_sem.at[x])
        for x in range(pairs)
    ]
    triples = [Share(p, o_triple.at[x], s_sem.at[5 + x]) for x in range(pairs)]
    for h in range(4):
        shares[h].start((p_down, p_up)[h // 2][h % 2])
    merge_total.start()

    lane = lax.broadcasted_iota(jnp.int32, (1, 128), 1)
    heads = [lane < HD, lane >= HD]
    row = lax.broadcasted_iota(jnp.int32, (bk, bk), 0)
    col = lax.broadcasted_iota(jnp.int32, (bk, bk), 1)

    def attention(x, events):
        def lanes(c):
            return slice(c * width + x * 128, c * width + (x + 1) * 128)

        def prepare(i):
            sl = pl.ds(pl.multiple_of(i * bk, bk), bk)
            z = jnp.zeros((bk, 128), BF)
            for h in range(2):
                qm[h, sl, :] = jnp.where(heads[h], mixed[sl, lanes(0)], z)
                km[h, sl, :] = jnp.where(heads[h], mixed[sl, lanes(1)], z)
                do = jnp.where(heads[h], gatt[sl, lanes(0)], z)
                dom[h, sl, :] = do
                prod = do.astype(F32) * att[sl, lanes(0)].astype(F32)
                dd = jnp.broadcast_to(jnp.sum(prod, axis=1, keepdims=True), (bk, 128))
                dsc[h:h + 1, sl] = jnp.transpose(dd)[0:1, :]
            dq_acc[sl, :] = jnp.zeros((bk, 128), F32)

        loop(n // bk, prepare)

        def tile(j, i, dk, dv, diag):
            ks, qs = pl.ds(pl.multiple_of(j * bk, bk), bk), pl.ds(pl.multiple_of(i * bk, bk), bk)
            kb, vb = mixed[ks, lanes(1)], mixed[ks, lanes(2)]
            dq = None
            for h in range(2):
                qh, doh = qm[h, qs, :], dom[h, qs, :]
                s = mm(kb, qh, NT)
                dp = mm(vb, doh, NT)
                e = jnp.exp2(jnp.abs(s) * SC - lse[x, h:h + 1, qs])
                if diag:
                    e = jnp.where(row <= col, e, 0.0)
                sg = sgn_of(s)
                a = sg * e
                ds = (a * (sg * dp - dsc[h:h + 1, qs])).astype(BF)
                dv = dv + mm(a.astype(BF), doh, NN)
                dk = dk + mm(ds, qh, NN)
                t = mm(ds, km[h, ks, :], TN)
                dq = t if dq is None else dq + t
            dq_acc[qs, :] += dq
            return dk, dv

        def block(j):
            for at, event in events:
                @pl.when(j == at)
                def _():
                    event()

            z = jnp.zeros((bk, 128), F32)
            dk, dv = tile(j, j, z, z, True)
            dk, dv = lax.fori_loop(
                j + 1, n // bk, lambda i, c: tile(j, i, c[0], c[1], False), (dk, dv)
            )
            ks = pl.ds(pl.multiple_of(j * bk, bk), bk)
            gm[1, ks, x * 128:(x + 1) * 128] = (dk * HD ** (-0.5)).astype(BF)
            gm[2, ks, x * 128:(x + 1) * 128] = dv.astype(BF)

        loop(n // bk, block)
        gm[0, :, x * 128:(x + 1) * 128] = (dq_acc[...] * HD ** (-0.5)).astype(BF)

    def flat(ref, cols):
        y = ref[:, :, :, cols]
        return y.reshape(n, y.shape[3])

    def weights(x):
        y = jnp.concatenate([gm[c, :, x * 128:(x + 1) * 128] for c in range(3)], axis=1)
        deep = g_triple.shape[4]

        def tile(i):
            z = mm(flat(full, pl.ds(pl.multiple_of(i * 256, 256), 256)), y, TN).astype(BF)
            for e in range(256 // deep):
                f = i * (256 // deep) + e
                for c in range(3):
                    g_triple[x, f // p.line, f % p.line, c] = z[
                        e * deep:(e + 1) * deep, c * 128:(c + 1) * 128
                    ]

        loop(d // 256, tile)
        totals[x].start()

    schedule = [[] for _ in range(pairs)]
    schedule[0] = [(2, shares[0].spread), (3, shares[1].spread)]
    schedule[-1] = schedule[-1] + [
        (1, shares[2].spread),
        (2, merge_total.halve),
        (3, shares[3].spread),
    ]
    for x in range(pairs):
        attention(x, schedule[x])
        weights(x)
        if x == 0 and pairs > 1:
            continue
    totals[0].halve()

    scatter = Scatter(g, part, in_near, out_far, in_far, sem)

    def back(k):
        def tile(j):
            cols = pl.ds(pl.multiple_of(j * 256, 256), 256)
            z = 0.0
            for c in range(3):
                y = jnp.concatenate(
                    [
                        gm[c, pl.ds(pl.multiple_of((s * CHUNKS + k) * rows, rows), rows), :]
                        for s in range(size)
                    ],
                    axis=0,
                )
                z = z + mm(y, w[c, cols, :], NT)
            for s in range(size):
                part[s, k, :, cols] = z[s * rows:(s + 1) * rows].astype(BF)

        loop(d // 256, tile)
        scatter.send(k)

    loop(CHUNKS, back)
    loop(CHUNKS, scatter.combine)
    for x in range(1, pairs):
        totals[x].halve()
    merge_share.start(merge_total.settle())
    triples[0].start(totals[0].settle())
    small[...] = small_in[...]
    units = bias_in.shape[1]
    small[6:7, :units] = bias_in[0:1, :]
    for c in range(3):
        small[7:8, c * width:(c + 1) * width] = col_sum(gm[c].astype(F32))
    span = lambda k: pl.ds(pl.multiple_of(k * rows, rows), rows)

    def pull(k):
        gf = scatter.final(k)
        unit, inverse = norm_stats(tok[span(k), :].astype(F32))
        gtok[span(k), :] = gres[span(k), :] + norm_pull(gf, unit, inverse, gain[...])
        small[0:1, :] += col_sum(gf * unit)
        small[1:2, :] += col_sum(gf)

    loop(CHUNKS, pull)
    group_sum = Everyone("tensor", size, t_buf, t_sems)
    group_sum.start(small[...])
    merge_share.spread()
    for x in range(1, pairs):
        triples[x].start(totals[x].settle())
    total = group_sum.finish()
    keep = lax.broadcasted_iota(jnp.int32, (8, 1), 0) < 6
    all_sum = Everyone("dp", count, d_buf, d_sems)
    all_sum.start(jnp.where(keep, total, small[...]))
    triples[0].spread()
    for x in range(1, pairs):
        triples[x].spread()
    small[...] = all_sum.finish()
    for share in shares + [merge_share] + triples:
        share.finish()
    merge_total.drain()
    for t in totals:
        t.drain()
    loop(CHUNKS, scatter.drain)


def late(size, count, mixed, att, gatt, lse, full, w, tokens, gres, gain, p_down, p_up, g_merge,
         small_in, bias_in):
    rows, d = tokens.shape
    n, width = att.shape
    r = rows // CHUNKS
    line = count // 2
    pairs = width // 128
    bk = min(512, n)
    shape = jax.ShapeDtypeStruct
    piece = d // count
    vm = pltpu.VMEM
    dma = pltpu.SemaphoreType.DMA
    deep = g_merge.shape[2]
    units = bias_in.shape[1]
    return pl.pallas_call(
        functools.partial(late_kernel, size, count, bk),
        out_shape=(
            shape((rows, d), F32),
            shape((2, 2, line) + p_down.shape[1:], BF),
            shape((2, 2, line) + p_up.shape[1:], BF),
            shape(g_merge.shape, BF),
            shape((pairs, 2, line, 3, piece, 128), BF),
            shape((8, d), F32),
        ),
        in_specs=[VMEM_SPEC] * 14,
        out_specs=(VMEM_SPEC,) * 6,
        scratch_shapes=[vm((2, n, 128), BF)] * 3
        + [vm((8, n), F32), vm((n, 128), F32), vm((3, n, width), BF)]
        + [vm((pairs, 2, line, 3, piece, 128), BF)]
        + scatter_scratch(size, r, d)
        + [sems(size)]
        + total_scratch(line, (deep, d))
        + [vm((pairs, line, 3, piece, 128), BF)] * 2
        + [vm((pairs, line - 1, 3, piece, 128), BF), dma((pairs, 2, line)), dma((5 + pairs, 2, line))]
        + [vm((size, 8, d), F32), dma((2, size)), vm((count, 8, d), F32), dma((2, count))],
        compiler_params=pltpu.CompilerParams(
            collective_id=3, has_side_effects=True, vmem_limit_bytes=63 << 20
        ),
        name="late",
    )(mixed, att, gatt, lse, full, w, tokens, gres, gain, p_down, p_up, g_merge, small_in, bias_in)


def on_device(
    tokens,
    first_gain,
    first_shift,
    triple_weight,
    triple_bias,
    merge_weight,
    merge_bias,
    second_gain,
    second_shift,
    up_weight,
    up_bias,
    down_weight,
    down_bias,
    lengths,
    cotangent,
):
    size = lax.axis_size("tensor")
    count = lax.axis_size("dp")
    row_count, d = tokens.shape
    rows = row_count // CHUNKS
    width = triple_weight.shape[2]
    units = up_weight.shape[1]
    n = row_count * size
    fused = units % (64 * count) == 0 and width % (8 * count) == 0 and 3 * width <= d and units <= d
    count = count if fused else 0
    line = lambda v: v.reshape(1, -1)
    w = jnp.transpose(triple_weight, (1, 0, 2))
    full, mixed, top = project(
        size, lengths, tokens, cotangent, line(first_gain), line(first_shift), w, line(triple_bias)
    )
    mixed = mixed.reshape(n, 3 * width)
    every_top = lax.all_gather(top, "tensor", axis=0, tiled=True).reshape(size, CHUNKS, rows, d)
    attended, log_total = attend_fwd(mixed, lengths)
    blocks = lambda x: x.reshape(size, CHUNKS, rows, x.shape[-1])
    gatt, gres, resid, pout, g_up, g_down, g_merge, small_b, bias_b, *pieces = middle(
        size, count, lengths, blocks(attended), tokens, every_top, merge_weight, line(merge_bias),
        line(second_gain), line(second_shift), up_weight, line(up_bias), down_weight,
    )
    branch = lax.psum_scatter(pout.reshape(n, d), "tensor", scatter_dimension=0, tiled=True)
    gatt = gatt.reshape(n, width)
    if fused:
        gtok, down, up, merge, triple, small = late(
            size, count, mixed, attended, gatt, log_total, full, w, tokens, gres, line(first_gain),
            pieces[0], pieces[1], g_merge, small_b, bias_b,
        )
        down = down.reshape(units, d).astype(F32)
        up = up.reshape(d, units).astype(F32)
        merge = merge.reshape(width, d).astype(F32)
        triple = jnp.transpose(triple, (1, 2, 4, 3, 0, 5)).reshape(d, 3, width).astype(F32)
        triple_b, up_b = small[7, :3 * width].reshape(3, width), small[6, :units]
    else:
        dq, dk, dv = attend_bwd(mixed, attended, log_total, gatt)
        gtok, g_triple, small_c, bias_c = tail(
            size, blocks(dq), blocks(dk), blocks(dv), full, w, tokens, gres, line(first_gain)
        )
        merge, up, down, triple = lax.psum((g_merge, g_up, g_down, g_triple), "dp")
        triple_b, up_b = lax.psum((bias_c[0], bias_b[0]), "dp")
        small = lax.psum(small_b + small_c, ("dp", "tensor"))
        triple = jnp.transpose(triple, (1, 0, 2)).astype(F32)
        triple_b = triple_b.reshape(3, width)
        merge, up, down = merge.astype(F32), up.astype(F32), down.astype(F32)
    output = (resid + branch.astype(F32) + down_bias).astype(BF)
    return (
        output,
        gtok,
        small[0],
        small[1],
        triple,
        triple_b,
        merge,
        small[2],
        small[3],
        small[4],
        up,
        up_b,
        down,
        small[5],
    )


def solution(mesh):
    in_specs = (
        P(("dp", "tensor"), None),
        P(),
        P(),
        P(None, None, "tensor"),
        P(None, "tensor"),
        P("tensor", None),
        P(),
        P(),
        P(),
        P(None, "tensor"),
        P("tensor"),
        P("tensor", None),
        P(),
        P("dp"),
        P(("dp", "tensor"), None),
    )
    out_specs = (
        P(("dp", "tensor"), None),
        P(("dp", "tensor"), None),
        P(),
        P(),
        P(None, None, "tensor"),
        P(None, "tensor"),
        P("tensor", None),
        P(),
        P(),
        P(),
        P(None, "tensor"),
        P("tensor"),
        P("tensor", None),
        P(),
    )
    return jax.shard_map(
        on_device, mesh=mesh, in_specs=in_specs, out_specs=out_specs, check_vma=False
    )
```

```python
import functools

import jax
import jax.numpy as jnp
from jax import lax
from jax.experimental import pallas as pl
from jax.experimental.pallas import tpu as pltpu
from jax.sharding import PartitionSpec as P

EPS = 1e-05
HD = 64
LOG2E = 1.4426950408889634
SC = HD ** (-0.5) * LOG2E
BIG = 1e30
NT = (((1,), (1,)), ((), ()))
TN = (((0,), (0,)), ((), ()))
NN = (((1,), (0,)), ((), ()))


def mm(a, b, dims):
    return lax.dot_general(a, b, dims, preferred_element_type=jnp.float32)


def sgn_of(s):
    return jnp.minimum(jnp.maximum(s * BIG, -1.0), 1.0)


def bwd_kernel(bq, bk, q_ref, k_ref, v_ref, do_ref, o_ref, lse_ref, dq_ref, dk_ref, dv_ref,
               qm, km, dom, dsc, dq_acc):
    n = q_ref.shape[0]
    lane = lax.broadcasted_iota(jnp.int32, (1, 128), 1)
    hm = [lane < HD, lane >= HD]
    for h in range(2):
        for r in range(0, n, 512):
            sl = pl.ds(r, 512)
            z = jnp.zeros((512, 128), jnp.bfloat16)
            qm[h, sl, :] = jnp.where(hm[h], q_ref[sl, :], z)
            km[h, sl, :] = jnp.where(hm[h], k_ref[sl, :], z)
            d = jnp.where(hm[h], do_ref[sl, :], z)
            dom[h, sl, :] = d
            prod = d.astype(jnp.float32) * o_ref[sl, :].astype(jnp.float32)
            dd = jnp.broadcast_to(jnp.sum(prod, axis=1, keepdims=True), (512, 128))
            dsc[h:h + 1, sl] = jnp.transpose(dd)[0:1, :]
    dq_acc[...] = jnp.zeros_like(dq_acc)
    row = lax.broadcasted_iota(jnp.int32, (bk, bq), 0)
    col = lax.broadcasted_iota(jnp.int32, (bk, bq), 1)

    def tile(j, i, dk, dv, diag):
        k0 = pl.multiple_of(j * bk, bk)
        q0 = pl.multiple_of(i * bq, bq)
        ks, qs = pl.ds(k0, bk), pl.ds(q0, bq)
        kb, vb = k_ref[ks, :], v_ref[ks, :]
        dq = None
        for h in range(2):
            qh = qm[h, qs, :]
            doh = dom[h, qs, :]
            s = mm(kb, qh, NT)
            dp = mm(vb, doh, NT)
            p = jnp.exp2(jnp.abs(s) * SC - lse_ref[0, h:h + 1, qs])
            if diag:
                p = jnp.where((row + k0) <= (col + q0), p, 0.0)
            sg = sgn_of(s)
            w = sg * p
            ds = (w * (sg * dp - dsc[h:h + 1, qs])).astype(jnp.bfloat16)
            dv = dv + mm(w.astype(jnp.bfloat16), doh, NN)
            dk = dk + mm(ds, qh, NN)
            t = mm(ds, km[h, ks, :], TN)
            dq = t if dq is None else dq + t
        dq_acc[qs, :] += dq
        return dk, dv

    r = bk // bq
    def kvblock(j, _):
        z = jnp.zeros((bk, 128), jnp.float32)
        dk, dv = z, z
        for a in range(r):
            dk, dv = tile(j, j * r + a, dk, dv, True)
        dk, dv = lax.fori_loop((j + 1) * r, n // bq, lambda i, c: tile(j, i, c[0], c[1], False), (dk, dv))
        ks = pl.ds(pl.multiple_of(j * bk, bk), bk)
        dk_ref[ks, :] = (dk * HD ** (-0.5)).astype(jnp.bfloat16)
        dv_ref[ks, :] = dv.astype(jnp.bfloat16)
        return 0

    lax.fori_loop(0, n // bk, kvblock, 0)
    dq_ref[...] = (dq_acc[...] * HD ** (-0.5)).astype(jnp.bfloat16)


def attend_bwd(mixed, attended, lse, grad, bq=512, bk=512):
    n = mixed.shape[0]
    width = mixed.shape[1] // 3
    pairs = width // 128
    spec = lambda off: pl.BlockSpec((n, 128), lambda p, off=off: (0, off + p))
    o = jax.ShapeDtypeStruct((n, width), jnp.bfloat16)
    return pl.pallas_call(
        functools.partial(bwd_kernel, bq, bk),
        grid=(pairs,),
        out_shape=(o, o, o),
        in_specs=[spec(0), spec(pairs), spec(2 * pairs), spec(0), spec(0), pl.BlockSpec((1, 8, n), lambda p: (p, 0, 0))],
        out_specs=(spec(0),) * 3,
        scratch_shapes=[pltpu.VMEM((2, n, 128), jnp.bfloat16)] * 3 + [pltpu.VMEM((8, n), jnp.float32), pltpu.VMEM((n, 128), jnp.float32)],
        compiler_params=pltpu.CompilerParams(vmem_limit_bytes=48 << 20),
        cost_estimate=pl.CostEstimate(flops=10 * n * n * width, bytes_accessed=16 * n * width, transcendentals=n * n * width // 128),
        name="attend_bwd",
    )(mixed, mixed, mixed, grad, attended, lse)


BF = jnp.bfloat16
F32 = jnp.float32
CHUNKS = 4
VMEM_SPEC = pl.BlockSpec(memory_space=pltpu.VMEM)
SMEM_SPEC = pl.BlockSpec(memory_space=pltpu.SMEM)


def remote(src, dst, send_sem, recv_sem, axis, index):
    return pltpu.make_async_remote_copy(
        src_ref=src,
        dst_ref=dst,
        send_sem=send_sem,
        recv_sem=recv_sem,
        device_id={axis: index},
        device_id_type=pl.DeviceIdType.MESH,
    )


class Group:
    def __init__(self, size):
        self.size = size
        self.chips = size // 2
        self.me = lax.axis_index("tensor")
        self.chip = self.me // 2
        self.core = self.me % 2
        self.sibling = self.chip * 2 + 1 - self.core

    def same(self, off):
        return (self.chip + off) % self.chips * 2 + self.core

    def other(self, off):
        return (self.chip + off) % self.chips * 2 + 1 - self.core

    def greet(self, barrier):
        peers = [self.sibling] + [self.same(off) for off in range(1, self.chips)]
        for peer in peers:
            pl.semaphore_signal(
                barrier, inc=1, device_id={"tensor": peer}, device_id_type=pl.DeviceIdType.MESH
            )
        return len(peers)


def loop(count, body):
    def step(k, carry):
        body(k)
        return carry

    lax.fori_loop(0, count, step, 0)


def loop_range(low, high, body):
    def step(k, carry):
        body(k)
        return carry

    lax.fori_loop(low, high, step, 0)


class Gather:
    def __init__(self, group, buf, sem):
        self.g, self.buf, self.sem = group, buf, sem

    def own(self, off, k):
        g, sem = self.g, self.sem
        here = self.buf.at[g.me, k]
        if off == 0:
            return remote(here, here, sem.at[0, 0, k], sem.at[3, 0, k], "tensor", g.sibling)
        return remote(
            here, here, sem.at[0, off, k], sem.at[2, g.chips - off, k], "tensor", g.same(off)
        )

    def passed(self, off, k):
        here = self.buf.at[self.g.same(off), k]
        sem = self.sem
        return remote(here, here, sem.at[1, off, k], sem.at[3, off, k], "tensor", self.g.sibling)

    def send(self, k):
        for off in list(range(1, self.g.chips)) + [0]:
            self.own(off, k).start()

    def forward(self, k):
        g, sem = self.g, self.sem
        for off in range(1, g.chips):
            here = self.buf.at[g.same(off), k]
            remote(
                here, here, sem.at[0, off, k], sem.at[2, off, k], "tensor", g.same(off)
            ).wait_recv()
            self.passed(off, k).start()

    def wait(self, k):
        g, sem = self.g, self.sem
        for off in range(g.chips):
            here = self.buf.at[g.other(off), k]
            remote(
                here, here, sem.at[0, 0, k], sem.at[3, off, k], "tensor", g.sibling
            ).wait_recv()

    def drain(self, k):
        for off in range(self.g.chips):
            self.own(off, k).wait_send()
            if off:
                self.passed(off, k).wait_send()


class Scatter:
    def __init__(self, group, part, in_near, out_far, in_far, sem):
        self.g, self.part, self.sem = group, part, sem
        self.in_near, self.out_far, self.in_far = in_near, out_far, in_far

    def near(self, off, k):
        sem = self.sem
        return remote(
            self.part.at[self.g.other(off), k], self.in_near.at[off, k], sem.at[0, off, k],
            sem.at[1, off, k], "tensor", self.g.sibling,
        )

    def far(self, off, k):
        g, sem = self.g, self.sem
        back = g.chips - off
        return remote(
            self.out_far.at[off - 1, k], self.in_far.at[back - 1, k], sem.at[2, off, k],
            sem.at[3, back, k], "tensor", g.same(off),
        )

    def send(self, k):
        for off in list(range(1, self.g.chips)) + [0]:
            self.near(off, k).start()

    def combine(self, k):
        g = self.g
        for off in range(1, g.chips):
            self.near(off, k).wait_recv()
            total = self.part[g.same(off), k].astype(F32) + self.in_near[off, k].astype(F32)
            self.out_far[off - 1, k] = total.astype(BF)
            self.far(off, k).start()

    def final(self, k):
        g, sem = self.g, self.sem
        self.near(0, k).wait_recv()
        total = self.part[g.me, k].astype(F32) + self.in_near[0, k].astype(F32)
        for off in range(1, g.chips):
            remote(
                self.out_far.at[off - 1, k], self.in_far.at[off - 1, k], sem.at[2, off, k],
                sem.at[3, off, k], "tensor", g.same(off),
            ).wait_recv()
            total = total + self.in_far[off - 1, k].astype(F32)
        return total

    def drain(self, k):
        for off in range(self.g.chips):
            self.near(off, k).wait_send()
            if off:
                self.far(off, k).wait_send()


def scatter_scratch(size, rows, d):
    chips = size // 2
    block = lambda c: pltpu.VMEM((c, CHUNKS, rows, d), BF)
    return [pltpu.VMEM((size, CHUNKS, rows, d), BF), block(chips), block(chips - 1), block(chips - 1)]


def sems(group):
    return pltpu.SemaphoreType.DMA((4, group // 2, CHUNKS))


class Place:
    def __init__(self, count):
        self.count = count
        self.line = count // 2
        self.me = lax.axis_index("dp")
        self.row = self.me // 2
        self.side = self.me % 2
        self.partner = self.row * 2 + 1 - self.side

    def step(self, off):
        return (self.row + off) % self.line

    def peer(self, off):
        return self.step(off) * 2 + self.side

    def greet(self, barrier):
        peers = [self.partner] + [self.peer(off) for off in range(1, self.line)]
        for peer in peers:
            pl.semaphore_signal(
                barrier, inc=1, device_id={"dp": peer}, device_id_type=pl.DeviceIdType.MESH
            )
        return len(peers)


class Total:
    def __init__(self, place, src, near, far, sem):
        self.p, self.src, self.near, self.far, self.sem = place, src, near, far, sem

    def pair(self):
        p, sem = self.p, self.sem
        return remote(
            self.src.at[1 - p.side], self.near, sem.at[0, 0], sem.at[1, 0], "dp", p.partner
        )

    def piece(self, off):
        p, sem = self.p, self.sem
        back = p.line - off
        return remote(
            self.near.at[p.step(off)], self.far.at[back - 1], sem.at[0, off], sem.at[1, back],
            "dp", p.peer(off),
        )

    def start(self):
        self.pair().start()

    def add(self):
        self.pair().wait_recv()
        for j in range(self.p.line):
            total = self.src[self.p.side, j].astype(F32) + self.near[j].astype(F32)
            self.near[j] = total.astype(BF)

    def scatter(self):
        for off in range(1, self.p.line):
            self.piece(off).start()

    def halve(self):
        self.add()
        self.scatter()

    def settle(self):
        p, sem = self.p, self.sem
        total = self.near[p.row].astype(F32)
        for off in range(1, p.line):
            remote(
                self.near.at[p.row], self.far.at[off - 1], sem.at[0, off], sem.at[1, off],
                "dp", p.peer(off),
            ).wait_recv()
            total = total + self.far[off - 1].astype(F32)
        return total.astype(BF)

    def drain(self, pair=True, pieces=True):
        if pair:
            self.pair().wait_send()
        for off in range(1, self.p.line) if pieces else ():
            self.piece(off).wait_send()


class Share:
    def __init__(self, place, piece, half, sem):
        self.p, self.piece_at, self.half_at, self.sem = place, piece, half, sem

    def piece(self, off):
        p, sem = self.p, self.sem
        here = self.piece_at(p.side, p.row)
        return remote(here, here, sem.at[0, off], sem.at[1, p.line - off], "dp", p.peer(off))

    def half(self):
        p, sem = self.p, self.sem
        here = self.half_at(p.side)
        return remote(here, here, sem.at[0, 0], sem.at[1, 0], "dp", p.partner)

    def start(self, piece):
        self.piece_at(self.p.side, self.p.row)[...] = piece
        for off in range(1, self.p.line):
            self.piece(off).start()

    def spread(self):
        p, sem = self.p, self.sem
        for off in range(1, p.line):
            here = self.piece_at(p.side, p.step(off))
            remote(here, here, sem.at[0, off], sem.at[1, off], "dp", p.peer(off)).wait_recv()
        self.half().start()

    def finish(self):
        p, sem = self.p, self.sem
        there = self.half_at(1 - p.side)
        remote(there, there, sem.at[0, 0], sem.at[1, 0], "dp", p.partner).wait_recv()
        for off in range(1, p.line):
            self.piece(off).wait_send()
        self.half().wait_send()


def total_scratch(line, block):
    return [
        pltpu.VMEM((line,) + block, BF),
        pltpu.VMEM((line - 1,) + block, BF),
        pltpu.SemaphoreType.DMA((2, line)),
    ]


ANY_SPEC = pl.BlockSpec(memory_space=pl.ANY)


class Move:
    def __init__(self, src, dst, sem):
        self.copy = pltpu.make_async_copy(src, dst, sem)

    def start(self):
        self.copy.start()
        return self

    def wait(self):
        self.copy.wait()


def norm_stats(x):
    centred = x - jnp.mean(x, axis=-1, keepdims=True)
    inverse = lax.rsqrt(jnp.mean(centred * centred, axis=-1, keepdims=True) + EPS)
    return centred * inverse, inverse


def norm_pull(grad, unit, inverse, gain):
    g = grad * gain
    g = g - jnp.mean(g, axis=-1, keepdims=True) - unit * jnp.mean(g * unit, axis=-1, keepdims=True)
    return g * inverse


def rows_of(ref, k, cols=slice(None)):
    x = ref[:, k, :, cols]
    return x.reshape(x.shape[0] * x.shape[1], x.shape[2])


def col_sum(x):
    return jnp.sum(x, axis=0, keepdims=True)


def enter_kernel(group):
    barrier = pltpu.get_barrier_semaphore()
    pl.semaphore_wait(barrier, group.greet(barrier))


def project_kernel(size, tok, gain, shift, w_hbm, b, full_hbm, mixed_hbm, full, mixed, w, sem, w_sem, out_sem):
    g = Group(size)
    rows = tok.shape[0] // CHUNKS
    width = w.shape[2]
    load = Move(w_hbm, w, w_sem).start()
    enter_kernel(g)
    gather = Gather(g, full, sem)

    def norm(k):
        unit, _ = norm_stats(tok[pl.ds(pl.multiple_of(k * rows, rows), rows), :].astype(F32))
        full[g.me, k] = (unit * gain[...] + shift[...]).astype(BF)
        gather.send(k)

    loop(CHUNKS, norm)
    load.wait()

    def stores(k):
        return (
            Move(full.at[:, k], full_hbm.at[:, k], out_sem.at[0, k]),
            Move(mixed.at[:, k], mixed_hbm.at[:, k], out_sem.at[1, k]),
        )

    def multiply(k):
        gather.wait(k)
        x = rows_of(full, k)
        for c in range(3):
            cols = slice(c * width, (c + 1) * width)
            y = (mm(x, w[c], NN) + b[c:c + 1, :]).astype(BF)
            for s in range(size):
                mixed[s, k, :, cols] = y[s * rows:(s + 1) * rows]
        for store in stores(k):
            store.start()

    def body(k):
        gather.forward(k)

        @pl.when(k > 0)
        def _():
            multiply(k - 1)

    loop(CHUNKS, body)
    multiply(CHUNKS - 1)

    def drain(k):
        gather.drain(k)
        for store in stores(k):
            store.wait()

    loop(CHUNKS, drain)


def project(size, tokens, gain, shift, w, b):
    rows, d = tokens.shape
    r = rows // CHUNKS
    shapes = ((size, CHUNKS, r, d), (size, CHUNKS, r, 3 * w.shape[2]))
    dma = pltpu.SemaphoreType.DMA
    return pl.pallas_call(
        functools.partial(project_kernel, size),
        out_shape=tuple(jax.ShapeDtypeStruct(x, BF) for x in shapes),
        in_specs=[VMEM_SPEC] * 3 + [ANY_SPEC, VMEM_SPEC],
        out_specs=(ANY_SPEC,) * 2,
        scratch_shapes=[pltpu.VMEM(x, BF) for x in shapes]
        + [pltpu.VMEM(w.shape, BF), sems(size), dma, dma((2, CHUNKS))],
        compiler_params=pltpu.CompilerParams(
            collective_id=0, has_side_effects=True, vmem_limit_bytes=63 << 20
        ),
        name="project",
    )(tokens, gain, shift, w, b)


def fold(x, op):
    r = x[:, :128]
    for c in range(1, x.shape[1] // 128):
        r = op(r, x[:, c * 128:(c + 1) * 128])
    return r


class Attend:
    def __init__(self, size, units, length, mixed, out, lse, scores, values):
        self.size, self.units, self.length = size, units, length
        self.mixed, self.out, self.lse, self.scores, self.values = mixed, out, lse, scores, values
        self.width = out.shape[-1]
        self.pairs = self.width // 128
        self.block = mixed.shape[0] // size
        self.rows = self.block // units
        lane = lax.broadcasted_iota(jnp.int32, (1, 128), 1)
        self.heads = [lane < HD, lane >= HD]

    def prepare(self):
        for x in range(self.pairs):
            for h in range(2):
                v = self.mixed[:, 2 * self.width + x * 128:2 * self.width + (x + 1) * 128]
                self.values[2 * x + h] = jnp.where(self.heads[h], v, jnp.zeros_like(v))

    def run(self, u, low, high):
        def body(i):
            self.unit(u, i // self.pairs, i % self.pairs)

        loop_range(low * self.pairs, high * self.pairs, body)

    def unit(self, u, s, x):
        bq, bk = self.rows, self.block
        lanes = pl.ds(pl.multiple_of(x * 128, 128), 128)
        k_lanes = pl.ds(pl.multiple_of(self.width + x * 128, 128), 128)
        k0 = pl.multiple_of(s * bk, bk)
        q0 = pl.multiple_of(s * bk + u * bq, bq)
        qb = self.mixed[pl.ds(q0, bq), lanes]
        qh = [jnp.where(self.heads[h], qb, jnp.zeros_like(qb)) for h in range(2)]
        edge = (u + 1) * bq
        row = lax.broadcasted_iota(jnp.int32, (bq, edge), 0) + u * bq
        mask = lax.broadcasted_iota(jnp.int32, (bq, edge), 1) <= row
        zero = jnp.zeros((bq, 128), F32)

        def first(j, most):
            kb = self.mixed[pl.ds(pl.multiple_of(j * bk, bk), bk), k_lanes]
            new = []
            for h in range(2):
                sc = mm(qh[h], kb, NT)
                self.scores[h, j] = sc
                new.append(jnp.maximum(most[h], fold(jnp.abs(sc), jnp.maximum)))
            return tuple(new)

        most = lax.fori_loop(0, s, first, (zero, zero))
        kb = self.mixed[pl.ds(k0, edge), k_lanes]
        top, state = [], []
        for h in range(2):
            sc = jnp.where(mask, mm(qh[h], kb, NT), 0.0)
            m = jnp.maximum(most[h], fold(jnp.abs(sc), jnp.maximum))
            top.append(jnp.max(m, axis=1, keepdims=True) * SC)
            e = jnp.where(mask, jnp.exp2(jnp.abs(sc) * SC - top[h]), 0.0)
            w = (sgn_of(sc) * e).astype(BF)
            state.append((mm(w, self.values[2 * x + h, pl.ds(k0, edge), :], NN), fold(e, jnp.add)))

        def second(j, carry):
            new = []
            for h in range(2):
                acc, total = carry[h]
                sc = self.scores[h, j]
                e = jnp.exp2(jnp.abs(sc) * SC - top[h])
                w = (sgn_of(sc) * e).astype(BF)
                rows = pl.ds(pl.multiple_of(j * bk, bk), bk)
                acc = acc + mm(w, self.values[2 * x + h, rows, :], NN)
                new.append((acc, total + fold(e, jnp.add)))
            return tuple(new)

        state = lax.fori_loop(0, s, second, tuple(state))
        result = 0.0
        for h in range(2):
            total = jnp.sum(state[h][1], axis=1, keepdims=True)
            result = result + state[h][0] / total
            log_total = jnp.broadcast_to(top[h] + jnp.log(total) * LOG2E, (bq, 128))
            self.lse[x, h:h + 1, pl.ds(q0, bq)] = jnp.transpose(log_total)[0:1, :]
        live = (lax.broadcasted_iota(jnp.int32, (bq, 1), 0) + q0) < self.length[0]
        self.out[pl.ds(q0, bq), lanes] = jnp.where(live, result, 0.0).astype(BF)


def core_kernel(
    size, count, length, mb, gain, shift, ub, mixed_hbm, tok_hbm, cot_hbm, mw_hbm, up_hbm, down_hbm,
    att, lse, gatt, gres_hbm, resid_hbm, pout_hbm, g_merge, small, bias, *rest,
):
    if count:
        (pieces, held, rest) = (rest[:3], rest[3], rest[4:])
    else:
        (g_up, g_down, rest) = (rest[0], rest[1], rest[2:])
    (
        mixed, tok, cot, mw, up, down, scores, values, resid, gres, pout, part, in_near, out_far, in_far,
        full, hid, gb, sem1, sem2, sem3, sem4, sem5, load_sem, cot_sem, out_sem, free,
    ) = rest[:27]
    rest = rest[27:]
    g = Group(size)
    rows, d = tok.shape[0] // CHUNKS, tok.shape[1]
    width, units = mw.shape[0], up.shape[1]
    step = min(512, units)
    p = Place(count) if count else None
    span = lambda k: pl.ds(pl.multiple_of(k * rows, rows), rows)
    loads = [
        Move(src, dst, load_sem.at[i]).start()
        for i, (src, dst) in enumerate(
            ((mixed_hbm, mixed), (tok_hbm, tok), (mw_hbm, mw), (up_hbm, up), (down_hbm, down))
        )
    ]
    own = lambda k: Move(cot_hbm.at[k], cot.at[g.me, k], cot_sem.at[k])
    loop(CHUNKS, lambda k: own(k).start())
    barrier = pltpu.get_barrier_semaphore()
    pl.semaphore_wait(barrier, g.greet(barrier) + (p.greet(barrier) if count else 0))
    tops = Gather(g, cot, sem5)
    first = Scatter(g, part, in_near, out_far, in_far, sem1)
    spread = Gather(g, full, sem2)
    second = Scatter(g, part, in_near, out_far, in_far, sem3)
    if units == d:
        gfull = hid
    else:
        gfull, rest = rest[0], rest[1:]
    back = Gather(g, gfull, sem4)
    sums = []
    if count:
        g_up, g_down, rest = rest[0], rest[1], rest[2:]
        for ref in (g_down, g_up):
            for h in range(2):
                near, far, sem = rest[:3]
                rest = rest[3:]
                sums.append(Total(p, ref.at[h], near, far, sem))

    def mask(k):
        own(k).wait()
        row = lax.broadcasted_iota(jnp.int32, (rows, 1), 0) + (g.me * CHUNKS + k) * rows
        cot[g.me, k] = jnp.where(row < length[0], cot[g.me, k].astype(F32), 0.0).astype(BF)
        tops.send(k)

    loop(CHUNKS, mask)
    attend = Attend(size, 2, length, mixed, att, lse, scores, values)
    loads[0].wait()
    attend.prepare()

    def at(s, k):
        return pl.ds(pl.multiple_of((s * CHUNKS + k) * rows, rows), rows)

    def merge(k):
        x = jnp.concatenate([att[at(s, k), :] for s in range(size)], axis=0)
        y = mm(x, mw[...], NN).astype(BF)
        for s in range(size):
            part[s, k] = y[s * rows:(s + 1) * rows]
        first.send(k)

    def resid_store(k):
        return Move(resid.at[span(k)], resid_hbm.at[span(k)], out_sem.at[0, k])

    def norm(k):
        x = tok[span(k), :].astype(F32) + first.final(k) + mb[...]
        resid[span(k), :] = x
        resid_store(k).start()
        unit, _ = norm_stats(x)
        full[g.me, k] = (unit * gain[...] + shift[...]).astype(BF)
        spread.send(k)

    def inner(k):
        spread.forward(k)
        spread.wait(k)
        x = rows_of(full, k)
        top = rows_of(cot, k)

        def tile(j):
            cols = pl.ds(pl.multiple_of(j * step, step), step)
            v = mm(x, up[:, cols], NN) + ub[:, cols]
            gh = mm(top, down[cols, :], NT)
            c0, c1 = 0.7978845608, 0.044715
            v2 = v * v
            th = jnp.tanh(c0 * (v + c1 * v2 * v))
            half = 0.5 * (1.0 + th)
            h = (v * half).astype(BF)
            slope = half + 0.5 * v * (1.0 - th * th) * (c0 * (1.0 + 3.0 * c1 * v2))
            gv = (gh * slope).astype(BF)
            bias[0:1, cols] += col_sum(gv.astype(F32))
            for s in range(size):
                hid[s, k, :, cols] = h[s * rows:(s + 1) * rows]
                gb[s, k, :, cols] = gv[s * rows:(s + 1) * rows]

        loop(units // step, tile)

    def pout_store(k):
        return Move(pout.at[k % 2], pout_hbm.at[:, k], out_sem.at[1, k])

    def leave(k):
        h, gv = rows_of(hid, k), rows_of(gb, k)

        @pl.when(k >= 2)
        def _():
            pout_store(k - 2).wait()

        def tile(j):
            cols = pl.ds(pl.multiple_of(j * 512, 512), 512)
            y = mm(h, down[:, cols], NN).astype(BF)
            z = mm(gv, up[cols, :], NT).astype(BF)
            for s in range(size):
                pout[k % 2, s, :, cols] = y[s * rows:(s + 1) * rows]
                part[s, k, :, cols] = z[s * rows:(s + 1) * rows]

        loop(d // 512, tile)
        pout_store(k).start()
        second.send(k)

    def flat(ref, cols):
        x = ref[:, :, :, cols]
        return x.reshape(size * CHUNKS * rows, x.shape[3])

    def products(ref, left, right, extent):
        tall = min(256, extent)

        def block(i):
            cols = pl.ds(pl.multiple_of(i * tall, tall), tall)
            y = mm(flat(left, cols), flat(right, slice(None)), TN).astype(BF)
            if not count:
                ref[cols, :] = y
            else:
                deep = ref.shape[3]
                for e in range(tall // deep):
                    f = i * (tall // deep) + e
                    ref[f // (2 * p.line), f // p.line % 2, f % p.line] = y[e * deep:(e + 1) * deep]

        return block, extent // tall

    def weights(ref, left, right, extent, pair):
        block, blocks = products(ref, left, right, extent)
        if not count:
            loop(blocks, block)
            return
        for h in range(2):
            loop_range(h * blocks // 2, (h + 1) * blocks // 2, block)
            pair[h].start()

    def gres_store(k):
        return Move(gres.at[k % 2], gres_hbm.at[span(k)], out_sem.at[2, k])

    def pull(k):
        gs = second.final(k)
        unit, inverse = norm_stats(resid[span(k), :])
        top = cot[g.me, k].astype(F32)
        gr = top + norm_pull(gs, unit, inverse, gain[...])

        @pl.when(k >= 2)
        def _():
            gres_store(k - 2).wait()

        gres[k % 2] = gr
        gres_store(k).start()
        gfull[g.me, k] = gr.astype(BF)
        back.send(k)
        small[2:3, :] += col_sum(gr)
        small[3:4, :] += col_sum(gs * unit)
        small[4:5, :] += col_sum(gs)
        small[5:6, :] += col_sum(top)

    def last(k):
        back.forward(k)
        back.wait(k)
        y = mm(rows_of(gfull, k), mw[...], NT)
        for s in range(size):
            row = lax.broadcasted_iota(jnp.int32, (rows, 1), 0) + (s * CHUNKS + k) * rows
            gatt[s, k] = jnp.where(row < length[0], y[s * rows:(s + 1) * rows], 0.0).astype(BF)

    def later(*steps):
        if count:
            for one in steps:
                one()

    bias[...] = jnp.zeros_like(bias)
    small[...] = jnp.zeros_like(small)
    attend.run(0, 0, size)
    for load in loads[1:]:
        load.wait()
    loop(2, merge)
    loop(2, first.combine)
    loop(2, tops.forward)
    attend.run(1, 0, size - 1)
    loop_range(2, CHUNKS, tops.forward)
    loop(2, norm)
    attend.run(1, size - 1, size)
    loop_range(2, CHUNKS, merge)
    loop_range(2, CHUNKS, first.combine)
    loop(CHUNKS, tops.wait)
    loop(2, inner)
    loop(2, first.drain)
    loop(2, leave)
    loop_range(2, CHUNKS, norm)
    loop(2, second.combine)
    loop_range(2, CHUNKS, first.drain)
    loop_range(2, CHUNKS, inner)
    weights(g_down, hid, cot, units, sums[:2])
    peers = g.greet(free)
    loop_range(2, CHUNKS, leave)
    loop_range(2, CHUNKS, second.combine)
    pl.semaphore_wait(free, peers)
    loop(2, pull)
    weights(g_up, full, gb, d, sums[2:])
    later(lambda: sums[0].halve())
    loop(CHUNKS, tops.drain)
    loop(CHUNKS, spread.drain)
    loop_range(2, CHUNKS, pull)
    later(lambda: sums[1].halve())
    loop(2, last)
    later(lambda: sums[2].halve())
    loop_range(2, CHUNKS, last)
    y = mm(att[...], flat(gfull, slice(None)), TN).astype(BF)
    if count:
        deep = g_merge.shape[2]
        for f in range(2 * p.line):
            g_merge[f // p.line, f % p.line] = y[f * deep:(f + 1) * deep]
        for h in range(3):
            pieces[h][...] = sums[h].settle()
        sums[3].add()
        held[...] = sums[3].near[...]
        for h in range(4):
            sums[h].drain(True, h < 3)
    else:
        g_merge[...] = y
    loop(CHUNKS, second.drain)
    loop(CHUNKS, back.drain)
    loop(CHUNKS, lambda k: resid_store(k).wait())
    loop_range(2, CHUNKS, lambda k: pout_store(k).wait())
    loop_range(2, CHUNKS, lambda k: gres_store(k).wait())


def core(size, count, lengths, mixed, mb, gain, shift, ub, tokens, cotangent, mw, up, down):
    rows, d = tokens.shape
    r = rows // CHUNKS
    n = rows * size
    width, units = mw.shape[0], up.shape[1]
    pairs = width // 128
    shape = jax.ShapeDtypeStruct
    dma = pltpu.SemaphoreType.DMA
    vm = pltpu.VMEM
    wide = lambda c: vm((size, CHUNKS, r, c), BF)
    line = count // 2
    if count:
        blocks = ((2, 2, line, d // (4 * line), units), (2, 2, line, units // (4 * line), d))
        merge = shape((2, line, width // (2 * line), d), BF)
        piece = [shape(b[3:], BF) for b in blocks[::-1]]
        extra = (piece[0], piece[0], piece[1], shape((line,) + blocks[0][3:], BF))
        scratch = [vm(b, BF) for b in blocks]
        for b in blocks[::-1]:
            scratch += total_scratch(line, b[3:]) * 2
    else:
        merge = shape((width, d), BF)
        extra = (shape((d, units), BF), shape((units, d), BF))
        scratch = []
    if units != d:
        scratch = [wide(d)] + scratch
    outs = (
        (shape((n, width), BF), VMEM_SPEC),
        (shape((pairs, 8, n), F32), VMEM_SPEC),
        (shape((size, CHUNKS, r, width), BF), VMEM_SPEC),
        (shape((rows, d), F32), ANY_SPEC),
        (shape((rows, d), F32), ANY_SPEC),
        (shape((size, CHUNKS, r, d), BF), ANY_SPEC),
        (merge, VMEM_SPEC),
        (shape((8, d), F32), VMEM_SPEC),
        (shape((8, units), F32), VMEM_SPEC),
        *((x, VMEM_SPEC) for x in extra),
    )
    return pl.pallas_call(
        functools.partial(core_kernel, size, count),
        out_shape=tuple(x for x, _ in outs),
        in_specs=[SMEM_SPEC] + [VMEM_SPEC] * 4 + [ANY_SPEC] * 6,
        out_specs=tuple(x for _, x in outs),
        scratch_shapes=[
            vm(mixed.shape, BF), vm((rows, d), BF), wide(d), vm((width, d), BF), vm((d, units), BF), vm((units, d), BF),
            vm((2, size, rows // 2, rows), F32), vm((2 * pairs, n, 128), BF), vm((rows, d), F32),
            vm((2, r, d), F32), vm((2, size, r, d), BF),
        ]
        + scatter_scratch(size, r, d)
        + [wide(d), wide(units), wide(units)]
        + [sems(size)] * 5
        + [dma((5,)), dma((CHUNKS,)), dma((3, CHUNKS)), pltpu.SemaphoreType.REGULAR]
        + scratch,
        compiler_params=pltpu.CompilerParams(
            collective_id=1, has_side_effects=True, vmem_limit_bytes=64 << 20
        ),
        name="core",
    )(lengths, mb, gain, shift, ub, mixed, tokens, cotangent.reshape(CHUNKS, r, d), mw, up, down)


def tail_kernel(
    size, dq, dk, dv, full, w, tok, gres, gain,
    gtok, g_triple, small, bias,
    part, in_near, out_far, in_far, sem,
):
    g = Group(size)
    rows, d = tok.shape[0] // CHUNKS, tok.shape[1]
    width = dq.shape[3]
    enter_kernel(g)
    scatter = Scatter(g, part, in_near, out_far, in_far, sem)
    span = lambda k: pl.ds(pl.multiple_of(k * rows, rows), rows)
    grads = (dq, dk, dv)

    def back(k):
        def tile(j):
            cols = pl.ds(pl.multiple_of(j * 256, 256), 256)
            z = sum(
                mm(rows_of(x, k), w[c, cols, :], NT)
                for c, x in enumerate(grads)
            )
            for s in range(size):
                part[s, k, :, cols] = z[s * rows:(s + 1) * rows].astype(BF)

        loop(d // 256, tile)
        scatter.send(k)

    loop(CHUNKS, back)
    loop(CHUNKS, scatter.combine)

    def flat(ref, cols):
        x = ref[:, :, :, cols]
        return x.reshape(size * CHUNKS * rows, x.shape[3])

    bias[...] = jnp.zeros_like(bias)
    for c, x in enumerate(grads):
        y = flat(x, slice(None))
        bias[0:1, c * width:(c + 1) * width] = col_sum(y.astype(F32))

        def tile(i):
            more = pl.ds(pl.multiple_of(i * 256, 256), 256)
            g_triple[c, more, :] = mm(flat(full, more), y, TN).astype(BF)

        loop(d // 256, tile)
    small[...] = jnp.zeros_like(small)

    def pull(k):
        gf = scatter.final(k)
        unit, inverse = norm_stats(tok[span(k), :].astype(F32))
        gtok[span(k), :] = gres[span(k), :] + norm_pull(gf, unit, inverse, gain[...])
        small[0:1, :] += col_sum(gf * unit)
        small[1:2, :] += col_sum(gf)

    loop(CHUNKS, pull)
    loop(CHUNKS, scatter.drain)


def tail(size, dq, dk, dv, full, w, tokens, gres, gain):
    rows, d = tokens.shape
    r = rows // CHUNKS
    width = dq.shape[-1]
    shape = jax.ShapeDtypeStruct
    return pl.pallas_call(
        functools.partial(tail_kernel, size),
        out_shape=(
            shape((rows, d), F32),
            shape((3, d, width), BF),
            shape((8, d), F32),
            shape((8, 3 * width), F32),
        ),
        in_specs=[VMEM_SPEC] * 8,
        out_specs=(VMEM_SPEC,) * 4,
        scratch_shapes=scatter_scratch(size, r, d) + [sems(size)],
        compiler_params=pltpu.CompilerParams(
            collective_id=2, has_side_effects=True, vmem_limit_bytes=56 << 20
        ),
        name="tail",
    )(dq, dk, dv, full, w, tokens, gres, gain)


class Everyone:
    def __init__(self, axis, count, buf, sem):
        self.axis, self.count, self.buf, self.sem = axis, count, buf, sem
        self.me = lax.axis_index(axis)

    def copy(self, owner, off, back):
        here = self.buf.at[owner]
        return remote(
            here, here, self.sem.at[0, off], self.sem.at[1, back], self.axis,
            (self.me + off) % self.count,
        )

    def start(self, value):
        self.buf[self.me] = value
        for off in range(1, self.count):
            self.copy(self.me, off, self.count - off).start()

    def finish(self):
        for off in range(1, self.count):
            self.copy((self.me + off) % self.count, off, off).wait_recv()
        total = self.buf[0]
        for j in range(1, self.count):
            total = total + self.buf[j]
        for off in range(1, self.count):
            self.copy(self.me, off, self.count - off).wait_send()
        return total


def late_kernel(
    size, count, bk, gain, db, p_down0, p_down1, p_up0, u_held, g_merge, small_in, bias_in,
    mixed_hbm, att_hbm, gatt_hbm, lse_hbm, full_hbm, w_hbm, tok_hbm, gres_hbm, resid_hbm, pout_hbm,
    out, gtok, o_down, o_up, o_merge, o_triple, small,
    mixed, att, gatt, lse, full, w, tok, gres, resid, pout, load_sem,
    qm, km, dom, dsc, dq_acc, gm, g_triple, part, in_near, out_far, in_far,
    in_near2, out_far2, in_far2, sem, sem2, u_far, u_sem,
    m_near, m_far, m_sem, t_near, t_far, t_sem, s_sem, t_buf, t_sems, d_buf, d_sems,
):
    loads = [
        Move(src, dst, load_sem.at[i]).start()
        for i, (src, dst) in enumerate(
            (
                (mixed_hbm, mixed), (gatt_hbm, gatt), (att_hbm, att), (lse_hbm, lse),
                (pout_hbm, pout), (resid_hbm, resid), (full_hbm, full), (w_hbm, w),
                (tok_hbm, tok), (gres_hbm, gres),
            )
        )
    ]
    g, p = Group(size), Place(count)
    n = mixed.shape[0]
    rows, d = tok.shape[0] // CHUNKS, tok.shape[1]
    width = att.shape[1]
    pairs = width // 128
    barrier = pltpu.get_barrier_semaphore()
    for axis, extent in (("tensor", size), ("dp", count)):
        for off in range(1, extent):
            pl.semaphore_signal(
                barrier,
                inc=1,
                device_id={axis: (lax.axis_index(axis) + off) % extent},
                device_id_type=pl.DeviceIdType.MESH,
            )
    pl.semaphore_wait(barrier, size + count - 2)

    def share(ref, sem):
        return Share(p, lambda side, line: ref.at[side, line], lambda side: ref.at[side], sem)

    def triple_share(x):
        lanes = pl.ds(x * 128, 128)
        return Share(
            p,
            lambda side, line: o_triple.at[:, side, line, :, lanes],
            lambda side: o_triple.at[:, side, :, :, lanes],
            s_sem.at[5 + x],
        )

    shares = [
        share(ref.at[h], s_sem.at[2 * a + h])
        for a, ref in enumerate((o_down, o_up))
        for h in range(2)
    ]
    merge_total = Total(p, g_merge, m_near, m_far, m_sem)
    merge_share = share(o_merge, s_sem.at[4])
    totals = [Total(p, g_triple.at[x], t_near.at[x], t_far.at[x], t_sem.at[x]) for x in range(pairs)]
    triples = [triple_share(x) for x in range(pairs)]
    branch = Scatter(g, pout, in_near2, out_far2, in_far2, sem2)
    up_total = Total(p, None, u_held, u_far, u_sem)
    up_total.scatter()
    for h, piece in enumerate((p_down0, p_down1, p_up0)):
        shares[h].start(piece[...])
    merge_total.start()
    for load in loads[:4]:
        load.wait()

    lane = lax.broadcasted_iota(jnp.int32, (1, 128), 1)
    heads = [lane < HD, lane >= HD]
    row = lax.broadcasted_iota(jnp.int32, (bk, bk), 0)
    col = lax.broadcasted_iota(jnp.int32, (bk, bk), 1)

    def attention(x, events):
        def lanes(c):
            return slice(c * width + x * 128, c * width + (x + 1) * 128)

        def prepare(i):
            sl = pl.ds(pl.multiple_of(i * bk, bk), bk)
            z = jnp.zeros((bk, 128), BF)
            for h in range(2):
                qm[h, sl, :] = jnp.where(heads[h], mixed[sl, lanes(0)], z)
                km[h, sl, :] = jnp.where(heads[h], mixed[sl, lanes(1)], z)
                do = jnp.where(heads[h], gatt[sl, lanes(0)], z)
                dom[h, sl, :] = do
                prod = do.astype(F32) * att[sl, lanes(0)].astype(F32)
                dd = jnp.broadcast_to(jnp.sum(prod, axis=1, keepdims=True), (bk, 128))
                dsc[h:h + 1, sl] = jnp.transpose(dd)[0:1, :]
            dq_acc[sl, :] = jnp.zeros((bk, 128), F32)

        loop(n // bk, prepare)

        def tile(j, i, dk, dv, diag):
            ks, qs = pl.ds(pl.multiple_of(j * bk, bk), bk), pl.ds(pl.multiple_of(i * bk, bk), bk)
            kb, vb = mixed[ks, lanes(1)], mixed[ks, lanes(2)]
            dq = None
            for h in range(2):
                qh, doh = qm[h, qs, :], dom[h, qs, :]
                s = mm(kb, qh, NT)
                dp = mm(vb, doh, NT)
                e = jnp.exp2(jnp.abs(s) * SC - lse[x, h:h + 1, qs])
                if diag:
                    e = jnp.where(row <= col, e, 0.0)
                sg = sgn_of(s)
                a = sg * e
                ds = (a * (sg * dp - dsc[h:h + 1, qs])).astype(BF)
                dv = dv + mm(a.astype(BF), doh, NN)
                dk = dk + mm(ds, qh, NN)
                t = mm(ds, km[h, ks, :], TN)
                dq = t if dq is None else dq + t
            dq_acc[qs, :] += dq
            return dk, dv

        def block(j):
            for at, event in events:
                @pl.when(j == at)
                def _():
                    event()

            z = jnp.zeros((bk, 128), F32)
            dk, dv = tile(j, j, z, z, True)
            dk, dv = lax.fori_loop(
                j + 1, n // bk, lambda i, c: tile(j, i, c[0], c[1], False), (dk, dv)
            )
            ks = pl.ds(pl.multiple_of(j * bk, bk), bk)
            gm[1, ks, x * 128:(x + 1) * 128] = (dk * HD ** (-0.5)).astype(BF)
            gm[2, ks, x * 128:(x + 1) * 128] = dv.astype(BF)

        loop(n // bk, block)
        gm[0, :, x * 128:(x + 1) * 128] = (dq_acc[...] * HD ** (-0.5)).astype(BF)

    def flat(ref, cols):
        y = ref[:, :, :, cols]
        return y.reshape(n, y.shape[3])

    def weights(x):
        y = jnp.concatenate([gm[c, :, x * 128:(x + 1) * 128] for c in range(3)], axis=1)
        deep = g_triple.shape[4]

        def tile(i):
            z = mm(flat(full, pl.ds(pl.multiple_of(i * 256, 256), 256)), y, TN).astype(BF)
            for e in range(256 // deep):
                f = i * (256 // deep) + e
                for c in range(3):
                    g_triple[x, f // p.line, f % p.line, c] = z[
                        e * deep:(e + 1) * deep, c * 128:(c + 1) * 128
                    ]

        loop(d // 256, tile)
        totals[x].start()

    span = lambda k: pl.ds(pl.multiple_of(k * rows, rows), rows)

    def branch_start():
        loads[4].wait()
        loop(CHUNKS, branch.send)

    def branch_end():
        loads[5].wait()

        def one(k):
            out[span(k), :] = (resid[span(k), :] + branch.final(k) + db[...]).astype(BF)

        loop(CHUNKS, one)

    schedule = [[] for _ in range(pairs)]
    schedule[0] = [
        (0, branch_start),
        (1, lambda: loop(CHUNKS, branch.combine)),
        (2, lambda: shares[3].start(up_total.settle())),
    ]
    schedule[-1] = schedule[-1] + [
        (0, shares[0].spread),
        (1, branch_end),
        (1, merge_total.halve),
        (2, shares[1].spread),
        (3, totals[0].halve),
    ]
    for x in range(pairs):
        attention(x, schedule[x])
        if x == 0:
            for load in loads[6:]:
                load.wait()
        weights(x)

    scatter = Scatter(g, part, in_near, out_far, in_far, sem)

    def back(k):
        def tile(j):
            cols = pl.ds(pl.multiple_of(j * 256, 256), 256)
            z = 0.0
            for c in range(3):
                y = jnp.concatenate(
                    [
                        gm[c, pl.ds(pl.multiple_of((s * CHUNKS + k) * rows, rows), rows), :]
                        for s in range(size)
                    ],
                    axis=0,
                )
                z = z + mm(y, w[c, cols, :], NT)
            for s in range(size):
                part[s, k, :, cols] = z[s * rows:(s + 1) * rows].astype(BF)

        loop(d // 256, tile)
        scatter.send(k)

    loop(CHUNKS, back)
    shares[2].spread()
    loop(CHUNKS, scatter.combine)
    shares[3].spread()
    merge_share.start(merge_total.settle())
    for x in range(1, pairs):
        totals[x].halve()
    triples[0].start(totals[0].settle())
    small[...] = small_in[...]
    units = bias_in.shape[1]
    small[6:7, :units] = bias_in[0:1, :]
    for c in range(3):
        small[7:8, c * width:(c + 1) * width] = col_sum(gm[c].astype(F32))

    def pull(k):
        gf = scatter.final(k)
        unit, inverse = norm_stats(tok[span(k), :].astype(F32))
        gtok[span(k), :] = gres[span(k), :] + norm_pull(gf, unit, inverse, gain[...])
        small[0:1, :] += col_sum(gf * unit)
        small[1:2, :] += col_sum(gf)

    loop(CHUNKS, pull)
    group_sum = Everyone("tensor", size, t_buf, t_sems)
    group_sum.start(small[...])
    merge_share.spread()
    for x in range(1, pairs):
        triples[x].start(totals[x].settle())
    total = group_sum.finish()
    keep = lax.broadcasted_iota(jnp.int32, (8, 1), 0) < 6
    all_sum = Everyone("dp", count, d_buf, d_sems)
    all_sum.start(jnp.where(keep, total, small[...]))
    triples[0].spread()
    for x in range(1, pairs):
        triples[x].spread()
    small[...] = all_sum.finish()
    for one in shares + [merge_share] + triples:
        one.finish()
    merge_total.drain()
    up_total.drain(False)
    for t in totals:
        t.drain()
    loop(CHUNKS, scatter.drain)
    loop(CHUNKS, branch.drain)


def late(size, count, gain, db, p_down0, p_down1, p_up0, u_held, g_merge, small_in, bias_in,
         mixed, att, gatt, lse, full, w, tokens, gres, resid, pout):
    rows, d = tokens.shape
    n, width = att.shape
    r = rows // CHUNKS
    line = count // 2
    pairs = width // 128
    bk = min(512, n)
    shape = jax.ShapeDtypeStruct
    piece = d // count
    vm = pltpu.VMEM
    dma = pltpu.SemaphoreType.DMA
    deep = g_merge.shape[2]
    scatter = scatter_scratch(size, r, d)
    loads = (mixed, att, gatt, lse, full, w, tokens, gres, resid, pout)
    return pl.pallas_call(
        functools.partial(late_kernel, size, count, bk),
        out_shape=(
            shape((rows, d), BF),
            shape((rows, d), F32),
            shape((2, 2, line) + p_down0.shape, BF),
            shape((2, 2, line) + p_up0.shape, BF),
            shape(g_merge.shape, BF),
            shape((3, 2, line, piece, width), BF),
            shape((8, d), F32),
        ),
        in_specs=[VMEM_SPEC] * 9 + [ANY_SPEC] * len(loads),
        out_specs=(VMEM_SPEC,) * 7,
        scratch_shapes=[vm(x.shape, x.dtype) for x in loads]
        + [dma((len(loads),))]
        + [vm((2, n, 128), BF)] * 3
        + [vm((8, n), F32), vm((n, 128), F32), vm((3, n, width), BF)]
        + [vm((pairs, 2, line, 3, piece, 128), BF)]
        + scatter
        + scatter[1:]
        + [sems(size)] * 2
        + total_scratch(line, p_up0.shape)[1:]
        + total_scratch(line, (deep, d))
        + [vm((pairs, line, 3, piece, 128), BF), vm((pairs, line - 1, 3, piece, 128), BF)]
        + [dma((pairs, 2, line)), dma((5 + pairs, 2, line))]
        + [vm((size, 8, d), F32), dma((2, size)), vm((count, 8, d), F32), dma((2, count))],
        compiler_params=pltpu.CompilerParams(
            collective_id=3, has_side_effects=True, vmem_limit_bytes=64 << 20
        ),
        name="late",
    )(gain, db, p_down0, p_down1, p_up0, u_held, g_merge, small_in, bias_in, *loads)


def widen_kernel(down, up, merge, triple, small, out, tok, o_down, o_up, o_merge, o_triple, o_out, o_tok, *o_small):
    for src, dst in ((down, o_down), (up, o_up), (merge, o_merge), (triple, o_triple)):
        dst[...] = src[...].astype(F32)
    o_out[...] = out[...]
    o_tok[...] = tok[...]

    @pl.when(pl.program_id(0) == 0)
    def _():
        for i, dst in enumerate(o_small[:7]):
            dst[...] = small[i:i + 1, :dst.shape[1]]
        width = o_small[7].shape[1]
        for c in range(3):
            o_small[7][c:c + 1, :] = small[7:8, c * width:(c + 1) * width]


def widen(down, up, merge, triple, small, out, tok):
    steps = 16
    d, units, width = small.shape[1], up.shape[1], triple.shape[2]

    def spec(x):
        axis = x.ndim - 2
        block = x.shape[:axis] + (x.shape[axis] // steps, x.shape[-1])
        return pl.BlockSpec(block, lambda i: (0,) * axis + (i, 0))

    def whole(shape):
        return pl.BlockSpec(shape, lambda i: (0, 0))

    arrays = (down, up, merge, triple)
    lines = [(1, d)] * 6 + [(1, units), (3, width)]
    outs = [(x.shape, F32, spec(x)) for x in arrays] + [(x.shape, x.dtype, spec(x)) for x in (out, tok)]
    outs += [(x, F32, whole(x)) for x in lines]
    return pl.pallas_call(
        widen_kernel,
        grid=(steps,),
        out_shape=tuple(jax.ShapeDtypeStruct(x, t) for x, t, _ in outs),
        in_specs=[spec(x) for x in arrays] + [whole(small.shape), spec(out), spec(tok)],
        out_specs=tuple(x for _, _, x in outs),
        compiler_params=pltpu.CompilerParams(vmem_limit_bytes=60 << 20),
        name="widen",
    )(down, up, merge, triple, small, out, tok)


def on_device(
    tokens,
    first_gain,
    first_shift,
    triple_weight,
    triple_bias,
    merge_weight,
    merge_bias,
    second_gain,
    second_shift,
    up_weight,
    up_bias,
    down_weight,
    down_bias,
    lengths,
    cotangent,
):
    size = lax.axis_size("tensor")
    count = lax.axis_size("dp")
    row_count, d = tokens.shape
    rows = row_count // CHUNKS
    width = triple_weight.shape[2]
    units = up_weight.shape[1]
    n = row_count * size
    fused = units % (64 * count) == 0 and width % (8 * count) == 0 and 3 * width <= d and units <= d
    count = count if fused else 0
    line = lambda v: v.reshape(1, -1)
    w = jnp.transpose(triple_weight, (1, 0, 2))
    full, mixed = project(
        size, tokens, line(first_gain), line(first_shift), w, triple_bias
    )
    mixed = mixed.reshape(n, 3 * width)
    attended, log_total, gatt, gres, resid, pout, g_merge, small_b, bias_b, *rest = core(
        size, count, lengths, mixed, line(merge_bias), line(second_gain), line(second_shift),
        line(up_bias), tokens, cotangent, merge_weight, up_weight, down_weight,
    )
    gatt = gatt.reshape(n, width)
    if fused:
        output, gtok, down, up, merge, triple, small = late(
            size, count, line(first_gain), line(down_bias), *rest, g_merge, small_b, bias_b,
            mixed, attended, gatt, log_total, full, w, tokens, gres, resid, pout,
        )
        down, up, merge, triple, output, gtok, *small, up_b, triple_b = widen(
            down.reshape(units, d), up.reshape(d, units), merge.reshape(width, d),
            triple.reshape(3, d, width), small, output, gtok,
        )
        triple = jnp.transpose(triple, (1, 0, 2))
        small = [x.reshape(d) for x in small]
        up_b = up_b.reshape(units)
    else:
        branch = lax.psum_scatter(pout.reshape(n, d), "tensor", scatter_dimension=0, tiled=True)
        g_up, g_down = rest
        blocks = lambda x: x.reshape(size, CHUNKS, rows, x.shape[-1])
        dq, dk, dv = attend_bwd(mixed, attended, log_total, gatt)
        gtok, g_triple, small_c, bias_c = tail(
            size, blocks(dq), blocks(dk), blocks(dv), full, w, tokens, gres, line(first_gain)
        )
        merge, up, down, triple = lax.psum((g_merge, g_up, g_down, g_triple), "dp")
        triple_b, up_b = lax.psum((bias_c[0], bias_b[0]), "dp")
        small = lax.psum(small_b + small_c, ("dp", "tensor"))
        triple = jnp.transpose(triple, (1, 0, 2)).astype(F32)
        triple_b = triple_b.reshape(3, width)
        merge, up, down = merge.astype(F32), up.astype(F32), down.astype(F32)
        output = (resid + branch.astype(F32) + down_bias).astype(BF)
    return (
        output,
        gtok,
        small[0],
        small[1],
        triple,
        triple_b,
        merge,
        small[2],
        small[3],
        small[4],
        up,
        up_b,
        down,
        small[5],
    )


def solution(mesh):
    in_specs = (
        P(("dp", "tensor"), None),
        P(),
        P(),
        P(None, None, "tensor"),
        P(None, "tensor"),
        P("tensor", None),
        P(),
        P(),
        P(),
        P(None, "tensor"),
        P("tensor"),
        P("tensor", None),
        P(),
        P("dp"),
        P(("dp", "tensor"), None),
    )
    out_specs = (
        P(("dp", "tensor"), None),
        P(("dp", "tensor"), None),
        P(),
        P(),
        P(None, None, "tensor"),
        P(None, "tensor"),
        P("tensor", None),
        P(),
        P(),
        P(),
        P(None, "tensor"),
        P("tensor"),
        P("tensor", None),
        P(),
    )
    return jax.shard_map(
        on_device, mesh=mesh, in_specs=in_specs, out_specs=out_specs, check_vma=False
    )
```

```python
import functools

import jax
import jax.numpy as jnp
from jax import lax
from jax.experimental import pallas as pl
from jax.experimental.pallas import tpu as pltpu
from jax.sharding import PartitionSpec as P

EPS = 1e-05
HD = 64
LOG2E = 1.4426950408889634
SC = HD ** (-0.5) * LOG2E
BIG = 1e30
NT = (((1,), (1,)), ((), ()))
TN = (((0,), (0,)), ((), ()))
NN = (((1,), (0,)), ((), ()))


def mm(a, b, dims):
    return lax.dot_general(a, b, dims, preferred_element_type=jnp.float32)


def sgn_of(s):
    return jnp.minimum(jnp.maximum(s * BIG, -1.0), 1.0)


def bwd_kernel(bq, bk, q_ref, k_ref, v_ref, do_ref, o_ref, lse_ref, dq_ref, dk_ref, dv_ref,
               qm, km, dom, dsc, dq_acc):
    n = q_ref.shape[0]
    lane = lax.broadcasted_iota(jnp.int32, (1, 128), 1)
    hm = [lane < HD, lane >= HD]
    for h in range(2):
        for r in range(0, n, 512):
            sl = pl.ds(r, 512)
            z = jnp.zeros((512, 128), jnp.bfloat16)
            qm[h, sl, :] = jnp.where(hm[h], q_ref[sl, :], z)
            km[h, sl, :] = jnp.where(hm[h], k_ref[sl, :], z)
            d = jnp.where(hm[h], do_ref[sl, :], z)
            dom[h, sl, :] = d
            prod = d.astype(jnp.float32) * o_ref[sl, :].astype(jnp.float32)
            dd = jnp.broadcast_to(jnp.sum(prod, axis=1, keepdims=True), (512, 128))
            dsc[h:h + 1, sl] = jnp.transpose(dd)[0:1, :]
    dq_acc[...] = jnp.zeros_like(dq_acc)
    row = lax.broadcasted_iota(jnp.int32, (bk, bq), 0)
    col = lax.broadcasted_iota(jnp.int32, (bk, bq), 1)

    def tile(j, i, dk, dv, diag):
        k0 = pl.multiple_of(j * bk, bk)
        q0 = pl.multiple_of(i * bq, bq)
        ks, qs = pl.ds(k0, bk), pl.ds(q0, bq)
        kb, vb = k_ref[ks, :], v_ref[ks, :]
        dq = None
        for h in range(2):
            qh = qm[h, qs, :]
            doh = dom[h, qs, :]
            s = mm(kb, qh, NT)
            dp = mm(vb, doh, NT)
            p = jnp.exp2(jnp.abs(s) * SC - lse_ref[0, h:h + 1, qs])
            if diag:
                p = jnp.where((row + k0) <= (col + q0), p, 0.0)
            sg = sgn_of(s)
            w = sg * p
            ds = (w * (sg * dp - dsc[h:h + 1, qs])).astype(jnp.bfloat16)
            dv = dv + mm(w.astype(jnp.bfloat16), doh, NN)
            dk = dk + mm(ds, qh, NN)
            t = mm(ds, km[h, ks, :], TN)
            dq = t if dq is None else dq + t
        dq_acc[qs, :] += dq
        return dk, dv

    r = bk // bq
    def kvblock(j, _):
        z = jnp.zeros((bk, 128), jnp.float32)
        dk, dv = z, z
        for a in range(r):
            dk, dv = tile(j, j * r + a, dk, dv, True)
        dk, dv = lax.fori_loop((j + 1) * r, n // bq, lambda i, c: tile(j, i, c[0], c[1], False), (dk, dv))
        ks = pl.ds(pl.multiple_of(j * bk, bk), bk)
        dk_ref[ks, :] = (dk * HD ** (-0.5)).astype(jnp.bfloat16)
        dv_ref[ks, :] = dv.astype(jnp.bfloat16)
        return 0

    lax.fori_loop(0, n // bk, kvblock, 0)
    dq_ref[...] = (dq_acc[...] * HD ** (-0.5)).astype(jnp.bfloat16)


def attend_bwd(mixed, attended, lse, grad, bq=512, bk=512):
    n = mixed.shape[0]
    width = mixed.shape[1] // 3
    pairs = width // 128
    spec = lambda off: pl.BlockSpec((n, 128), lambda p, off=off: (0, off + p))
    o = jax.ShapeDtypeStruct((n, width), jnp.bfloat16)
    return pl.pallas_call(
        functools.partial(bwd_kernel, bq, bk),
        grid=(pairs,),
        out_shape=(o, o, o),
        in_specs=[spec(0), spec(pairs), spec(2 * pairs), spec(0), spec(0), pl.BlockSpec((1, 8, n), lambda p: (p, 0, 0))],
        out_specs=(spec(0),) * 3,
        scratch_shapes=[pltpu.VMEM((2, n, 128), jnp.bfloat16)] * 3 + [pltpu.VMEM((8, n), jnp.float32), pltpu.VMEM((n, 128), jnp.float32)],
        compiler_params=pltpu.CompilerParams(vmem_limit_bytes=48 << 20),
        cost_estimate=pl.CostEstimate(flops=10 * n * n * width, bytes_accessed=16 * n * width, transcendentals=n * n * width // 128),
        name="attend_bwd",
    )(mixed, mixed, mixed, grad, attended, lse)


BF = jnp.bfloat16
F32 = jnp.float32
CHUNKS = 4
VMEM_SPEC = pl.BlockSpec(memory_space=pltpu.VMEM)
SMEM_SPEC = pl.BlockSpec(memory_space=pltpu.SMEM)


def remote(src, dst, send_sem, recv_sem, axis, index):
    return pltpu.make_async_remote_copy(
        src_ref=src,
        dst_ref=dst,
        send_sem=send_sem,
        recv_sem=recv_sem,
        device_id={axis: index},
        device_id_type=pl.DeviceIdType.MESH,
    )


class Group:
    def __init__(self, size):
        self.size = size
        self.chips = size // 2
        self.me = lax.axis_index("tensor")
        self.chip = self.me // 2
        self.core = self.me % 2
        self.sibling = self.chip * 2 + 1 - self.core

    def same(self, off):
        return (self.chip + off) % self.chips * 2 + self.core

    def other(self, off):
        return (self.chip + off) % self.chips * 2 + 1 - self.core

    def greet(self, barrier):
        peers = [self.sibling] + [self.same(off) for off in range(1, self.chips)]
        for peer in peers:
            pl.semaphore_signal(
                barrier, inc=1, device_id={"tensor": peer}, device_id_type=pl.DeviceIdType.MESH
            )
        return len(peers)


def loop(count, body):
    def step(k, carry):
        body(k)
        return carry

    lax.fori_loop(0, count, step, 0)


def loop_range(low, high, body):
    def step(k, carry):
        body(k)
        return carry

    lax.fori_loop(low, high, step, 0)


class Gather:
    def __init__(self, group, buf, sem):
        self.g, self.buf, self.sem = group, buf, sem

    def own(self, off, k):
        g, sem = self.g, self.sem
        here = self.buf.at[g.me, k]
        if off == 0:
            return remote(here, here, sem.at[0, 0, k], sem.at[3, 0, k], "tensor", g.sibling)
        return remote(
            here, here, sem.at[0, off, k], sem.at[2, g.chips - off, k], "tensor", g.same(off)
        )

    def passed(self, off, k):
        here = self.buf.at[self.g.same(off), k]
        sem = self.sem
        return remote(here, here, sem.at[1, off, k], sem.at[3, off, k], "tensor", self.g.sibling)

    def send(self, k):
        for off in list(range(1, self.g.chips)) + [0]:
            self.own(off, k).start()

    def forward(self, k):
        g, sem = self.g, self.sem
        for off in range(1, g.chips):
            here = self.buf.at[g.same(off), k]
            remote(
                here, here, sem.at[0, off, k], sem.at[2, off, k], "tensor", g.same(off)
            ).wait_recv()
            self.passed(off, k).start()

    def wait(self, k):
        g, sem = self.g, self.sem
        for off in range(g.chips):
            here = self.buf.at[g.other(off), k]
            remote(
                here, here, sem.at[0, 0, k], sem.at[3, off, k], "tensor", g.sibling
            ).wait_recv()

    def drain(self, k):
        for off in range(self.g.chips):
            self.own(off, k).wait_send()
            if off:
                self.passed(off, k).wait_send()


class Scatter:
    def __init__(self, group, part, in_near, out_far, in_far, sem):
        self.g, self.part, self.sem = group, part, sem
        self.in_near, self.out_far, self.in_far = in_near, out_far, in_far

    def near(self, off, k):
        sem = self.sem
        return remote(
            self.part.at[self.g.other(off), k], self.in_near.at[off, k], sem.at[0, off, k],
            sem.at[1, off, k], "tensor", self.g.sibling,
        )

    def far(self, off, k):
        g, sem = self.g, self.sem
        back = g.chips - off
        return remote(
            self.out_far.at[off - 1, k], self.in_far.at[back - 1, k], sem.at[2, off, k],
            sem.at[3, back, k], "tensor", g.same(off),
        )

    def send(self, k):
        for off in list(range(1, self.g.chips)) + [0]:
            self.near(off, k).start()

    def combine(self, k):
        g = self.g
        for off in range(1, g.chips):
            self.near(off, k).wait_recv()
            total = self.part[g.same(off), k].astype(F32) + self.in_near[off, k].astype(F32)
            self.out_far[off - 1, k] = total.astype(BF)
            self.far(off, k).start()

    def final(self, k):
        g, sem = self.g, self.sem
        self.near(0, k).wait_recv()
        total = self.part[g.me, k].astype(F32) + self.in_near[0, k].astype(F32)
        for off in range(1, g.chips):
            remote(
                self.out_far.at[off - 1, k], self.in_far.at[off - 1, k], sem.at[2, off, k],
                sem.at[3, off, k], "tensor", g.same(off),
            ).wait_recv()
            total = total + self.in_far[off - 1, k].astype(F32)
        return total

    def drain(self, k):
        for off in range(self.g.chips):
            self.near(off, k).wait_send()
            if off:
                self.far(off, k).wait_send()


def scatter_scratch(size, rows, d):
    chips = size // 2
    block = lambda c: pltpu.VMEM((c, CHUNKS, rows, d), BF)
    return [pltpu.VMEM((size, CHUNKS, rows, d), BF), block(chips), block(chips - 1), block(chips - 1)]


def sems(group):
    return pltpu.SemaphoreType.DMA((4, group // 2, CHUNKS))


class Place:
    def __init__(self, count):
        self.count = count
        self.line = count // 2
        self.me = lax.axis_index("dp")
        self.row = self.me // 2
        self.side = self.me % 2
        self.partner = self.row * 2 + 1 - self.side
        self.next = self.row + 1 - self.row % 2 * 2
        self.inner = self.next % 3 == 0

    def at(self, row):
        return row * 2 + self.side

    def peer(self, off):
        return self.at((self.row + off) % self.line)

    def greet(self, barrier):
        peers = [self.partner] + [self.peer(off) for off in range(1, self.line)]
        for peer in peers:
            pl.semaphore_signal(
                barrier, inc=1, device_id={"dp": peer}, device_id_type=pl.DeviceIdType.MESH
            )
        return len(peers)


class Total:
    def __init__(self, place, src, near, far, sem):
        self.p, self.src, self.near, self.far, self.sem = place, src, near, far, sem

    def pair(self):
        p, sem = self.p, self.sem
        return remote(
            self.src.at[1 - p.side], self.near, sem.at[0, 0], sem.at[1, 0], "dp", p.partner
        )

    def outward(self):
        p, sem = self.p, self.sem
        return remote(
            self.near.at[pl.ds(1 - p.row // 3, 3)], self.far.at[pl.ds(0, 3)], sem.at[0, 1],
            sem.at[1, 1], "dp", p.at(p.next),
        )

    def inward(self):
        p, sem = self.p, self.sem
        return remote(
            self.near.at[p.next], self.far.at[0], sem.at[0, 1], sem.at[1, 1], "dp", p.at(p.next)
        )

    def summed(self, i):
        p, sem = self.p, self.sem
        target = (3 - p.row, 3 - p.next)[i]
        return remote(
            self.near.at[target], self.far.at[3], sem.at[0, 2 + i], sem.at[1, 2], "dp", p.at(target)
        )

    def start(self):
        self.pair().start()

    def add(self):
        self.pair().wait_recv()
        for j in range(self.p.line):
            total = self.src[self.p.side, j].astype(F32) + self.near[j].astype(F32)
            self.near[j] = total.astype(BF)

    def scatter(self):
        @pl.when(self.p.inner)
        def _():
            self.inward().start()

        @pl.when(jnp.logical_not(self.p.inner))
        def _():
            self.outward().start()

    def halve(self):
        self.add()
        self.scatter()

    def relay(self):
        p = self.p

        @pl.when(p.inner)
        def _():
            self.outward().wait_recv()
            skip = 2 - p.row
            for i, target in enumerate((3 - p.row, 3 - p.next)):
                total = self.near[target].astype(F32) + self.far[target - skip].astype(F32)
                self.near[target] = total.astype(BF)
                self.summed(i).start()
            total = self.near[p.row].astype(F32) + self.far[p.row - skip].astype(F32)
            self.near[p.row] = total.astype(BF)

        @pl.when(jnp.logical_not(p.inner))
        def _():
            self.inward().wait_recv()
            total = self.near[p.row].astype(F32) + self.far[0].astype(F32)
            self.near[p.row] = total.astype(BF)

    def settle(self):
        self.summed(0).wait_recv()
        return (self.near[self.p.row].astype(F32) + self.far[3].astype(F32)).astype(BF)

    def drain(self, pair=True, pieces=True):
        if pair:
            self.pair().wait_send()
        if not pieces:
            return

        @pl.when(self.p.inner)
        def _():
            self.inward().wait_send()
            self.summed(0).wait_send()
            self.summed(1).wait_send()

        @pl.when(jnp.logical_not(self.p.inner))
        def _():
            self.outward().wait_send()


class Share:
    def __init__(self, place, piece, half, sem):
        self.p, self.piece_at, self.half_at, self.sem = place, piece, half, sem

    def piece(self, i, owner, target):
        p, sem = self.p, self.sem
        here = self.piece_at(p.side, owner)
        return remote(here, here, sem.at[0, i], sem.at[1, owner], "dp", p.at(target))

    def first(self):
        p = self.p
        second = jnp.where(p.inner, 3 - p.row, 3 - p.next)
        return self.piece(0, p.row, p.next), self.piece(1, p.row, second)

    def passed(self):
        p = self.p
        return self.piece(2, 3 - p.row, p.next), self.piece(3, 3 - p.next, p.next)

    def half(self):
        p, sem = self.p, self.sem
        here = self.half_at(p.side)
        return remote(here, here, sem.at[0, 4], sem.at[1, 4], "dp", p.partner)

    def start(self, piece):
        self.piece_at(self.p.side, self.p.row)[...] = piece
        for one in self.first():
            one.start()

    def relay(self):
        p = self.p

        @pl.when(p.inner)
        def _():
            for i, owner in ((2, 3 - p.row), (3, 3 - p.next)):
                self.piece(i, owner, p.next).wait_recv()
                self.piece(i, owner, p.next).start()

    def gathered(self):
        p = self.p
        self.piece(0, p.next, p.next).wait_recv()

        @pl.when(jnp.logical_not(p.inner))
        def _():
            self.piece(0, 3 - p.row, p.next).wait_recv()
            self.piece(0, 3 - p.next, p.next).wait_recv()

    def spread(self):
        self.gathered()
        self.half().start()

    def sent(self):
        p = self.p
        for one in self.first():
            one.wait_send()

        @pl.when(p.inner)
        def _():
            for one in self.passed():
                one.wait_send()

    def finish(self, pieces=True):
        p, sem = self.p, self.sem
        there = self.half_at(1 - p.side)
        remote(there, there, sem.at[0, 4], sem.at[1, 4], "dp", p.partner).wait_recv()
        if pieces:
            self.sent()
        self.half().wait_send()


def total_scratch(line, block):
    return [pltpu.VMEM((line,) + block, BF)] * 2 + [pltpu.SemaphoreType.DMA((2, line))]


ANY_SPEC = pl.BlockSpec(memory_space=pl.ANY)


class Move:
    def __init__(self, src, dst, sem):
        self.copy = pltpu.make_async_copy(src, dst, sem)

    def start(self):
        self.copy.start()
        return self

    def wait(self):
        self.copy.wait()


def norm_stats(x):
    centred = x - jnp.mean(x, axis=-1, keepdims=True)
    inverse = lax.rsqrt(jnp.mean(centred * centred, axis=-1, keepdims=True) + EPS)
    return centred * inverse, inverse


def norm_pull(grad, unit, inverse, gain):
    g = grad * gain
    g = g - jnp.mean(g, axis=-1, keepdims=True) - unit * jnp.mean(g * unit, axis=-1, keepdims=True)
    return g * inverse


def rows_of(ref, k, cols=slice(None)):
    x = ref[:, k, :, cols]
    return x.reshape(x.shape[0] * x.shape[1], x.shape[2])


def col_sum(x):
    return jnp.sum(x, axis=0, keepdims=True)


def enter_kernel(group):
    barrier = pltpu.get_barrier_semaphore()
    pl.semaphore_wait(barrier, group.greet(barrier))


def fold(x, op):
    r = x[:, :128]
    for c in range(1, x.shape[1] // 128):
        r = op(r, x[:, c * 128:(c + 1) * 128])
    return r


class Attend:
    def __init__(self, size, units, length, mixed, out, lse, scores, values):
        self.size, self.units, self.length = size, units, length
        self.mixed, self.out, self.lse, self.scores, self.values = mixed, out, lse, scores, values
        self.width = out.shape[-1]
        self.pairs = self.width // 128
        self.block = mixed.shape[0] // size
        self.rows = self.block // units
        lane = lax.broadcasted_iota(jnp.int32, (1, 128), 1)
        self.heads = [lane < HD, lane >= HD]

    def prepare(self):
        for x in range(self.pairs):
            for h in range(2):
                v = self.mixed[:, 2 * self.width + x * 128:2 * self.width + (x + 1) * 128]
                self.values[2 * x + h] = jnp.where(self.heads[h], v, jnp.zeros_like(v))

    def run(self, u, event=None):
        def body(i):
            self.unit(u, i // self.pairs, i % self.pairs)
            if event is not None:
                pl.when(i == (self.size - 1) * self.pairs - 1)(event)

        loop(self.size * self.pairs, body)

    def unit(self, u, s, x):
        bq, bk = self.rows, self.block
        lanes = pl.ds(pl.multiple_of(x * 128, 128), 128)
        k_lanes = pl.ds(pl.multiple_of(self.width + x * 128, 128), 128)
        k0 = pl.multiple_of(s * bk, bk)
        q0 = pl.multiple_of(s * bk + u * bq, bq)
        qb = self.mixed[pl.ds(q0, bq), lanes]
        qh = [jnp.where(self.heads[h], qb, jnp.zeros_like(qb)) for h in range(2)]
        edge = (u + 1) * bq
        row = lax.broadcasted_iota(jnp.int32, (bq, edge), 0) + u * bq
        mask = lax.broadcasted_iota(jnp.int32, (bq, edge), 1) <= row
        zero = jnp.zeros((bq, 128), F32)

        def first(j, most):
            kb = self.mixed[pl.ds(pl.multiple_of(j * bk, bk), bk), k_lanes]
            new = []
            for h in range(2):
                sc = mm(qh[h], kb, NT)
                self.scores[h, j] = sc
                new.append(jnp.maximum(most[h], fold(jnp.abs(sc), jnp.maximum)))
            return tuple(new)

        most = lax.fori_loop(0, s, first, (zero, zero))
        kb = self.mixed[pl.ds(k0, edge), k_lanes]
        top, state = [], []
        for h in range(2):
            sc = jnp.where(mask, mm(qh[h], kb, NT), 0.0)
            m = jnp.maximum(most[h], fold(jnp.abs(sc), jnp.maximum))
            top.append(jnp.max(m, axis=1, keepdims=True) * SC)
            e = jnp.where(mask, jnp.exp2(jnp.abs(sc) * SC - top[h]), 0.0)
            w = (sgn_of(sc) * e).astype(BF)
            state.append((mm(w, self.values[2 * x + h, pl.ds(k0, edge), :], NN), fold(e, jnp.add)))

        def second(j, carry):
            new = []
            for h in range(2):
                acc, total = carry[h]
                sc = self.scores[h, j]
                e = jnp.exp2(jnp.abs(sc) * SC - top[h])
                w = (sgn_of(sc) * e).astype(BF)
                rows = pl.ds(pl.multiple_of(j * bk, bk), bk)
                acc = acc + mm(w, self.values[2 * x + h, rows, :], NN)
                new.append((acc, total + fold(e, jnp.add)))
            return tuple(new)

        state = lax.fori_loop(0, s, second, tuple(state))
        result = 0.0
        for h in range(2):
            total = jnp.sum(state[h][1], axis=1, keepdims=True)
            result = result + state[h][0] / total
            log_total = jnp.broadcast_to(top[h] + jnp.log(total) * LOG2E, (bq, 128))
            self.lse[x, h:h + 1, pl.ds(q0, bq)] = jnp.transpose(log_total)[0:1, :]
        live = (lax.broadcasted_iota(jnp.int32, (bq, 1), 0) + q0) < self.length[0]
        self.out[pl.ds(q0, bq), lanes] = jnp.where(live, result, 0.0).astype(BF)


def core_kernel(
    size, count, length, gain1, shift1, tb, mb, gain, shift, ub,
    w_hbm, tok_hbm, cot_hbm, mw_hbm, up_hbm, down_hbm,
    full_hbm, mixed_hbm, att, lse, gatt, gres_hbm, resid_hbm, pout_hbm, g_merge, small, bias, *rest,
):
    if count:
        (pieces, held, raw, rest) = (rest[:2], rest[2], rest[3], rest[4:])
    else:
        (g_up, g_down, rest) = (rest[0], rest[1], rest[2:])
    (
        w, mixed, tok, cot, mw, up, down, scores, values, resid, gres, pout, part, in_near, out_far, in_far,
        full, hid, gb, sem0, sem1, sem2, sem3, sem4, sem5, load_sem, cot_sem, out_sem, free,
    ) = rest[:29]
    rest = rest[29:]
    g = Group(size)
    rows, d = tok.shape[0] // CHUNKS, tok.shape[1]
    width, units = mw.shape[0], up.shape[1]
    step = min(512, units)
    p = Place(count) if count else None
    span = lambda k: pl.ds(pl.multiple_of(k * rows, rows), rows)
    loads = [
        Move(src, dst, load_sem.at[i]).start()
        for i, (src, dst) in enumerate(
            ((tok_hbm, tok), (w_hbm, w), (mw_hbm, mw), (up_hbm, up), (down_hbm, down))
        )
    ]
    own = lambda k: Move(cot_hbm.at[k], cot.at[g.me, k], cot_sem.at[k])
    loop(CHUNKS, lambda k: own(k).start())
    begin = Gather(g, full, sem0)
    barrier = pltpu.get_barrier_semaphore()
    pl.semaphore_wait(barrier, g.greet(barrier) + (p.greet(barrier) if count else 0))
    tops = Gather(g, cot, sem5)
    first = Scatter(g, part, in_near, out_far, in_far, sem1)
    spread = Gather(g, full, sem2)
    second = Scatter(g, part, in_near, out_far, in_far, sem3)
    if units == d:
        gfull = hid
    else:
        gfull, rest = rest[0], rest[1:]
    back = Gather(g, gfull, sem4)
    sums = []
    if count:
        g_up, g_down, rest = rest[0], rest[1], rest[2:]
        for ref in (g_down.at[0], g_down.at[1], g_up.at[0]):
            near, far, sem = rest[:3]
            rest = rest[3:]
            sums.append(Total(p, ref, near, far, sem))

    def at(s, k):
        return pl.ds(pl.multiple_of((s * CHUNKS + k) * rows, rows), rows)

    def enter(k):
        unit, _ = norm_stats(tok[span(k), :].astype(F32))
        full[g.me, k] = (unit * gain1[...] + shift1[...]).astype(BF)
        begin.send(k)

    loads[0].wait()
    loop(CHUNKS, enter)

    def mask(k):
        own(k).wait()
        row = lax.broadcasted_iota(jnp.int32, (rows, 1), 0) + (g.me * CHUNKS + k) * rows
        cot[g.me, k] = jnp.where(row < length[0], cot[g.me, k].astype(F32), 0.0).astype(BF)
        tops.send(k)

    loop(CHUNKS, mask)
    loads[1].wait()

    def full_store(k):
        return Move(full.at[:, k], full_hbm.at[:, k], out_sem.at[3, k])

    def project(k):
        begin.wait(k)
        full_store(k).start()
        x = rows_of(full, k)
        for j in range(3):
            cols = slice(j * width, (j + 1) * width)
            y = (mm(x, w[j], NN) + tb[j:j + 1, :]).astype(BF)
            for s in range(size):
                mixed[at(s, k), cols] = y[s * rows:(s + 1) * rows]

    def begin_step(k):
        begin.forward(k)

        @pl.when(k > 0)
        def _():
            project(k - 1)

    loop(CHUNKS, begin_step)
    project(CHUNKS - 1)
    mixed_store = Move(mixed, mixed_hbm, load_sem.at[5]).start()
    attend = Attend(size, 2, length, mixed, att, lse, scores, values)
    attend.prepare()

    def merge(k):
        x = jnp.concatenate([att[at(s, k), :] for s in range(size)], axis=0)
        y = mm(x, mw[...], NN).astype(BF)
        for s in range(size):
            part[s, k] = y[s * rows:(s + 1) * rows]
        first.send(k)

    def resid_store(k):
        return Move(resid.at[span(k)], resid_hbm.at[span(k)], out_sem.at[0, k])

    def norm(k):
        x = tok[span(k), :].astype(F32) + first.final(k) + mb[...]
        resid[span(k), :] = x
        resid_store(k).start()
        unit, _ = norm_stats(x)
        full[g.me, k] = (unit * gain[...] + shift[...]).astype(BF)
        spread.send(k)

    def inner(k):
        spread.forward(k)
        spread.wait(k)
        x = rows_of(full, k)
        top = rows_of(cot, k)

        def tile(j):
            cols = pl.ds(pl.multiple_of(j * step, step), step)
            v = mm(x, up[:, cols], NN) + ub[:, cols]
            gh = mm(top, down[cols, :], NT)
            c0, c1 = 0.7978845608, 0.044715
            v2 = v * v
            th = jnp.tanh(c0 * (v + c1 * v2 * v))
            half = 0.5 * (1.0 + th)
            h = (v * half).astype(BF)
            slope = half + 0.5 * v * (1.0 - th * th) * (c0 * (1.0 + 3.0 * c1 * v2))
            gv = (gh * slope).astype(BF)
            bias[0:1, cols] += col_sum(gv.astype(F32))
            for s in range(size):
                hid[s, k, :, cols] = h[s * rows:(s + 1) * rows]
                gb[s, k, :, cols] = gv[s * rows:(s + 1) * rows]

        loop(units // step, tile)

    def pout_store(k):
        return Move(pout.at[k % 2], pout_hbm.at[:, k], out_sem.at[1, k])

    def leave(k):
        h, gv = rows_of(hid, k), rows_of(gb, k)

        @pl.when(k >= 2)
        def _():
            pout_store(k - 2).wait()

        def tile(j):
            cols = pl.ds(pl.multiple_of(j * 512, 512), 512)
            y = mm(h, down[:, cols], NN).astype(BF)
            z = mm(gv, up[cols, :], NT).astype(BF)
            for s in range(size):
                pout[k % 2, s, :, cols] = y[s * rows:(s + 1) * rows]
                part[s, k, :, cols] = z[s * rows:(s + 1) * rows]

        loop(d // 512, tile)
        pout_store(k).start()
        second.send(k)

    def flat(ref, cols):
        x = ref[:, :, :, cols]
        return x.reshape(size * CHUNKS * rows, x.shape[3])

    def products(ref, left, right, extent):
        tall = min(256, extent)

        def block(i):
            cols = pl.ds(pl.multiple_of(i * tall, tall), tall)
            y = mm(flat(left, cols), flat(right, slice(None)), TN).astype(BF)
            if not count:
                ref[cols, :] = y
            else:
                deep = ref.shape[3]
                for e in range(tall // deep):
                    f = i * (tall // deep) + e
                    ref[f // (2 * p.line), f // p.line % 2, f % p.line] = y[e * deep:(e + 1) * deep]

        return block, extent // tall

    def weights(ref, left, right, extent, event=None):
        block, blocks = products(ref, left, right, extent)
        after(0, blocks, block, {blocks // 2 - 1: event})

    def after(low, high, body, events):
        def step(k):
            body(k)
            for at_k, event in events.items():
                if count and event is not None:
                    pl.when(k == at_k)(event)

        loop_range(low, high, step)

    def gres_store(k):
        return Move(gres.at[k % 2], gres_hbm.at[span(k)], out_sem.at[2, k])

    def pull(k):
        gs = second.final(k)
        unit, inverse = norm_stats(resid[span(k), :])
        top = cot[g.me, k].astype(F32)
        gr = top + norm_pull(gs, unit, inverse, gain[...])

        @pl.when(k >= 2)
        def _():
            gres_store(k - 2).wait()

        gres[k % 2] = gr
        gres_store(k).start()
        gfull[g.me, k] = gr.astype(BF)
        back.send(k)
        small[2:3, :] += col_sum(gr)
        small[3:4, :] += col_sum(gs * unit)
        small[4:5, :] += col_sum(gs)
        small[5:6, :] += col_sum(top)

    def last(k):
        back.forward(k)
        back.wait(k)
        y = mm(rows_of(gfull, k), mw[...], NT)
        for s in range(size):
            row = lax.broadcasted_iota(jnp.int32, (rows, 1), 0) + (s * CHUNKS + k) * rows
            gatt[s, k] = jnp.where(row < length[0], y[s * rows:(s + 1) * rows], 0.0).astype(BF)

    def later(*steps):
        if count:
            for one in steps:
                one()

    bias[...] = jnp.zeros_like(bias)
    small[...] = jnp.zeros_like(small)
    attend.run(0)
    for load in loads[2:]:
        load.wait()
    loop(CHUNKS, begin.drain)
    loop(CHUNKS, lambda k: full_store(k).wait())
    loop(2, merge)
    loop(2, first.combine)
    loop(2, tops.forward)

    def between():
        loop_range(2, CHUNKS, tops.forward)
        loop(2, norm)

    attend.run(1, between)
    loop_range(2, CHUNKS, merge)
    loop_range(2, CHUNKS, first.combine)
    loop(CHUNKS, tops.wait)
    loop(2, inner)
    loop(2, first.drain)
    loop(2, leave)
    loop_range(2, CHUNKS, norm)
    loop(2, second.combine)
    loop_range(2, CHUNKS, first.drain)
    loop_range(2, CHUNKS, inner)
    weights(g_down, hid, cot, units, sums[0].start if count else None)
    pl.semaphore_wait(free, g.greet(free))
    loop(2, pull)
    after(2, CHUNKS, leave, {2: sums[1].start if count else None})
    loop_range(2, CHUNKS, second.combine)
    later(lambda: sums[0].halve())
    weights(g_up, full, gb, d)
    later(lambda: sums[2].start())
    loop(CHUNKS, tops.drain)
    loop(CHUNKS, spread.drain)

    def turn():
        sums[0].relay()
        sums[1].halve()

    after(2, CHUNKS, pull, {2: turn})
    after(0, CHUNKS, last, {0: lambda: sums[1].relay()})
    y = mm(att[...], flat(gfull, slice(None)), TN).astype(BF)
    if count:
        deep = g_merge.shape[2]
        for f in range(2 * p.line):
            g_merge[f // p.line, f % p.line] = y[f * deep:(f + 1) * deep]
        raw[...] = g_up[1]
        sums[2].add()
        held[...] = sums[2].near[...]
        pieces[0][...] = sums[0].settle()
        pieces[1][...] = sums[1].settle()
        for h in range(3):
            sums[h].drain(True, h < 2)
    else:
        g_merge[...] = y
    loop(CHUNKS, second.drain)
    loop(CHUNKS, back.drain)
    loop(CHUNKS, lambda k: resid_store(k).wait())
    mixed_store.wait()
    loop_range(2, CHUNKS, lambda k: pout_store(k).wait())
    loop_range(2, CHUNKS, lambda k: gres_store(k).wait())


def core(size, count, lengths, gain1, shift1, tb, mb, gain, shift, ub, w, tokens, cotangent, mw,
         up, down):
    rows, d = tokens.shape
    r = rows // CHUNKS
    n = rows * size
    width, units = mw.shape[0], up.shape[1]
    pairs = width // 128
    shape = jax.ShapeDtypeStruct
    dma = pltpu.SemaphoreType.DMA
    vm = pltpu.VMEM
    wide = lambda c: vm((size, CHUNKS, r, c), BF)
    line = count // 2
    if count:
        blocks = ((2, 2, line, d // (4 * line), units), (2, 2, line, units // (4 * line), d))
        merge = shape((2, line, width // (2 * line), d), BF)
        piece = [shape(b[3:], BF) for b in blocks[::-1]]
        extra = (piece[0], piece[0], shape((line,) + blocks[0][3:], BF), shape(blocks[0][1:], BF))
        scratch = [vm(b, BF) for b in blocks]
        scratch += total_scratch(line, blocks[1][3:]) * 2 + total_scratch(line, blocks[0][3:])
    else:
        merge = shape((width, d), BF)
        extra = (shape((d, units), BF), shape((units, d), BF))
        scratch = []
    if units != d:
        scratch = [wide(d)] + scratch
    outs = (
        (shape((size, CHUNKS, r, d), BF), ANY_SPEC),
        (shape((n, 3 * width), BF), ANY_SPEC),
        (shape((n, width), BF), VMEM_SPEC),
        (shape((pairs, 8, n), F32), VMEM_SPEC),
        (shape((size, CHUNKS, r, width), BF), VMEM_SPEC),
        (shape((rows, d), F32), ANY_SPEC),
        (shape((rows, d), F32), ANY_SPEC),
        (shape((size, CHUNKS, r, d), BF), ANY_SPEC),
        (merge, VMEM_SPEC),
        (shape((8, d), F32), VMEM_SPEC),
        (shape((8, units), F32), VMEM_SPEC),
        *((x, VMEM_SPEC) for x in extra),
    )
    return pl.pallas_call(
        functools.partial(core_kernel, size, count),
        out_shape=tuple(x for x, _ in outs),
        in_specs=[SMEM_SPEC] + [VMEM_SPEC] * 7 + [ANY_SPEC] * 6,
        out_specs=tuple(x for _, x in outs),
        scratch_shapes=[
            vm(w.shape, BF), vm((n, 3 * width), BF), vm((rows, d), BF), wide(d), vm((width, d), BF), vm((d, units), BF), vm((units, d), BF),
            vm((2, size, rows // 2, rows), F32), vm((2 * pairs, n, 128), BF), vm((rows, d), F32),
            vm((2, r, d), F32), vm((2, size, r, d), BF),
        ]
        + scatter_scratch(size, r, d)
        + [wide(d), wide(units), wide(units)]
        + [sems(size)] * 6
        + [dma((6,)), dma((CHUNKS,)), dma((4, CHUNKS)), pltpu.SemaphoreType.REGULAR]
        + scratch,
        compiler_params=pltpu.CompilerParams(
            collective_id=1, has_side_effects=True, vmem_limit_bytes=64 << 20
        ),
        name="core",
    )(lengths, gain1, shift1, tb, mb, gain, shift, ub, w, tokens, cotangent.reshape(CHUNKS, r, d), mw,
      up, down)


def tail_kernel(
    size, dq, dk, dv, full, w, tok, gres, gain,
    gtok, g_triple, small, bias,
    part, in_near, out_far, in_far, sem,
):
    g = Group(size)
    rows, d = tok.shape[0] // CHUNKS, tok.shape[1]
    width = dq.shape[3]
    enter_kernel(g)
    scatter = Scatter(g, part, in_near, out_far, in_far, sem)
    span = lambda k: pl.ds(pl.multiple_of(k * rows, rows), rows)
    grads = (dq, dk, dv)

    def back(k):
        def tile(j):
            cols = pl.ds(pl.multiple_of(j * 256, 256), 256)
            z = sum(
                mm(rows_of(x, k), w[c, cols, :], NT)
                for c, x in enumerate(grads)
            )
            for s in range(size):
                part[s, k, :, cols] = z[s * rows:(s + 1) * rows].astype(BF)

        loop(d // 256, tile)
        scatter.send(k)

    loop(CHUNKS, back)
    loop(CHUNKS, scatter.combine)

    def flat(ref, cols):
        x = ref[:, :, :, cols]
        return x.reshape(size * CHUNKS * rows, x.shape[3])

    bias[...] = jnp.zeros_like(bias)
    for c, x in enumerate(grads):
        y = flat(x, slice(None))
        bias[0:1, c * width:(c + 1) * width] = col_sum(y.astype(F32))

        def tile(i):
            more = pl.ds(pl.multiple_of(i * 256, 256), 256)
            g_triple[c, more, :] = mm(flat(full, more), y, TN).astype(BF)

        loop(d // 256, tile)
    small[...] = jnp.zeros_like(small)

    def pull(k):
        gf = scatter.final(k)
        unit, inverse = norm_stats(tok[span(k), :].astype(F32))
        gtok[span(k), :] = gres[span(k), :] + norm_pull(gf, unit, inverse, gain[...])
        small[0:1, :] += col_sum(gf * unit)
        small[1:2, :] += col_sum(gf)

    loop(CHUNKS, pull)
    loop(CHUNKS, scatter.drain)


def tail(size, dq, dk, dv, full, w, tokens, gres, gain):
    rows, d = tokens.shape
    r = rows // CHUNKS
    width = dq.shape[-1]
    shape = jax.ShapeDtypeStruct
    return pl.pallas_call(
        functools.partial(tail_kernel, size),
        out_shape=(
            shape((rows, d), F32),
            shape((3, d, width), BF),
            shape((8, d), F32),
            shape((8, 3 * width), F32),
        ),
        in_specs=[VMEM_SPEC] * 8,
        out_specs=(VMEM_SPEC,) * 4,
        scratch_shapes=scatter_scratch(size, r, d) + [sems(size)],
        compiler_params=pltpu.CompilerParams(
            collective_id=2, has_side_effects=True, vmem_limit_bytes=56 << 20
        ),
        name="tail",
    )(dq, dk, dv, full, w, tokens, gres, gain)


class Everyone:
    def __init__(self, axis, count, buf, sem):
        self.axis, self.count, self.buf, self.sem = axis, count, buf, sem
        self.me = lax.axis_index(axis)

    def copy(self, owner, off, back):
        here = self.buf.at[owner]
        return remote(
            here, here, self.sem.at[0, off], self.sem.at[1, back], self.axis,
            (self.me + off) % self.count,
        )

    def start(self, value):
        self.buf[self.me] = value
        for off in range(1, self.count):
            self.copy(self.me, off, self.count - off).start()

    def finish(self):
        for off in range(1, self.count):
            self.copy((self.me + off) % self.count, off, off).wait_recv()
        total = self.buf[0]
        for j in range(1, self.count):
            total = total + self.buf[j]
        for off in range(1, self.count):
            self.copy(self.me, off, self.count - off).wait_send()
        return total


def late_kernel(
    size, count, bk, gain, db, p_down0, p_down1, u_held, u_raw, g_merge, small_in, bias_in,
    mixed_hbm, att_hbm, gatt_hbm, lse_hbm, full_hbm, w_hbm, tok_hbm, gres_hbm, resid_hbm, pout_hbm,
    out, gtok_hbm, o_down, o_up, o_merge, o_triple, small,
    mixed, att, gatt, lse, full, w, tok, gres, resid, pout, load_sem,
    qm, km, dom, dsc, dq_acc, gm, g_triple, part, in_near, out_far, in_far,
    in_near2, out_far2, in_far2, sem, sem2, u_far, u_sem, v_near, v_far, v_sem,
    m_near, m_far, m_sem, t_near, t_far, t_sem, s_sem, t_buf, t_sems, d_buf, d_sems, g_sem,
):
    loads = [
        Move(src, dst, load_sem.at[i]).start()
        for i, (src, dst) in enumerate(
            (
                (mixed_hbm, mixed), (gatt_hbm, gatt), (att_hbm, att), (lse_hbm, lse),
                (pout_hbm, pout), (resid_hbm, resid), (full_hbm, full), (w_hbm, w),
                (tok_hbm, tok), (gres_hbm, gres),
            )
        )
    ]
    g, p = Group(size), Place(count)
    n = mixed.shape[0]
    rows, d = tok.shape[0] // CHUNKS, tok.shape[1]
    width = att.shape[1]
    pairs = width // 128
    barrier = pltpu.get_barrier_semaphore()
    for axis, extent in (("tensor", size), ("dp", count)):
        for off in range(1, extent):
            pl.semaphore_signal(
                barrier,
                inc=1,
                device_id={axis: (lax.axis_index(axis) + off) % extent},
                device_id_type=pl.DeviceIdType.MESH,
            )
    pl.semaphore_wait(barrier, size + count - 2)

    def share(ref, sem):
        return Share(p, lambda side, line: ref.at[side, line], lambda side: ref.at[side], sem)

    deep = g_triple.shape[5]

    def triple_share(x, h):
        lanes, part_rows = pl.ds(x * 128, 128), pl.ds(h * deep, deep)
        return Share(
            p,
            lambda side, line: o_triple.at[:, side, line, part_rows, lanes],
            lambda side: o_triple.at[:, side, :, part_rows, lanes],
            s_sem.at[5 + 2 * x + h],
        )

    def triple_total(x, h):
        return Total(p, g_triple.at[x, h], t_near.at[x, h], t_far.at[x, h], t_sem.at[x, h])

    shares = [
        share(ref.at[h], s_sem.at[2 * a + h])
        for a, ref in enumerate((o_down, o_up))
        for h in range(2)
    ]
    merge_total = Total(p, g_merge, m_near, m_far, m_sem)
    merge_share = share(o_merge, s_sem.at[4])
    totals = [triple_total(x, h) for x in range(pairs) for h in range(2)]
    triples = [triple_share(x, h) for x in range(pairs) for h in range(2)]
    branch = Scatter(g, pout, in_near2, out_far2, in_far2, sem2)
    up_total = Total(p, None, u_held, u_far, u_sem)
    up_total.scatter()
    raw_total = Total(p, u_raw, v_near, v_far, v_sem)
    raw_total.start()
    shares[0].start(p_down0[...])
    for load in loads[:4]:
        load.wait()

    lane = lax.broadcasted_iota(jnp.int32, (1, 128), 1)
    heads = [lane < HD, lane >= HD]
    row = lax.broadcasted_iota(jnp.int32, (bk, bk), 0)
    col = lax.broadcasted_iota(jnp.int32, (bk, bk), 1)

    def attention(x, events):
        def lanes(c):
            return pl.ds(pl.multiple_of(c * width + x * 128, 128), 128)

        def prepare(i):
            sl = pl.ds(pl.multiple_of(i * bk, bk), bk)
            z = jnp.zeros((bk, 128), BF)
            for h in range(2):
                qm[h, sl, :] = jnp.where(heads[h], mixed[sl, lanes(0)], z)
                km[h, sl, :] = jnp.where(heads[h], mixed[sl, lanes(1)], z)
                do = jnp.where(heads[h], gatt[sl, lanes(0)], z)
                dom[h, sl, :] = do
                prod = do.astype(F32) * att[sl, lanes(0)].astype(F32)
                dd = jnp.broadcast_to(jnp.sum(prod, axis=1, keepdims=True), (bk, 128))
                dsc[h:h + 1, sl] = jnp.transpose(dd)[0:1, :]
            dq_acc[sl, :] = jnp.zeros((bk, 128), F32)

        loop(n // bk, prepare)

        def tile(j, i, dk, dv, diag):
            ks, qs = pl.ds(pl.multiple_of(j * bk, bk), bk), pl.ds(pl.multiple_of(i * bk, bk), bk)
            kb, vb = mixed[ks, lanes(1)], mixed[ks, lanes(2)]
            dq = None
            for h in range(2):
                qh, doh = qm[h, qs, :], dom[h, qs, :]
                s = mm(kb, qh, NT)
                dp = mm(vb, doh, NT)
                e = jnp.exp2(jnp.abs(s) * SC - lse[x, h:h + 1, qs])
                if diag:
                    e = jnp.where(row <= col, e, 0.0)
                sg = sgn_of(s)
                a = sg * e
                ds = (a * (sg * dp - dsc[h:h + 1, qs])).astype(BF)
                dv = dv + mm(a.astype(BF), doh, NN)
                dk = dk + mm(ds, qh, NN)
                t = mm(ds, km[h, ks, :], TN)
                dq = t if dq is None else dq + t
            dq_acc[qs, :] += dq
            return dk, dv

        def serve(j, i):
            for at_x, at_j, at_i, event in events:
                pl.when((x == at_x) & (j == at_j) & (i == at_i))(event)

        def block(j):
            serve(j, j)
            z = jnp.zeros((bk, 128), F32)
            dk, dv = tile(j, j, z, z, True)

            def more(i, c):
                serve(j, i)
                return tile(j, i, c[0], c[1], False)

            dk, dv = lax.fori_loop(j + 1, n // bk, more, (dk, dv))
            ks = pl.ds(pl.multiple_of(j * bk, bk), bk)
            gm[1, ks, lanes(0)] = (dk * HD ** (-0.5)).astype(BF)
            gm[2, ks, lanes(0)] = dv.astype(BF)

        loop(n // bk, block)
        gm[0, :, lanes(0)] = (dq_acc[...] * HD ** (-0.5)).astype(BF)

    def flat(ref, cols):
        y = ref[:, :, :, cols]
        return y.reshape(n, y.shape[3])

    def weights(x):
        mine = pl.ds(pl.multiple_of(x * 128, 128), 128)
        y = jnp.concatenate([gm[c, :, mine] for c in range(3)], axis=1)

        def tile(i):
            z = mm(flat(full, pl.ds(pl.multiple_of(i * 256, 256), 256)), y, TN).astype(BF)
            for e in range(128 // deep):
                f = i * (128 // deep) + e
                for h in range(2):
                    at = (2 * e + h) * deep
                    for c in range(3):
                        g_triple[x, h, f // p.line, f % p.line, c] = z[
                            at:at + deep, c * 128:(c + 1) * 128
                        ]

        loop(d // 256, tile)
        triple_total(x, 0).start()

    span = lambda k: pl.ds(pl.multiple_of(k * rows, rows), rows)

    def branch_start():
        loads[4].wait()
        loop(CHUNKS, branch.send)

    def branch_end():
        loads[5].wait()

        def one(k):
            out[span(k), :] = (resid[span(k), :] + branch.final(k) + db[...]).astype(BF)

        loop(CHUNKS, one)

    span = lambda k: pl.ds(pl.multiple_of(k * rows, rows), rows)

    def branch_start():
        loads[4].wait()
        loop(CHUNKS, branch.send)

    def branch_end():
        loads[5].wait()

        def one(k):
            out[span(k), :] = (resid[span(k), :] + branch.final(k) + db[...]).astype(BF)

        loop(CHUNKS, one)

    schedule = [[] for _ in range(pairs)]
    end = pairs - 1
    events = [
        (0, 0, 0, branch_start),
        (0, 0, 2, merge_total.start),
        (0, 1, 1, lambda: loop(CHUNKS, branch.combine)),
        (0, 1, 2, up_total.relay),
        (0, 1, 2, raw_total.halve),
        (0, 1, 3, shares[0].relay),
        (0, 1, 3, lambda: shares[1].start(p_down1[...])),
        (0, 2, 3, lambda: shares[2].start(up_total.settle())),
        (0, 3, 3, shares[0].spread),
        (0, 3, 3, raw_total.relay),
        (0, 3, 3, shares[1].relay),
        (end, 0, 1, totals[1].start),
        (end, 0, 1, shares[2].relay),
        (end, 0, 1, lambda: shares[3].start(raw_total.settle())),
        (end, 0, 2, shares[1].spread),
        (end, 0, 3, merge_total.halve),
        (end, 1, 1, shares[3].relay),
        (end, 1, 1, branch_end),
        (end, 1, 2, shares[2].spread),
        (end, 1, 3, totals[0].halve),
        (end, 2, 2, merge_total.relay),
        (end, 2, 3, totals[1].halve),
        (end, 3, 3, totals[0].relay),
        (end, 3, 3, lambda: merge_share.start(merge_total.settle())),
    ]

    def pair(x):
        attention(x, events)

        @pl.when(x == 0)
        def _():
            for load in loads[6:]:
                load.wait()

        weights(x)

    loop(pairs, pair)

    scatter = Scatter(g, part, in_near, out_far, in_far, sem)

    def back(k):
        def tile(j):
            cols = pl.ds(pl.multiple_of(j * 256, 256), 256)
            z = 0.0
            for c in range(3):
                y = jnp.concatenate(
                    [
                        gm[c, pl.ds(pl.multiple_of((s * CHUNKS + k) * rows, rows), rows), :]
                        for s in range(size)
                    ],
                    axis=0,
                )
                z = z + mm(y, w[c, cols, :], NT)
            for s in range(size):
                part[s, k, :, cols] = z[s * rows:(s + 1) * rows].astype(BF)

        loop(d // 256, tile)
        scatter.send(k)

    near_end, far_end = totals[-2:]

    def back_step(k):
        back(k)
        pl.when(k == 0)(totals[1].relay)
        pl.when(k == 1)(far_end.start)
        pl.when(k == 1)(lambda: triples[0].start(totals[0].settle()))
        pl.when(k == 2)(lambda: triples[1].start(totals[1].settle()))
        pl.when(k == 2)(merge_share.relay)
        pl.when(k == 3)(shares[3].spread)

        @pl.when(k > 0)
        def _():
            scatter.combine(k - 1)

    loop(CHUNKS, back_step)
    near_end.halve()
    scatter.combine(CHUNKS - 1)
    small[...] = small_in[...]
    units = bias_in.shape[1]
    small[6:7, :units] = bias_in[0:1, :]
    for c in range(3):
        small[7:8, c * width:(c + 1) * width] = col_sum(gm[c].astype(F32))

    def gtok_store(k):
        return Move(gres.at[span(k)], gtok_hbm.at[span(k)], g_sem.at[k])

    def pull(k):
        gf = scatter.final(k)
        unit, inverse = norm_stats(tok[span(k), :].astype(F32))
        gres[span(k), :] += norm_pull(gf, unit, inverse, gain[...])
        gtok_store(k).start()
        small[0:1, :] += col_sum(gf * unit)
        small[1:2, :] += col_sum(gf)

    triples[0].relay()
    far_end.halve()
    near_end.relay()
    triples[1].relay()

    def pull_step(k):
        pull(k)

        @pl.when(k == 0)
        def _():
            merge_share.spread()
            triples[-2].start(near_end.settle())
            far_end.relay()

        @pl.when(k == 1)
        def _():
            triples[0].spread()
            triples[1].spread()
            triples[-1].start(far_end.settle())
            triples[-2].relay()

        pl.when(k == 2)(triples[-2].spread)

    loop(CHUNKS, pull_step)
    group_sum = Everyone("tensor", size, t_buf, t_sems)
    group_sum.start(small[...])
    triples[-1].relay()
    total = group_sum.finish()
    keep = lax.broadcasted_iota(jnp.int32, (8, 1), 0) < 6
    all_sum = Everyone("dp", count, d_buf, d_sems)
    all_sum.start(jnp.where(keep, total, small[...]))
    triples[-1].spread()
    small[...] = all_sum.finish()
    for one in shares + [merge_share] + triples:
        one.finish()
    merge_total.drain()
    up_total.drain(False)
    raw_total.drain()
    for t in totals:
        t.drain()
    loop(CHUNKS, scatter.drain)
    loop(CHUNKS, branch.drain)
    loop(CHUNKS, lambda k: gtok_store(k).wait())


def late(size, count, gain, db, p_down0, p_down1, u_held, u_raw, g_merge, small_in, bias_in,
         mixed, att, gatt, lse, full, w, tokens, gres, resid, pout):
    rows, d = tokens.shape
    n, width = att.shape
    r = rows // CHUNKS
    line = count // 2
    pairs = width // 128
    bk = min(512, n)
    shape = jax.ShapeDtypeStruct
    piece = d // count
    vm = pltpu.VMEM
    dma = pltpu.SemaphoreType.DMA
    deep = g_merge.shape[2]
    scatter = scatter_scratch(size, r, d)
    loads = (mixed, att, gatt, lse, full, w, tokens, gres, resid, pout)
    return pl.pallas_call(
        functools.partial(late_kernel, size, count, bk),
        out_shape=(
            shape((rows, d), BF),
            shape((rows, d), F32),
            shape((2, 2, line) + p_down1.shape, BF),
            shape((2, 2, line) + u_raw.shape[2:], BF),
            shape(g_merge.shape, BF),
            shape((3, 2, line, piece, width), BF),
            shape((8, d), F32),
        ),
        in_specs=[VMEM_SPEC] * 9 + [ANY_SPEC] * len(loads),
        out_specs=(VMEM_SPEC, ANY_SPEC) + (VMEM_SPEC,) * 5,
        scratch_shapes=[vm(x.shape, x.dtype) for x in loads]
        + [dma((len(loads),))]
        + [vm((2, n, 128), BF)] * 3
        + [vm((8, n), F32), vm((n, 128), F32), vm((3, n, width), BF)]
        + [vm((pairs, 2, 2, line, 3, piece // 2, 128), BF)]
        + scatter
        + scatter[1:]
        + [sems(size)] * 2
        + total_scratch(line, u_raw.shape[2:])[1:] + total_scratch(line, u_raw.shape[2:])
        + total_scratch(line, (deep, d))
        + [vm((pairs, 2, line, 3, piece // 2, 128), BF)] * 2
        + [dma((pairs, 2, 2, line)), dma((5 + 2 * pairs, 2, line + 1))]
        + [vm((size, 8, d), F32), dma((2, size)), vm((count, 8, d), F32), dma((2, count)), dma((CHUNKS,))],
        compiler_params=pltpu.CompilerParams(
            collective_id=3, has_side_effects=True, vmem_limit_bytes=64 << 20
        ),
        name="late",
    )(gain, db, p_down0, p_down1, u_held, u_raw, g_merge, small_in, bias_in, *loads)


def widen_kernel(down, up, merge, triple, small, out, tok, o_down, o_up, o_merge, o_triple, o_out, o_tok, *o_small):
    for src, dst in ((down, o_down), (up, o_up), (merge, o_merge), (triple, o_triple)):
        dst[...] = src[...].astype(F32)
    o_out[...] = out[...]
    o_tok[...] = tok[...]

    @pl.when(pl.program_id(0) == 0)
    def _():
        for i, dst in enumerate(o_small[:7]):
            dst[...] = small[i:i + 1, :dst.shape[1]]
        width = o_small[7].shape[1]
        for c in range(3):
            o_small[7][c:c + 1, :] = small[7:8, c * width:(c + 1) * width]


def widen(down, up, merge, triple, small, out, tok):
    steps = 2
    d, units, width = small.shape[1], up.shape[1], triple.shape[2]

    def spec(x):
        axis = x.ndim - 2
        block = x.shape[:axis] + (x.shape[axis] // steps, x.shape[-1])
        return pl.BlockSpec(block, lambda i: (0,) * axis + (i, 0))

    def whole(shape):
        return pl.BlockSpec(shape, lambda i: (0, 0))

    arrays = (down, up, merge, triple)
    lines = [(1, d)] * 6 + [(1, units), (3, width)]
    outs = [(x.shape, F32, spec(x)) for x in arrays] + [(x.shape, x.dtype, spec(x)) for x in (out, tok)]
    outs += [(x, F32, whole(x)) for x in lines]
    return pl.pallas_call(
        widen_kernel,
        grid=(steps,),
        out_shape=tuple(jax.ShapeDtypeStruct(x, t) for x, t, _ in outs),
        in_specs=[spec(x) for x in arrays] + [whole(small.shape), spec(out), spec(tok)],
        out_specs=tuple(x for _, _, x in outs),
        compiler_params=pltpu.CompilerParams(vmem_limit_bytes=60 << 20),
        name="widen",
    )(down, up, merge, triple, small, out, tok)


def on_device(
    tokens,
    first_gain,
    first_shift,
    triple_weight,
    triple_bias,
    merge_weight,
    merge_bias,
    second_gain,
    second_shift,
    up_weight,
    up_bias,
    down_weight,
    down_bias,
    lengths,
    cotangent,
):
    size = lax.axis_size("tensor")
    count = lax.axis_size("dp")
    row_count, d = tokens.shape
    rows = row_count // CHUNKS
    width = triple_weight.shape[2]
    units = up_weight.shape[1]
    n = row_count * size
    fused = (
        count == 8 and units % 512 == 0 and width % 256 == 0 and 3 * width <= d and units <= d
    )
    count = count if fused else 0
    line = lambda v: v.reshape(1, -1)
    w = jnp.transpose(triple_weight, (1, 0, 2))
    full, mixed, attended, log_total, gatt, gres, resid, pout, g_merge, small_b, bias_b, *rest = core(
        size, count, lengths, line(first_gain), line(first_shift), triple_bias, line(merge_bias),
        line(second_gain), line(second_shift), line(up_bias), w, tokens, cotangent, merge_weight,
        up_weight, down_weight,
    )
    gatt = gatt.reshape(n, width)
    if fused:
        output, gtok, down, up, merge, triple, small = late(
            size, count, line(first_gain), line(down_bias), *rest, g_merge, small_b, bias_b,
            mixed, attended, gatt, log_total, full, w, tokens, gres, resid, pout,
        )
        down, up, merge, triple, output, gtok, *small, up_b, triple_b = widen(
            down.reshape(units, d), up.reshape(d, units), merge.reshape(width, d),
            triple.reshape(3, d, width), small, output, gtok,
        )
        triple = jnp.transpose(triple, (1, 0, 2))
        small = [x.reshape(d) for x in small]
        up_b = up_b.reshape(units)
    else:
        branch = lax.psum_scatter(pout.reshape(n, d), "tensor", scatter_dimension=0, tiled=True)
        g_up, g_down = rest
        blocks = lambda x: x.reshape(size, CHUNKS, rows, x.shape[-1])
        dq, dk, dv = attend_bwd(mixed, attended, log_total, gatt)
        gtok, g_triple, small_c, bias_c = tail(
            size, blocks(dq), blocks(dk), blocks(dv), full, w, tokens, gres, line(first_gain)
        )
        merge, up, down, triple = lax.psum((g_merge, g_up, g_down, g_triple), "dp")
        triple_b, up_b = lax.psum((bias_c[0], bias_b[0]), "dp")
        small = lax.psum(small_b + small_c, ("dp", "tensor"))
        triple = jnp.transpose(triple, (1, 0, 2)).astype(F32)
        triple_b = triple_b.reshape(3, width)
        merge, up, down = merge.astype(F32), up.astype(F32), down.astype(F32)
        output = (resid + branch.astype(F32) + down_bias).astype(BF)
    return (
        output,
        gtok,
        small[0],
        small[1],
        triple,
        triple_b,
        merge,
        small[2],
        small[3],
        small[4],
        up,
        up_b,
        down,
        small[5],
    )


def solution(mesh):
    in_specs = (
        P(("dp", "tensor"), None),
        P(),
        P(),
        P(None, None, "tensor"),
        P(None, "tensor"),
        P("tensor", None),
        P(),
        P(),
        P(),
        P(None, "tensor"),
        P("tensor"),
        P("tensor", None),
        P(),
        P("dp"),
        P(("dp", "tensor"), None),
    )
    out_specs = (
        P(("dp", "tensor"), None),
        P(("dp", "tensor"), None),
        P(),
        P(),
        P(None, None, "tensor"),
        P(None, "tensor"),
        P("tensor", None),
        P(),
        P(),
        P(),
        P(None, "tensor"),
        P("tensor"),
        P("tensor", None),
        P(),
    )
    return jax.shard_map(
        on_device, mesh=mesh, in_specs=in_specs, out_specs=out_specs, check_vma=False
    )
```

```python
import functools

import jax
import jax.numpy as jnp
from jax import lax
from jax.experimental import pallas as pl
from jax.experimental.pallas import tpu as pltpu
from jax.sharding import PartitionSpec as P

EPS = 1e-05
HD = 64
LOG2E = 1.4426950408889634
SC = HD ** (-0.5) * LOG2E
BIG = 1e30
NT = (((1,), (1,)), ((), ()))
TN = (((0,), (0,)), ((), ()))
NN = (((1,), (0,)), ((), ()))


def mm(a, b, dims):
    return lax.dot_general(a, b, dims, preferred_element_type=jnp.float32)


def sgn_of(s):
    return jnp.minimum(jnp.maximum(s * BIG, -1.0), 1.0)


def bwd_kernel(bq, bk, q_ref, k_ref, v_ref, do_ref, o_ref, lse_ref, dq_ref, dk_ref, dv_ref,
               qm, km, dom, dsc, dq_acc):
    n = q_ref.shape[0]
    lane = lax.broadcasted_iota(jnp.int32, (1, 128), 1)
    hm = [lane < HD, lane >= HD]
    for h in range(2):
        for r in range(0, n, 512):
            sl = pl.ds(r, 512)
            z = jnp.zeros((512, 128), jnp.bfloat16)
            qm[h, sl, :] = jnp.where(hm[h], q_ref[sl, :], z)
            km[h, sl, :] = jnp.where(hm[h], k_ref[sl, :], z)
            d = jnp.where(hm[h], do_ref[sl, :], z)
            dom[h, sl, :] = d
            prod = d.astype(jnp.float32) * o_ref[sl, :].astype(jnp.float32)
            dd = jnp.broadcast_to(jnp.sum(prod, axis=1, keepdims=True), (512, 128))
            dsc[h:h + 1, sl] = jnp.transpose(dd)[0:1, :]
    dq_acc[...] = jnp.zeros_like(dq_acc)
    row = lax.broadcasted_iota(jnp.int32, (bk, bq), 0)
    col = lax.broadcasted_iota(jnp.int32, (bk, bq), 1)

    def tile(j, i, dk, dv, diag):
        k0 = pl.multiple_of(j * bk, bk)
        q0 = pl.multiple_of(i * bq, bq)
        ks, qs = pl.ds(k0, bk), pl.ds(q0, bq)
        kb, vb = k_ref[ks, :], v_ref[ks, :]
        dq = None
        for h in range(2):
            qh = qm[h, qs, :]
            doh = dom[h, qs, :]
            s = mm(kb, qh, NT)
            dp = mm(vb, doh, NT)
            p = jnp.exp2(jnp.abs(s) * SC - lse_ref[0, h:h + 1, qs])
            if diag:
                p = jnp.where((row + k0) <= (col + q0), p, 0.0)
            sg = sgn_of(s)
            w = sg * p
            ds = (w * (sg * dp - dsc[h:h + 1, qs])).astype(jnp.bfloat16)
            dv = dv + mm(w.astype(jnp.bfloat16), doh, NN)
            dk = dk + mm(ds, qh, NN)
            t = mm(ds, km[h, ks, :], TN)
            dq = t if dq is None else dq + t
        dq_acc[qs, :] += dq
        return dk, dv

    r = bk // bq
    def kvblock(j, _):
        z = jnp.zeros((bk, 128), jnp.float32)
        dk, dv = z, z
        for a in range(r):
            dk, dv = tile(j, j * r + a, dk, dv, True)
        dk, dv = lax.fori_loop((j + 1) * r, n // bq, lambda i, c: tile(j, i, c[0], c[1], False), (dk, dv))
        ks = pl.ds(pl.multiple_of(j * bk, bk), bk)
        dk_ref[ks, :] = (dk * HD ** (-0.5)).astype(jnp.bfloat16)
        dv_ref[ks, :] = dv.astype(jnp.bfloat16)
        return 0

    lax.fori_loop(0, n // bk, kvblock, 0)
    dq_ref[...] = (dq_acc[...] * HD ** (-0.5)).astype(jnp.bfloat16)


def attend_bwd(mixed, attended, lse, grad, bq=512, bk=512):
    n = mixed.shape[0]
    width = mixed.shape[1] // 3
    pairs = width // 128
    spec = lambda off: pl.BlockSpec((n, 128), lambda p, off=off: (0, off + p))
    o = jax.ShapeDtypeStruct((n, width), jnp.bfloat16)
    return pl.pallas_call(
        functools.partial(bwd_kernel, bq, bk),
        grid=(pairs,),
        out_shape=(o, o, o),
        in_specs=[spec(0), spec(pairs), spec(2 * pairs), spec(0), spec(0), pl.BlockSpec((1, 8, n), lambda p: (p, 0, 0))],
        out_specs=(spec(0),) * 3,
        scratch_shapes=[pltpu.VMEM((2, n, 128), jnp.bfloat16)] * 3 + [pltpu.VMEM((8, n), jnp.float32), pltpu.VMEM((n, 128), jnp.float32)],
        compiler_params=pltpu.CompilerParams(vmem_limit_bytes=48 << 20),
        cost_estimate=pl.CostEstimate(flops=10 * n * n * width, bytes_accessed=16 * n * width, transcendentals=n * n * width // 128),
        name="attend_bwd",
    )(mixed, mixed, mixed, grad, attended, lse)


BF = jnp.bfloat16
F32 = jnp.float32
CHUNKS = 4
VMEM_SPEC = pl.BlockSpec(memory_space=pltpu.VMEM)
SMEM_SPEC = pl.BlockSpec(memory_space=pltpu.SMEM)


def remote(src, dst, send_sem, recv_sem, axis, index):
    return pltpu.make_async_remote_copy(
        src_ref=src,
        dst_ref=dst,
        send_sem=send_sem,
        recv_sem=recv_sem,
        device_id={axis: index},
        device_id_type=pl.DeviceIdType.MESH,
    )


class Group:
    def __init__(self, size):
        self.size = size
        self.chips = size // 2
        self.me = lax.axis_index("tensor")
        self.chip = self.me // 2
        self.core = self.me % 2
        self.sibling = self.chip * 2 + 1 - self.core

    def same(self, off):
        return (self.chip + off) % self.chips * 2 + self.core

    def other(self, off):
        return (self.chip + off) % self.chips * 2 + 1 - self.core

    def greet(self, barrier):
        peers = [self.sibling] + [self.same(off) for off in range(1, self.chips)]
        for peer in peers:
            pl.semaphore_signal(
                barrier, inc=1, device_id={"tensor": peer}, device_id_type=pl.DeviceIdType.MESH
            )
        return len(peers)


def loop(count, body):
    def step(k, carry):
        body(k)
        return carry

    lax.fori_loop(0, count, step, 0)


def loop_range(low, high, body):
    def step(k, carry):
        body(k)
        return carry

    lax.fori_loop(low, high, step, 0)


class Gather:
    def __init__(self, group, buf, sem):
        self.g, self.buf, self.sem = group, buf, sem

    def own(self, off, k):
        g, sem = self.g, self.sem
        here = self.buf.at[g.me, k]
        if off == 0:
            return remote(here, here, sem.at[0, 0, k], sem.at[3, 0, k], "tensor", g.sibling)
        return remote(
            here, here, sem.at[0, off, k], sem.at[2, g.chips - off, k], "tensor", g.same(off)
        )

    def passed(self, off, k):
        here = self.buf.at[self.g.same(off), k]
        sem = self.sem
        return remote(here, here, sem.at[1, off, k], sem.at[3, off, k], "tensor", self.g.sibling)

    def send(self, k):
        for off in list(range(1, self.g.chips)) + [0]:
            self.own(off, k).start()

    def forward(self, k):
        g, sem = self.g, self.sem
        for off in range(1, g.chips):
            here = self.buf.at[g.same(off), k]
            remote(
                here, here, sem.at[0, off, k], sem.at[2, off, k], "tensor", g.same(off)
            ).wait_recv()
            self.passed(off, k).start()

    def wait(self, k):
        g, sem = self.g, self.sem
        for off in range(g.chips):
            here = self.buf.at[g.other(off), k]
            remote(
                here, here, sem.at[0, 0, k], sem.at[3, off, k], "tensor", g.sibling
            ).wait_recv()

    def drain(self, k):
        for off in range(self.g.chips):
            self.own(off, k).wait_send()
            if off:
                self.passed(off, k).wait_send()


class Scatter:
    def __init__(self, group, part, in_near, out_far, in_far, sem):
        self.g, self.part, self.sem = group, part, sem
        self.in_near, self.out_far, self.in_far = in_near, out_far, in_far

    def near(self, off, k):
        sem = self.sem
        return remote(
            self.part.at[self.g.other(off), k], self.in_near.at[off, k], sem.at[0, off, k],
            sem.at[1, off, k], "tensor", self.g.sibling,
        )

    def far(self, off, k):
        g, sem = self.g, self.sem
        back = g.chips - off
        return remote(
            self.out_far.at[off - 1, k], self.in_far.at[back - 1, k], sem.at[2, off, k],
            sem.at[3, back, k], "tensor", g.same(off),
        )

    def send(self, k):
        for off in list(range(1, self.g.chips)) + [0]:
            self.near(off, k).start()

    def combine(self, k):
        g = self.g
        for off in range(1, g.chips):
            self.near(off, k).wait_recv()
            total = self.part[g.same(off), k].astype(F32) + self.in_near[off, k].astype(F32)
            self.out_far[off - 1, k] = total.astype(BF)
            self.far(off, k).start()

    def final(self, k):
        g, sem = self.g, self.sem
        self.near(0, k).wait_recv()
        total = self.part[g.me, k].astype(F32) + self.in_near[0, k].astype(F32)
        for off in range(1, g.chips):
            remote(
                self.out_far.at[off - 1, k], self.in_far.at[off - 1, k], sem.at[2, off, k],
                sem.at[3, off, k], "tensor", g.same(off),
            ).wait_recv()
            total = total + self.in_far[off - 1, k].astype(F32)
        return total

    def drain(self, k):
        for off in range(self.g.chips):
            self.near(off, k).wait_send()
            if off:
                self.far(off, k).wait_send()


def scatter_scratch(size, rows, d):
    chips = size // 2
    block = lambda c: pltpu.VMEM((c, CHUNKS, rows, d), BF)
    return [pltpu.VMEM((size, CHUNKS, rows, d), BF), block(chips), block(chips - 1), block(chips - 1)]


def sems(group):
    return pltpu.SemaphoreType.DMA((4, group // 2, CHUNKS))


class Place:
    def __init__(self, count):
        self.count = count
        self.line = count // 2
        self.me = lax.axis_index("dp")
        self.row = self.me // 2
        self.side = self.me % 2
        self.partner = self.row * 2 + 1 - self.side
        self.next = self.row + 1 - self.row % 2 * 2
        self.inner = self.next % 3 == 0

    def at(self, row):
        return row * 2 + self.side

    def peer(self, off):
        return self.at((self.row + off) % self.line)

    def greet(self, barrier):
        peers = [self.partner] + [self.peer(off) for off in range(1, self.line)]
        for peer in peers:
            pl.semaphore_signal(
                barrier, inc=1, device_id={"dp": peer}, device_id_type=pl.DeviceIdType.MESH
            )
        return len(peers)


class Total:
    def __init__(self, place, src, near, far, sem):
        self.p, self.src, self.near, self.far, self.sem = place, src, near, far, sem

    def pair(self):
        p, sem = self.p, self.sem
        return remote(
            self.src.at[1 - p.side], self.near, sem.at[0, 0], sem.at[1, 0], "dp", p.partner
        )

    def outward(self):
        p, sem = self.p, self.sem
        return remote(
            self.near.at[pl.ds(1 - p.row // 3, 3)], self.far.at[pl.ds(0, 3)], sem.at[0, 1],
            sem.at[1, 1], "dp", p.at(p.next),
        )

    def inward(self):
        p, sem = self.p, self.sem
        return remote(
            self.near.at[p.next], self.far.at[0], sem.at[0, 1], sem.at[1, 1], "dp", p.at(p.next)
        )

    def summed(self, i):
        p, sem = self.p, self.sem
        target = (3 - p.row, 3 - p.next)[i]
        return remote(
            self.near.at[target], self.far.at[3], sem.at[0, 2 + i], sem.at[1, 2], "dp", p.at(target)
        )

    def start(self):
        self.pair().start()

    def add(self):
        self.pair().wait_recv()
        for j in range(self.p.line):
            total = self.src[self.p.side, j].astype(F32) + self.near[j].astype(F32)
            self.near[j] = total.astype(BF)

    def scatter(self):
        @pl.when(self.p.inner)
        def _():
            self.inward().start()

        @pl.when(jnp.logical_not(self.p.inner))
        def _():
            self.outward().start()

    def halve(self):
        self.add()
        self.scatter()

    def relay(self):
        p = self.p

        @pl.when(p.inner)
        def _():
            self.outward().wait_recv()
            skip = 2 - p.row
            for i, target in enumerate((3 - p.row, 3 - p.next)):
                total = self.near[target].astype(F32) + self.far[target - skip].astype(F32)
                self.near[target] = total.astype(BF)
                self.summed(i).start()
            total = self.near[p.row].astype(F32) + self.far[p.row - skip].astype(F32)
            self.near[p.row] = total.astype(BF)

        @pl.when(jnp.logical_not(p.inner))
        def _():
            self.inward().wait_recv()
            total = self.near[p.row].astype(F32) + self.far[0].astype(F32)
            self.near[p.row] = total.astype(BF)

    def settle(self):
        self.summed(0).wait_recv()
        return (self.near[self.p.row].astype(F32) + self.far[3].astype(F32)).astype(BF)

    def drain(self, pair=True, pieces=True):
        if pair:
            self.pair().wait_send()
        if not pieces:
            return

        @pl.when(self.p.inner)
        def _():
            self.inward().wait_send()
            self.summed(0).wait_send()
            self.summed(1).wait_send()

        @pl.when(jnp.logical_not(self.p.inner))
        def _():
            self.outward().wait_send()


class Share:
    def __init__(self, place, piece, half, sem):
        self.p, self.piece_at, self.half_at, self.sem = place, piece, half, sem

    def piece(self, i, owner, target):
        p, sem = self.p, self.sem
        here = self.piece_at(p.side, owner)
        return remote(here, here, sem.at[0, i], sem.at[1, owner], "dp", p.at(target))

    def first(self):
        p = self.p
        second = jnp.where(p.inner, 3 - p.row, 3 - p.next)
        return self.piece(0, p.row, p.next), self.piece(1, p.row, second)

    def passed(self):
        p = self.p
        return self.piece(2, 3 - p.row, p.next), self.piece(3, 3 - p.next, p.next)

    def half(self):
        p, sem = self.p, self.sem
        here = self.half_at(p.side)
        return remote(here, here, sem.at[0, 4], sem.at[1, 4], "dp", p.partner)

    def start(self, piece):
        self.piece_at(self.p.side, self.p.row)[...] = piece
        for one in self.first():
            one.start()

    def relay(self):
        p = self.p

        @pl.when(p.inner)
        def _():
            for i, owner in ((2, 3 - p.row), (3, 3 - p.next)):
                self.piece(i, owner, p.next).wait_recv()
                self.piece(i, owner, p.next).start()

    def gathered(self):
        p = self.p
        self.piece(0, p.next, p.next).wait_recv()

        @pl.when(jnp.logical_not(p.inner))
        def _():
            self.piece(0, 3 - p.row, p.next).wait_recv()
            self.piece(0, 3 - p.next, p.next).wait_recv()

    def spread(self):
        self.gathered()
        self.half().start()

    def sent(self):
        p = self.p
        for one in self.first():
            one.wait_send()

        @pl.when(p.inner)
        def _():
            for one in self.passed():
                one.wait_send()

    def finish(self, pieces=True):
        p, sem = self.p, self.sem
        there = self.half_at(1 - p.side)
        remote(there, there, sem.at[0, 4], sem.at[1, 4], "dp", p.partner).wait_recv()
        if pieces:
            self.sent()
        self.half().wait_send()


def total_scratch(line, block):
    return [pltpu.VMEM((line,) + block, BF)] * 2 + [pltpu.SemaphoreType.DMA((2, line))]


ANY_SPEC = pl.BlockSpec(memory_space=pl.ANY)


class Move:
    def __init__(self, src, dst, sem):
        self.copy = pltpu.make_async_copy(src, dst, sem)

    def start(self):
        self.copy.start()
        return self

    def wait(self):
        self.copy.wait()


def norm_stats(x):
    centred = x - jnp.mean(x, axis=-1, keepdims=True)
    inverse = lax.rsqrt(jnp.mean(centred * centred, axis=-1, keepdims=True) + EPS)
    return centred * inverse, inverse


def norm_pull(grad, unit, inverse, gain):
    g = grad * gain
    g = g - jnp.mean(g, axis=-1, keepdims=True) - unit * jnp.mean(g * unit, axis=-1, keepdims=True)
    return g * inverse


def rows_of(ref, k, cols=slice(None)):
    x = ref[:, k, :, cols]
    return x.reshape(x.shape[0] * x.shape[1], x.shape[2])


def col_sum(x):
    return jnp.sum(x, axis=0, keepdims=True)


def enter_kernel(group):
    barrier = pltpu.get_barrier_semaphore()
    pl.semaphore_wait(barrier, group.greet(barrier))


def fold(x, op):
    r = x[:, :128]
    for c in range(1, x.shape[1] // 128):
        r = op(r, x[:, c * 128:(c + 1) * 128])
    return r


class Attend:
    def __init__(self, size, units, length, mixed, out, lse, scores, values):
        self.size, self.units, self.length = size, units, length
        self.mixed, self.out, self.lse, self.scores, self.values = mixed, out, lse, scores, values
        self.width = out.shape[-1]
        self.pairs = self.width // 128
        self.block = mixed.shape[0] // size
        self.rows = self.block // units
        lane = lax.broadcasted_iota(jnp.int32, (1, 128), 1)
        self.heads = [lane < HD, lane >= HD]

    def prepare(self):
        for x in range(self.pairs):
            for h in range(2):
                v = self.mixed[:, 2 * self.width + x * 128:2 * self.width + (x + 1) * 128]
                self.values[2 * x + h] = jnp.where(self.heads[h], v, jnp.zeros_like(v))

    def run(self, u, event=None):
        def body(i):
            self.unit(u, i // self.pairs, i % self.pairs)
            if event is not None:
                pl.when(i == (self.size - 1) * self.pairs - 1)(event)

        loop(self.size * self.pairs, body)

    def unit(self, u, s, x):
        bq, bk = self.rows, self.block
        lanes = pl.ds(pl.multiple_of(x * 128, 128), 128)
        k_lanes = pl.ds(pl.multiple_of(self.width + x * 128, 128), 128)
        k0 = pl.multiple_of(s * bk, bk)
        q0 = pl.multiple_of(s * bk + u * bq, bq)
        qb = self.mixed[pl.ds(q0, bq), lanes]
        qh = [jnp.where(self.heads[h], qb, jnp.zeros_like(qb)) for h in range(2)]
        edge = (u + 1) * bq
        row = lax.broadcasted_iota(jnp.int32, (bq, edge), 0) + u * bq
        mask = lax.broadcasted_iota(jnp.int32, (bq, edge), 1) <= row
        zero = jnp.zeros((bq, 128), F32)

        def first(j, most):
            kb = self.mixed[pl.ds(pl.multiple_of(j * bk, bk), bk), k_lanes]
            new = []
            for h in range(2):
                sc = mm(qh[h], kb, NT)
                self.scores[h, j] = sc
                new.append(jnp.maximum(most[h], fold(jnp.abs(sc), jnp.maximum)))
            return tuple(new)

        most = lax.fori_loop(0, s, first, (zero, zero))
        kb = self.mixed[pl.ds(k0, edge), k_lanes]
        top, state = [], []
        for h in range(2):
            sc = jnp.where(mask, mm(qh[h], kb, NT), 0.0)
            m = jnp.maximum(most[h], fold(jnp.abs(sc), jnp.maximum))
            top.append(jnp.max(m, axis=1, keepdims=True) * SC)
            e = jnp.where(mask, jnp.exp2(jnp.abs(sc) * SC - top[h]), 0.0)
            w = (sgn_of(sc) * e).astype(BF)
            state.append((mm(w, self.values[2 * x + h, pl.ds(k0, edge), :], NN), fold(e, jnp.add)))

        def second(j, carry):
            new = []
            for h in range(2):
                acc, total = carry[h]
                sc = self.scores[h, j]
                e = jnp.exp2(jnp.abs(sc) * SC - top[h])
                w = (sgn_of(sc) * e).astype(BF)
                rows = pl.ds(pl.multiple_of(j * bk, bk), bk)
                acc = acc + mm(w, self.values[2 * x + h, rows, :], NN)
                new.append((acc, total + fold(e, jnp.add)))
            return tuple(new)

        state = lax.fori_loop(0, s, second, tuple(state))
        result = 0.0
        for h in range(2):
            total = jnp.sum(state[h][1], axis=1, keepdims=True)
            result = result + state[h][0] / total
            log_total = jnp.broadcast_to(top[h] + jnp.log(total) * LOG2E, (bq, 128))
            self.lse[x, h:h + 1, pl.ds(q0, bq)] = jnp.transpose(log_total)[0:1, :]
        live = (lax.broadcasted_iota(jnp.int32, (bq, 1), 0) + q0) < self.length[0]
        self.out[pl.ds(q0, bq), lanes] = jnp.where(live, result, 0.0).astype(BF)


def core_kernel(
    size, count, length, gain1, shift1, tb, mb, gain, shift, ub,
    w_hbm, tok_hbm, cot_hbm, mw_hbm, up_hbm, down_hbm,
    full_hbm, mixed_hbm, att, lse, gatt, gres_hbm, resid_hbm, pout_hbm, g_merge, small, bias, *rest,
):
    if count:
        (pieces, held, raw, rest) = (rest[:2], rest[2], rest[3], rest[4:])
    else:
        (g_up, g_down, rest) = (rest[0], rest[1], rest[2:])
    (
        w, mixed, tok, cot, mw, up, down, scores, values, resid, gres, pout, part, in_near, out_far, in_far,
        full, hid, gb, sem0, sem1, sem2, sem3, sem4, sem5, load_sem, cot_sem, out_sem, free,
    ) = rest[:29]
    rest = rest[29:]
    g = Group(size)
    rows, d = tok.shape[0] // CHUNKS, tok.shape[1]
    width, units = mw.shape[0], up.shape[1]
    step = min(512, units)
    p = Place(count) if count else None
    span = lambda k: pl.ds(pl.multiple_of(k * rows, rows), rows)
    loads = [
        Move(src, dst, load_sem.at[i]).start()
        for i, (src, dst) in enumerate(
            ((tok_hbm, tok), (w_hbm, w), (mw_hbm, mw), (up_hbm, up), (down_hbm, down))
        )
    ]
    own = lambda k: Move(cot_hbm.at[k], cot.at[g.me, k], cot_sem.at[k])
    loop(CHUNKS, lambda k: own(k).start())
    begin = Gather(g, full, sem0)
    barrier = pltpu.get_barrier_semaphore()
    pl.semaphore_wait(barrier, g.greet(barrier) + (p.greet(barrier) if count else 0))
    tops = Gather(g, cot, sem5)
    first = Scatter(g, part, in_near, out_far, in_far, sem1)
    spread = Gather(g, full, sem2)
    second = Scatter(g, part, in_near, out_far, in_far, sem3)
    if units == d:
        gfull = hid
    else:
        gfull, rest = rest[0], rest[1:]
    back = Gather(g, gfull, sem4)
    sums = []
    if count:
        g_up, g_down, rest = rest[0], rest[1], rest[2:]
        for ref in (g_down.at[0], g_down.at[1], g_up.at[0]):
            near, far, sem = rest[:3]
            rest = rest[3:]
            sums.append(Total(p, ref, near, far, sem))

    def at(s, k):
        return pl.ds(pl.multiple_of((s * CHUNKS + k) * rows, rows), rows)

    def enter(k):
        unit, _ = norm_stats(tok[span(k), :].astype(F32))
        full[g.me, k] = (unit * gain1[...] + shift1[...]).astype(BF)
        begin.send(k)

    loads[0].wait()
    loop(CHUNKS, enter)

    def mask(k):
        own(k).wait()
        row = lax.broadcasted_iota(jnp.int32, (rows, 1), 0) + (g.me * CHUNKS + k) * rows
        cot[g.me, k] = jnp.where(row < length[0], cot[g.me, k].astype(F32), 0.0).astype(BF)
        tops.send(k)

    loop(CHUNKS, mask)
    loads[1].wait()

    def full_store(k):
        return Move(full.at[:, k], full_hbm.at[:, k], out_sem.at[3, k])

    def project(k):
        begin.wait(k)
        full_store(k).start()
        x = rows_of(full, k)
        for j in range(3):
            cols = slice(j * width, (j + 1) * width)
            y = (mm(x, w[j], NN) + tb[j:j + 1, :]).astype(BF)
            for s in range(size):
                mixed[at(s, k), cols] = y[s * rows:(s + 1) * rows]

    def begin_step(k):
        begin.forward(k)

        @pl.when(k > 0)
        def _():
            project(k - 1)

    loop(CHUNKS, begin_step)
    project(CHUNKS - 1)
    mixed_store = Move(mixed, mixed_hbm, load_sem.at[5]).start()
    attend = Attend(size, 2, length, mixed, att, lse, scores, values)
    attend.prepare()

    def merge(k):
        x = jnp.concatenate([att[at(s, k), :] for s in range(size)], axis=0)
        y = mm(x, mw[...], NN).astype(BF)
        for s in range(size):
            part[s, k] = y[s * rows:(s + 1) * rows]
        first.send(k)

    def resid_store(k):
        return Move(resid.at[span(k)], resid_hbm.at[span(k)], out_sem.at[0, k])

    def norm(k):
        x = tok[span(k), :].astype(F32) + first.final(k) + mb[...]
        resid[span(k), :] = x
        resid_store(k).start()
        unit, _ = norm_stats(x)
        full[g.me, k] = (unit * gain[...] + shift[...]).astype(BF)
        spread.send(k)

    def inner(k):
        spread.forward(k)
        spread.wait(k)
        x = rows_of(full, k)
        top = rows_of(cot, k)

        def tile(j):
            cols = pl.ds(pl.multiple_of(j * step, step), step)
            v = mm(x, up[:, cols], NN) + ub[:, cols]
            gh = mm(top, down[cols, :], NT)
            c0, c1 = 0.7978845608, 0.044715
            v2 = v * v
            th = jnp.tanh(c0 * (v + c1 * v2 * v))
            half = 0.5 * (1.0 + th)
            h = (v * half).astype(BF)
            slope = half + 0.5 * v * (1.0 - th * th) * (c0 * (1.0 + 3.0 * c1 * v2))
            gv = (gh * slope).astype(BF)
            bias[0:1, cols] += col_sum(gv.astype(F32))
            for s in range(size):
                hid[s, k, :, cols] = h[s * rows:(s + 1) * rows]
                gb[s, k, :, cols] = gv[s * rows:(s + 1) * rows]

        loop(units // step, tile)

    def pout_store(k):
        return Move(pout.at[k % 2], pout_hbm.at[:, k], out_sem.at[1, k])

    def leave(k):
        h, gv = rows_of(hid, k), rows_of(gb, k)

        @pl.when(k >= 2)
        def _():
            pout_store(k - 2).wait()

        def tile(j):
            cols = pl.ds(pl.multiple_of(j * 512, 512), 512)
            y = mm(h, down[:, cols], NN).astype(BF)
            z = mm(gv, up[cols, :], NT).astype(BF)
            for s in range(size):
                pout[k % 2, s, :, cols] = y[s * rows:(s + 1) * rows]
                part[s, k, :, cols] = z[s * rows:(s + 1) * rows]

        loop(d // 512, tile)
        pout_store(k).start()
        second.send(k)

    def flat(ref, cols):
        x = ref[:, :, :, cols]
        return x.reshape(size * CHUNKS * rows, x.shape[3])

    def products(ref, left, right, extent):
        tall = min(256, extent)

        def block(i):
            cols = pl.ds(pl.multiple_of(i * tall, tall), tall)
            y = mm(flat(left, cols), flat(right, slice(None)), TN).astype(BF)
            if not count:
                ref[cols, :] = y
            else:
                deep = ref.shape[3]
                for e in range(tall // deep):
                    f = i * (tall // deep) + e
                    ref[f // (2 * p.line), f // p.line % 2, f % p.line] = y[e * deep:(e + 1) * deep]

        return block, extent // tall

    def weights(ref, left, right, extent, event=None):
        block, blocks = products(ref, left, right, extent)
        after(0, blocks, block, {blocks // 2 - 1: event})

    def after(low, high, body, events):
        def step(k):
            body(k)
            for at_k, event in events.items():
                if count and event is not None:
                    pl.when(k == at_k)(event)

        loop_range(low, high, step)

    def gres_store(k):
        return Move(gres.at[k % 2], gres_hbm.at[span(k)], out_sem.at[2, k])

    def pull(k):
        gs = second.final(k)
        unit, inverse = norm_stats(resid[span(k), :])
        top = cot[g.me, k].astype(F32)
        gr = top + norm_pull(gs, unit, inverse, gain[...])

        @pl.when(k >= 2)
        def _():
            gres_store(k - 2).wait()

        gres[k % 2] = gr
        gres_store(k).start()
        gfull[g.me, k] = gr.astype(BF)
        back.send(k)
        small[2:3, :] += col_sum(gr)
        small[3:4, :] += col_sum(gs * unit)
        small[4:5, :] += col_sum(gs)
        small[5:6, :] += col_sum(top)

    def last(k):
        back.forward(k)
        back.wait(k)
        y = mm(rows_of(gfull, k), mw[...], NT)
        for s in range(size):
            row = lax.broadcasted_iota(jnp.int32, (rows, 1), 0) + (s * CHUNKS + k) * rows
            gatt[s, k] = jnp.where(row < length[0], y[s * rows:(s + 1) * rows], 0.0).astype(BF)

    def later(*steps):
        if count:
            for one in steps:
                one()

    bias[...] = jnp.zeros_like(bias)
    small[...] = jnp.zeros_like(small)
    attend.run(0)
    for load in loads[2:]:
        load.wait()
    loop(CHUNKS, begin.drain)
    loop(CHUNKS, lambda k: full_store(k).wait())
    loop(2, merge)
    loop(2, first.combine)
    loop(2, tops.forward)

    def between():
        loop_range(2, CHUNKS, tops.forward)
        loop(2, norm)

    attend.run(1, between)
    loop_range(2, CHUNKS, merge)
    loop_range(2, CHUNKS, first.combine)
    loop(CHUNKS, tops.wait)
    loop(2, inner)
    loop(2, first.drain)
    loop(2, leave)
    loop_range(2, CHUNKS, norm)
    loop(2, second.combine)
    loop_range(2, CHUNKS, first.drain)
    loop_range(2, CHUNKS, inner)
    weights(g_down, hid, cot, units, sums[0].start if count else None)
    pl.semaphore_wait(free, g.greet(free))
    loop(2, pull)
    after(2, CHUNKS, leave, {2: sums[1].start if count else None})
    loop_range(2, CHUNKS, second.combine)
    later(lambda: sums[0].halve())
    weights(g_up, full, gb, d)
    later(lambda: sums[2].start())
    loop(CHUNKS, tops.drain)
    loop(CHUNKS, spread.drain)

    def turn():
        sums[0].relay()
        sums[1].halve()

    after(2, CHUNKS, pull, {2: turn})
    after(0, CHUNKS, last, {0: lambda: sums[1].relay()})
    y = mm(att[...], flat(gfull, slice(None)), TN).astype(BF)
    if count:
        deep = g_merge.shape[2]
        for f in range(2 * p.line):
            g_merge[f // p.line, f % p.line] = y[f * deep:(f + 1) * deep]
        raw[...] = g_up[1]
        sums[2].add()
        held[...] = sums[2].near[...]
        pieces[0][...] = sums[0].settle()
        pieces[1][...] = sums[1].settle()
        for h in range(3):
            sums[h].drain(True, h < 2)
    else:
        g_merge[...] = y
    loop(CHUNKS, second.drain)
    loop(CHUNKS, back.drain)
    loop(CHUNKS, lambda k: resid_store(k).wait())
    mixed_store.wait()
    loop_range(2, CHUNKS, lambda k: pout_store(k).wait())
    loop_range(2, CHUNKS, lambda k: gres_store(k).wait())


def core(size, count, lengths, gain1, shift1, tb, mb, gain, shift, ub, w, tokens, cotangent, mw,
         up, down):
    rows, d = tokens.shape
    r = rows // CHUNKS
    n = rows * size
    width, units = mw.shape[0], up.shape[1]
    pairs = width // 128
    shape = jax.ShapeDtypeStruct
    dma = pltpu.SemaphoreType.DMA
    vm = pltpu.VMEM
    wide = lambda c: vm((size, CHUNKS, r, c), BF)
    line = count // 2
    if count:
        blocks = ((2, 2, line, d // (4 * line), units), (2, 2, line, units // (4 * line), d))
        merge = shape((2, line, width // (2 * line), d), BF)
        piece = [shape(b[3:], BF) for b in blocks[::-1]]
        extra = (piece[0], piece[0], shape((line,) + blocks[0][3:], BF), shape(blocks[0][1:], BF))
        scratch = [vm(b, BF) for b in blocks]
        scratch += total_scratch(line, blocks[1][3:]) * 2 + total_scratch(line, blocks[0][3:])
    else:
        merge = shape((width, d), BF)
        extra = (shape((d, units), BF), shape((units, d), BF))
        scratch = []
    if units != d:
        scratch = [wide(d)] + scratch
    outs = (
        (shape((size, CHUNKS, r, d), BF), ANY_SPEC),
        (shape((n, 3 * width), BF), ANY_SPEC),
        (shape((n, width), BF), VMEM_SPEC),
        (shape((pairs, 8, n), F32), VMEM_SPEC),
        (shape((size, CHUNKS, r, width), BF), VMEM_SPEC),
        (shape((rows, d), F32), ANY_SPEC),
        (shape((rows, d), F32), ANY_SPEC),
        (shape((size, CHUNKS, r, d), BF), ANY_SPEC),
        (merge, VMEM_SPEC),
        (shape((8, d), F32), VMEM_SPEC),
        (shape((8, units), F32), VMEM_SPEC),
        *((x, VMEM_SPEC) for x in extra),
    )
    return pl.pallas_call(
        functools.partial(core_kernel, size, count),
        out_shape=tuple(x for x, _ in outs),
        in_specs=[SMEM_SPEC] + [VMEM_SPEC] * 7 + [ANY_SPEC] * 6,
        out_specs=tuple(x for _, x in outs),
        scratch_shapes=[
            vm(w.shape, BF), vm((n, 3 * width), BF), vm((rows, d), BF), wide(d), vm((width, d), BF), vm((d, units), BF), vm((units, d), BF),
            vm((2, size, rows // 2, rows), F32), vm((2 * pairs, n, 128), BF), vm((rows, d), F32),
            vm((2, r, d), F32), vm((2, size, r, d), BF),
        ]
        + scatter_scratch(size, r, d)
        + [wide(d), wide(units), wide(units)]
        + [sems(size)] * 6
        + [dma((6,)), dma((CHUNKS,)), dma((4, CHUNKS)), pltpu.SemaphoreType.REGULAR]
        + scratch,
        compiler_params=pltpu.CompilerParams(
            collective_id=1, has_side_effects=True, vmem_limit_bytes=64 << 20
        ),
        name="core",
    )(lengths, gain1, shift1, tb, mb, gain, shift, ub, w, tokens, cotangent.reshape(CHUNKS, r, d), mw,
      up, down)


def tail_kernel(
    size, dq, dk, dv, full, w, tok, gres, gain,
    gtok, g_triple, small, bias,
    part, in_near, out_far, in_far, sem,
):
    g = Group(size)
    rows, d = tok.shape[0] // CHUNKS, tok.shape[1]
    width = dq.shape[3]
    enter_kernel(g)
    scatter = Scatter(g, part, in_near, out_far, in_far, sem)
    span = lambda k: pl.ds(pl.multiple_of(k * rows, rows), rows)
    grads = (dq, dk, dv)

    def back(k):
        def tile(j):
            cols = pl.ds(pl.multiple_of(j * 256, 256), 256)
            z = sum(
                mm(rows_of(x, k), w[c, cols, :], NT)
                for c, x in enumerate(grads)
            )
            for s in range(size):
                part[s, k, :, cols] = z[s * rows:(s + 1) * rows].astype(BF)

        loop(d // 256, tile)
        scatter.send(k)

    loop(CHUNKS, back)
    loop(CHUNKS, scatter.combine)

    def flat(ref, cols):
        x = ref[:, :, :, cols]
        return x.reshape(size * CHUNKS * rows, x.shape[3])

    bias[...] = jnp.zeros_like(bias)
    for c, x in enumerate(grads):
        y = flat(x, slice(None))
        bias[0:1, c * width:(c + 1) * width] = col_sum(y.astype(F32))

        def tile(i):
            more = pl.ds(pl.multiple_of(i * 256, 256), 256)
            g_triple[c, more, :] = mm(flat(full, more), y, TN).astype(BF)

        loop(d // 256, tile)
    small[...] = jnp.zeros_like(small)

    def pull(k):
        gf = scatter.final(k)
        unit, inverse = norm_stats(tok[span(k), :].astype(F32))
        gtok[span(k), :] = gres[span(k), :] + norm_pull(gf, unit, inverse, gain[...])
        small[0:1, :] += col_sum(gf * unit)
        small[1:2, :] += col_sum(gf)

    loop(CHUNKS, pull)
    loop(CHUNKS, scatter.drain)


def tail(size, dq, dk, dv, full, w, tokens, gres, gain):
    rows, d = tokens.shape
    r = rows // CHUNKS
    width = dq.shape[-1]
    shape = jax.ShapeDtypeStruct
    return pl.pallas_call(
        functools.partial(tail_kernel, size),
        out_shape=(
            shape((rows, d), F32),
            shape((3, d, width), BF),
            shape((8, d), F32),
            shape((8, 3 * width), F32),
        ),
        in_specs=[VMEM_SPEC] * 8,
        out_specs=(VMEM_SPEC,) * 4,
        scratch_shapes=scatter_scratch(size, r, d) + [sems(size)],
        compiler_params=pltpu.CompilerParams(
            collective_id=2, has_side_effects=True, vmem_limit_bytes=56 << 20
        ),
        name="tail",
    )(dq, dk, dv, full, w, tokens, gres, gain)


class Everyone:
    def __init__(self, axis, count, buf, sem):
        self.axis, self.count, self.buf, self.sem = axis, count, buf, sem
        self.me = lax.axis_index(axis)

    def copy(self, owner, off, back):
        here = self.buf.at[owner]
        return remote(
            here, here, self.sem.at[0, off], self.sem.at[1, back], self.axis,
            (self.me + off) % self.count,
        )

    def start(self, value):
        self.buf[self.me] = value
        for off in range(1, self.count):
            self.copy(self.me, off, self.count - off).start()

    def finish(self):
        for off in range(1, self.count):
            self.copy((self.me + off) % self.count, off, off).wait_recv()
        total = self.buf[0]
        for j in range(1, self.count):
            total = total + self.buf[j]
        for off in range(1, self.count):
            self.copy(self.me, off, self.count - off).wait_send()
        return total


def late_kernel(
    size, count, bk, gain, db, p_down0, p_down1, u_held, u_raw, g_merge, small_in, bias_in,
    mixed_hbm, att_hbm, gatt_hbm, lse_hbm, full_hbm, w_hbm, tok_hbm, gres_hbm, resid_hbm, pout_hbm,
    out_hbm, gtok_hbm, down_hbm, up_hbm, merge_hbm, o_triple, small,
    mixed, att, gatt, lse, full, w, tok, gres, resid, pout, load_sem,
    qm, km, dom, dsc, dq_acc, gm, g_triple, part, in_near, out_far, in_far,
    in_near2, out_far2, in_far2, sem, sem2, u_far, u_sem, v_near, v_far, v_sem,
    m_near, m_far, m_sem, t_near, t_far, t_sem, s_sem, t_buf, t_sems, d_buf, d_sems, g_sem,
    t_buf2, t_sems2, d_buf2, d_sems2, o_down, o_up, o_merge, o_sem, out_sem,
):
    loads = [
        Move(src, dst, load_sem.at[i]).start()
        for i, (src, dst) in enumerate(
            (
                (mixed_hbm, mixed), (gatt_hbm, gatt), (att_hbm, att), (lse_hbm, lse),
                (pout_hbm, pout), (resid_hbm, resid), (full_hbm, full), (w_hbm, w),
                (tok_hbm, tok), (gres_hbm, gres),
            )
        )
    ]
    g, p = Group(size), Place(count)
    n = mixed.shape[0]
    rows, d = tok.shape[0] // CHUNKS, tok.shape[1]
    width = att.shape[1]
    pairs = width // 128
    barrier = pltpu.get_barrier_semaphore()
    for axis, extent in (("tensor", size), ("dp", count)):
        for off in range(1, extent):
            pl.semaphore_signal(
                barrier,
                inc=1,
                device_id={axis: (lax.axis_index(axis) + off) % extent},
                device_id_type=pl.DeviceIdType.MESH,
            )
    pl.semaphore_wait(barrier, size + count - 2)

    def share(ref, sem):
        return Share(p, lambda side, line: ref.at[side, line], lambda side: ref.at[side], sem)

    deep = g_triple.shape[5]

    def triple_share(x, h):
        lanes, part_rows = pl.ds(x * 128, 128), pl.ds(h * deep, deep)
        return Share(
            p,
            lambda side, line: o_triple.at[:, side, line, part_rows, lanes],
            lambda side: o_triple.at[:, side, :, part_rows, lanes],
            s_sem.at[5 + 2 * x + h],
        )

    def triple_total(x, h):
        return Total(p, g_triple.at[x, h], t_near.at[x, h], t_far.at[x, h], t_sem.at[x, h])

    shares = [
        share(ref.at[h], s_sem.at[2 * a + h])
        for a, ref in enumerate((o_down, o_up))
        for h in range(2)
    ]
    merge_total = Total(p, g_merge, m_near, m_far, m_sem)
    merge_share = share(o_merge, s_sem.at[4])
    totals = [triple_total(x, h) for x in range(pairs) for h in range(2)]
    triples = [triple_share(x, h) for x in range(pairs) for h in range(2)]
    branch = Scatter(g, pout, in_near2, out_far2, in_far2, sem2)
    up_total = Total(p, None, u_held, u_far, u_sem)
    raw_total = Total(p, u_raw, v_near, v_far, v_sem)
    raw_total.start()
    shares[0].start(p_down0[...])
    group_early = Everyone("tensor", size, t_buf, t_sems)
    all_early = Everyone("dp", count, d_buf, d_sems)
    group_early.start(small_in[...])

    def early():
        small[...] = group_early.finish()
    for load in loads[:4]:
        load.wait()

    lane = lax.broadcasted_iota(jnp.int32, (1, 128), 1)
    heads = [lane < HD, lane >= HD]
    row = lax.broadcasted_iota(jnp.int32, (bk, bk), 0)
    col = lax.broadcasted_iota(jnp.int32, (bk, bk), 1)

    def attention(x, events):
        def lanes(c):
            return pl.ds(pl.multiple_of(c * width + x * 128, 128), 128)

        def prepare(i):
            sl = pl.ds(pl.multiple_of(i * bk, bk), bk)
            z = jnp.zeros((bk, 128), BF)
            for h in range(2):
                qm[h, sl, :] = jnp.where(heads[h], mixed[sl, lanes(0)], z)
                km[h, sl, :] = jnp.where(heads[h], mixed[sl, lanes(1)], z)
                do = jnp.where(heads[h], gatt[sl, lanes(0)], z)
                dom[h, sl, :] = do
                prod = do.astype(F32) * att[sl, lanes(0)].astype(F32)
                dd = jnp.broadcast_to(jnp.sum(prod, axis=1, keepdims=True), (bk, 128))
                dsc[h:h + 1, sl] = jnp.transpose(dd)[0:1, :]
            dq_acc[sl, :] = jnp.zeros((bk, 128), F32)

        loop(n // bk, prepare)

        def tile(j, i, dk, dv, diag):
            ks, qs = pl.ds(pl.multiple_of(j * bk, bk), bk), pl.ds(pl.multiple_of(i * bk, bk), bk)
            kb, vb = mixed[ks, lanes(1)], mixed[ks, lanes(2)]
            dq = None
            for h in range(2):
                qh, doh = qm[h, qs, :], dom[h, qs, :]
                s = mm(kb, qh, NT)
                dp = mm(vb, doh, NT)
                e = jnp.exp2(jnp.abs(s) * SC - lse[x, h:h + 1, qs])
                if diag:
                    e = jnp.where(row <= col, e, 0.0)
                sg = sgn_of(s)
                a = sg * e
                ds = (a * (sg * dp - dsc[h:h + 1, qs])).astype(BF)
                dv = dv + mm(a.astype(BF), doh, NN)
                dk = dk + mm(ds, qh, NN)
                t = mm(ds, km[h, ks, :], TN)
                dq = t if dq is None else dq + t
            dq_acc[qs, :] += dq
            return dk, dv

        def serve(j, i):
            for at_x, at_j, at_i, event in events:
                pl.when((x == at_x) & (j == at_j) & (i == at_i))(event)

        def block(j):
            serve(j, j)
            z = jnp.zeros((bk, 128), F32)
            dk, dv = tile(j, j, z, z, True)

            def more(i, c):
                serve(j, i)
                return tile(j, i, c[0], c[1], False)

            dk, dv = lax.fori_loop(j + 1, n // bk, more, (dk, dv))
            ks = pl.ds(pl.multiple_of(j * bk, bk), bk)
            gm[1, ks, lanes(0)] = (dk * HD ** (-0.5)).astype(BF)
            gm[2, ks, lanes(0)] = dv.astype(BF)

        loop(n // bk, block)
        gm[0, :, lanes(0)] = (dq_acc[...] * HD ** (-0.5)).astype(BF)

    def flat(ref, cols):
        y = ref[:, :, :, cols]
        return y.reshape(n, y.shape[3])

    def weights(x):
        mine = pl.ds(pl.multiple_of(x * 128, 128), 128)
        y = jnp.concatenate([gm[c, :, mine] for c in range(3)], axis=1)

        def tile(i):
            z = mm(flat(full, pl.ds(pl.multiple_of(i * 256, 256), 256)), y, TN).astype(BF)
            for e in range(128 // deep):
                f = i * (128 // deep) + e
                for h in range(2):
                    at = (2 * e + h) * deep
                    for c in range(3):
                        g_triple[x, h, f // p.line, f % p.line, c] = z[
                            at:at + deep, c * 128:(c + 1) * 128
                        ]

        loop(d // 256, tile)
        triple_total(x, 0).start()

    span = lambda k: pl.ds(pl.multiple_of(k * rows, rows), rows)

    def branch_start():
        loads[4].wait()
        loop(CHUNKS, branch.send)

    def out_store(k):
        return Move(pout.at[g.me, k], out_hbm.at[span(k)], out_sem.at[k])

    def branch_end():
        loads[5].wait()

        def one(k):
            pout[g.me, k] = (resid[span(k), :] + branch.final(k) + db[...]).astype(BF)
            out_store(k).start()

        loop(CHUNKS, one)

    span = lambda k: pl.ds(pl.multiple_of(k * rows, rows), rows)

    def branch_start():
        loads[4].wait()
        loop(CHUNKS, branch.send)

    def out_store(k):
        return Move(pout.at[g.me, k], out_hbm.at[span(k)], out_sem.at[k])

    def branch_end():
        loads[5].wait()

        def one(k):
            pout[g.me, k] = (resid[span(k), :] + branch.final(k) + db[...]).astype(BF)
            out_store(k).start()

        loop(CHUNKS, one)

    schedule = [[] for _ in range(pairs)]
    end = pairs - 1
    events = [
        (0, 0, 0, branch_start),
        (0, 0, 2, up_total.scatter),
        (0, 1, 1, shares[0].relay),
        (0, 1, 1, lambda: loop(CHUNKS, branch.combine)),
        (0, 1, 1, early),
        (0, 1, 2, lambda: shares[1].start(p_down1[...])),
        (0, 1, 3, shares[0].spread),
        (0, 1, 3, raw_total.halve),
        (0, 2, 2, up_total.relay),
        (0, 3, 3, shares[1].relay),
        (0, 3, 3, merge_total.start),
        (end, 0, 0, raw_total.relay),
        (end, 0, 1, lambda: shares[2].start(up_total.settle())),
        (end, 0, 1, shares[1].spread),
        (end, 0, 2, totals[1].start),
        (end, 0, 3, lambda: shares[3].start(raw_total.settle())),
        (end, 0, 3, shares[2].relay),
        (end, 1, 1, branch_end),
        (end, 1, 1, totals[0].halve),
        (end, 1, 2, merge_total.halve),
        (end, 1, 3, shares[2].spread),
        (end, 2, 2, shares[3].relay),
        (end, 2, 3, totals[1].halve),
        (end, 2, 3, totals[0].relay),
        (end, 3, 3, merge_total.relay),
        (end, 3, 3, shares[3].spread),
    ]

    def pair(x):
        attention(x, events)

        @pl.when(x < end)
        def _():
            pl.when(x == 0)(lambda: [load.wait() for load in loads[6:]] and None)
            weights(x)

    loop(pairs, pair)

    scatter = Scatter(g, part, in_near, out_far, in_far, sem)

    def back(k):
        def tile(j):
            cols = pl.ds(pl.multiple_of(j * 256, 256), 256)
            z = 0.0
            for c in range(3):
                y = jnp.concatenate(
                    [
                        gm[c, pl.ds(pl.multiple_of((s * CHUNKS + k) * rows, rows), rows), :]
                        for s in range(size)
                    ],
                    axis=0,
                )
                z = z + mm(y, w[c, cols, :], NT)
            for s in range(size):
                part[s, k, :, cols] = z[s * rows:(s + 1) * rows].astype(BF)

        loop(d // 256, tile)
        scatter.send(k)

    near_end, far_end = totals[-2:]
    loop(2, back)
    scatter.combine(0)
    triples[0].start(totals[0].settle())
    scatter.combine(1)
    totals[1].relay()
    weights(end)
    merge_share.start(merge_total.settle())

    def back_step(k):
        back(k)

        @pl.when(k == 2)
        def _():
            far_end.start()
            triples[1].start(totals[1].settle())

    loop_range(2, CHUNKS, back_step)
    scatter.combine(2)
    merge_share.relay()
    scatter.combine(3)
    units = bias_in.shape[1]
    small[6:7, :units] = bias_in[0:1, :]
    for c in range(3):
        small[7:8, c * width:(c + 1) * width] = col_sum(gm[c].astype(F32))
    all_early.start(small[...])
    small[0:2, :] = jnp.zeros((2, d), F32)

    def gtok_store(k):
        return Move(gres.at[span(k)], gtok_hbm.at[span(k)], g_sem.at[k])

    def pull(k):
        gf = scatter.final(k)
        unit, inverse = norm_stats(tok[span(k), :].astype(F32))
        gres[span(k), :] += norm_pull(gf, unit, inverse, gain[...])
        gtok_store(k).start()
        small[0:1, :] += col_sum(gf * unit)
        small[1:2, :] += col_sum(gf)

    near_end.halve()
    triples[0].relay()
    merge_share.spread()
    far_end.halve()
    near_end.relay()
    triples[1].relay()
    triples[0].spread()

    def pull_step(k):
        pull(k)

        @pl.when(k == 1)
        def _():
            triples[-2].start(near_end.settle())
            far_end.relay()
            triples[1].spread()
            triples[-2].relay()
            triples[-1].start(far_end.settle())

        @pl.when(k == 2)
        def _():
            triples[-2].spread()
            triples[-1].relay()

    loop(CHUNKS, pull_step)
    quarter = d // 4
    group_sum = Everyone("tensor", size, t_buf2, t_sems2)
    all_sum = Everyone("dp", count, d_buf2, d_sems2)
    group_sum.start(
        jnp.concatenate(
            [small[r:r + 1, c * quarter:(c + 1) * quarter] for r in range(2) for c in range(4)],
            axis=0,
        )
    )
    triples[-1].spread()
    all_sum.start(group_sum.finish())
    stores = [
        Move(ref, hbm, o_sem.at[i])
        for i, (ref, hbm) in enumerate(((o_down, down_hbm), (o_up, up_hbm), (o_merge, merge_hbm)))
    ]
    for one, store in ((shares[:2], stores[0]), (shares[2:], stores[1]), ([merge_share], stores[2])):
        for x in one:
            x.finish()
        store.start()
    small[...] = all_early.finish()
    total = all_sum.finish()
    for r in range(2):
        for c in range(4):
            i = 4 * r + c
            small[r:r + 1, c * quarter:(c + 1) * quarter] = total[i:i + 1, :]
    for one in triples:
        one.finish()
    for store in stores:
        store.wait()
    merge_total.drain()
    up_total.drain(False)
    raw_total.drain()
    for t in totals:
        t.drain()
    loop(CHUNKS, scatter.drain)
    loop(CHUNKS, branch.drain)
    loop(CHUNKS, lambda k: gtok_store(k).wait())
    loop(CHUNKS, lambda k: out_store(k).wait())


def late(size, count, gain, db, p_down0, p_down1, u_held, u_raw, g_merge, small_in, bias_in,
         mixed, att, gatt, lse, full, w, tokens, gres, resid, pout):
    rows, d = tokens.shape
    n, width = att.shape
    r = rows // CHUNKS
    line = count // 2
    pairs = width // 128
    bk = min(512, n)
    shape = jax.ShapeDtypeStruct
    piece = d // count
    vm = pltpu.VMEM
    dma = pltpu.SemaphoreType.DMA
    deep = g_merge.shape[2]
    scatter = scatter_scratch(size, r, d)
    loads = (mixed, att, gatt, lse, full, w, tokens, gres, resid, pout)
    return pl.pallas_call(
        functools.partial(late_kernel, size, count, bk),
        out_shape=(
            shape((rows, d), BF),
            shape((rows, d), F32),
            shape((2, 2, line) + p_down1.shape, BF),
            shape((2, 2, line) + u_raw.shape[2:], BF),
            shape(g_merge.shape, BF),
            shape((3, 2, line, piece, width), BF),
            shape((8, d), F32),
        ),
        in_specs=[VMEM_SPEC] * 9 + [ANY_SPEC] * len(loads),
        out_specs=(ANY_SPEC,) * 5 + (VMEM_SPEC,) * 2,
        scratch_shapes=[vm(x.shape, x.dtype) for x in loads]
        + [dma((len(loads),))]
        + [vm((2, n, 128), BF)] * 3
        + [vm((8, n), F32), vm((n, 128), F32), vm((3, n, width), BF)]
        + [vm((pairs, 2, 2, line, 3, piece // 2, 128), BF)]
        + scatter
        + scatter[1:]
        + [sems(size)] * 2
        + total_scratch(line, u_raw.shape[2:])[1:] + total_scratch(line, u_raw.shape[2:])
        + total_scratch(line, (deep, d))
        + [vm((pairs, 2, line, 3, piece // 2, 128), BF)] * 2
        + [dma((pairs, 2, 2, line)), dma((5 + 2 * pairs, 2, line + 1))]
        + [vm((size, 8, d), F32), dma((2, size)), vm((count, 8, d), F32), dma((2, count)), dma((CHUNKS,))]
        + [vm((size, 8, d // 4), F32), dma((2, size)), vm((count, 8, d // 4), F32), dma((2, count))]
        + [vm((2, 2, line) + p_down1.shape, BF), vm((2, 2, line) + u_raw.shape[2:], BF)]
        + [vm(g_merge.shape, BF), dma((3,)), dma((CHUNKS,))],
        compiler_params=pltpu.CompilerParams(
            collective_id=3, has_side_effects=True, vmem_limit_bytes=64 << 20
        ),
        name="late",
    )(gain, db, p_down0, p_down1, u_held, u_raw, g_merge, small_in, bias_in, *loads)


def widen_kernel(down, up, merge, triple, small, out, tok, o_down, o_up, o_merge, o_triple, o_out, o_tok, *o_small):
    for src, dst in ((down, o_down), (up, o_up), (merge, o_merge), (triple, o_triple)):
        dst[...] = src[...].astype(F32)
    o_out[...] = out[...]
    o_tok[...] = tok[...]

    @pl.when(pl.program_id(0) == 0)
    def _():
        for i, dst in enumerate(o_small[:7]):
            dst[...] = small[i:i + 1, :dst.shape[1]]
        width = o_small[7].shape[1]
        for c in range(3):
            o_small[7][c:c + 1, :] = small[7:8, c * width:(c + 1) * width]


def widen(down, up, merge, triple, small, out, tok):
    steps = 2
    d, units, width = small.shape[1], up.shape[1], triple.shape[2]

    def spec(x):
        axis = x.ndim - 2
        block = x.shape[:axis] + (x.shape[axis] // steps, x.shape[-1])
        return pl.BlockSpec(block, lambda i: (0,) * axis + (i, 0))

    def whole(shape):
        return pl.BlockSpec(shape, lambda i: (0, 0))

    arrays = (down, up, merge, triple)
    lines = [(1, d)] * 6 + [(1, units), (3, width)]
    outs = [(x.shape, F32, spec(x)) for x in arrays] + [(x.shape, x.dtype, spec(x)) for x in (out, tok)]
    outs += [(x, F32, whole(x)) for x in lines]
    return pl.pallas_call(
        widen_kernel,
        grid=(steps,),
        out_shape=tuple(jax.ShapeDtypeStruct(x, t) for x, t, _ in outs),
        in_specs=[spec(x) for x in arrays] + [whole(small.shape), spec(out), spec(tok)],
        out_specs=tuple(x for _, _, x in outs),
        compiler_params=pltpu.CompilerParams(vmem_limit_bytes=60 << 20),
        name="widen",
    )(down, up, merge, triple, small, out, tok)


def on_device(
    tokens,
    first_gain,
    first_shift,
    triple_weight,
    triple_bias,
    merge_weight,
    merge_bias,
    second_gain,
    second_shift,
    up_weight,
    up_bias,
    down_weight,
    down_bias,
    lengths,
    cotangent,
):
    size = lax.axis_size("tensor")
    count = lax.axis_size("dp")
    row_count, d = tokens.shape
    rows = row_count // CHUNKS
    width = triple_weight.shape[2]
    units = up_weight.shape[1]
    n = row_count * size
    fused = (
        count == 8 and units % 512 == 0 and width % 256 == 0 and 3 * width <= d and units <= d
    )
    count = count if fused else 0
    line = lambda v: v.reshape(1, -1)
    w = jnp.transpose(triple_weight, (1, 0, 2))
    full, mixed, attended, log_total, gatt, gres, resid, pout, g_merge, small_b, bias_b, *rest = core(
        size, count, lengths, line(first_gain), line(first_shift), triple_bias, line(merge_bias),
        line(second_gain), line(second_shift), line(up_bias), w, tokens, cotangent, merge_weight,
        up_weight, down_weight,
    )
    gatt = gatt.reshape(n, width)
    if fused:
        output, gtok, down, up, merge, triple, small = late(
            size, count, line(first_gain), line(down_bias), *rest, g_merge, small_b, bias_b,
            mixed, attended, gatt, log_total, full, w, tokens, gres, resid, pout,
        )
        down, up, merge, triple, output, gtok, *small, up_b, triple_b = widen(
            down.reshape(units, d), up.reshape(d, units), merge.reshape(width, d),
            triple.reshape(3, d, width), small, output, gtok,
        )
        triple = jnp.transpose(triple, (1, 0, 2))
        small = [x.reshape(d) for x in small]
        up_b = up_b.reshape(units)
    else:
        branch = lax.psum_scatter(pout.reshape(n, d), "tensor", scatter_dimension=0, tiled=True)
        g_up, g_down = rest
        blocks = lambda x: x.reshape(size, CHUNKS, rows, x.shape[-1])
        dq, dk, dv = attend_bwd(mixed, attended, log_total, gatt)
        gtok, g_triple, small_c, bias_c = tail(
            size, blocks(dq), blocks(dk), blocks(dv), full, w, tokens, gres, line(first_gain)
        )
        merge, up, down, triple = lax.psum((g_merge, g_up, g_down, g_triple), "dp")
        triple_b, up_b = lax.psum((bias_c[0], bias_b[0]), "dp")
        small = lax.psum(small_b + small_c, ("dp", "tensor"))
        triple = jnp.transpose(triple, (1, 0, 2)).astype(F32)
        triple_b = triple_b.reshape(3, width)
        merge, up, down = merge.astype(F32), up.astype(F32), down.astype(F32)
        output = (resid + branch.astype(F32) + down_bias).astype(BF)
    return (
        output,
        gtok,
        small[0],
        small[1],
        triple,
        triple_b,
        merge,
        small[2],
        small[3],
        small[4],
        up,
        up_b,
        down,
        small[5],
    )


def solution(mesh):
    in_specs = (
        P(("dp", "tensor"), None),
        P(),
        P(),
        P(None, None, "tensor"),
        P(None, "tensor"),
        P("tensor", None),
        P(),
        P(),
        P(),
        P(None, "tensor"),
        P("tensor"),
        P("tensor", None),
        P(),
        P("dp"),
        P(("dp", "tensor"), None),
    )
    out_specs = (
        P(("dp", "tensor"), None),
        P(("dp", "tensor"), None),
        P(),
        P(),
        P(None, None, "tensor"),
        P(None, "tensor"),
        P("tensor", None),
        P(),
        P(),
        P(),
        P(None, "tensor"),
        P("tensor"),
        P("tensor", None),
        P(),
    )
    return jax.shard_map(
        on_device, mesh=mesh, in_specs=in_specs, out_specs=out_specs, check_vma=False
    )
```

```python
import functools

import jax
import jax.numpy as jnp
from jax import lax
from jax.experimental import pallas as pl
from jax.experimental.pallas import tpu as pltpu
from jax.sharding import PartitionSpec as P

EPS = 1e-05
HD = 64
LOG2E = 1.4426950408889634
SC = HD ** (-0.5) * LOG2E
BIG = 1e30
NT = (((1,), (1,)), ((), ()))
TN = (((0,), (0,)), ((), ()))
NN = (((1,), (0,)), ((), ()))


def mm(a, b, dims):
    return lax.dot_general(a, b, dims, preferred_element_type=jnp.float32)


def sgn_of(s):
    return jnp.minimum(jnp.maximum(s * BIG, -1.0), 1.0)


def bwd_kernel(bq, bk, q_ref, k_ref, v_ref, do_ref, o_ref, lse_ref, dq_ref, dk_ref, dv_ref,
               qm, km, dom, dsc, dq_acc):
    n = q_ref.shape[0]
    lane = lax.broadcasted_iota(jnp.int32, (1, 128), 1)
    hm = [lane < HD, lane >= HD]
    for h in range(2):
        for r in range(0, n, 512):
            sl = pl.ds(r, 512)
            z = jnp.zeros((512, 128), jnp.bfloat16)
            qm[h, sl, :] = jnp.where(hm[h], q_ref[sl, :], z)
            km[h, sl, :] = jnp.where(hm[h], k_ref[sl, :], z)
            d = jnp.where(hm[h], do_ref[sl, :], z)
            dom[h, sl, :] = d
            prod = d.astype(jnp.float32) * o_ref[sl, :].astype(jnp.float32)
            dd = jnp.broadcast_to(jnp.sum(prod, axis=1, keepdims=True), (512, 128))
            dsc[h:h + 1, sl] = jnp.transpose(dd)[0:1, :]
    dq_acc[...] = jnp.zeros_like(dq_acc)
    row = lax.broadcasted_iota(jnp.int32, (bk, bq), 0)
    col = lax.broadcasted_iota(jnp.int32, (bk, bq), 1)

    def tile(j, i, dk, dv, diag):
        k0 = pl.multiple_of(j * bk, bk)
        q0 = pl.multiple_of(i * bq, bq)
        ks, qs = pl.ds(k0, bk), pl.ds(q0, bq)
        kb, vb = k_ref[ks, :], v_ref[ks, :]
        dq = None
        for h in range(2):
            qh = qm[h, qs, :]
            doh = dom[h, qs, :]
            s = mm(kb, qh, NT)
            dp = mm(vb, doh, NT)
            p = jnp.exp2(jnp.abs(s) * SC - lse_ref[0, h:h + 1, qs])
            if diag:
                p = jnp.where((row + k0) <= (col + q0), p, 0.0)
            sg = sgn_of(s)
            w = sg * p
            ds = (w * (sg * dp - dsc[h:h + 1, qs])).astype(jnp.bfloat16)
            dv = dv + mm(w.astype(jnp.bfloat16), doh, NN)
            dk = dk + mm(ds, qh, NN)
            t = mm(ds, km[h, ks, :], TN)
            dq = t if dq is None else dq + t
        dq_acc[qs, :] += dq
        return dk, dv

    r = bk // bq
    def kvblock(j, _):
        z = jnp.zeros((bk, 128), jnp.float32)
        dk, dv = z, z
        for a in range(r):
            dk, dv = tile(j, j * r + a, dk, dv, True)
        dk, dv = lax.fori_loop((j + 1) * r, n // bq, lambda i, c: tile(j, i, c[0], c[1], False), (dk, dv))
        ks = pl.ds(pl.multiple_of(j * bk, bk), bk)
        dk_ref[ks, :] = (dk * HD ** (-0.5)).astype(jnp.bfloat16)
        dv_ref[ks, :] = dv.astype(jnp.bfloat16)
        return 0

    lax.fori_loop(0, n // bk, kvblock, 0)
    dq_ref[...] = (dq_acc[...] * HD ** (-0.5)).astype(jnp.bfloat16)


def attend_bwd(mixed, attended, lse, grad, bq=512, bk=512):
    n = mixed.shape[0]
    width = mixed.shape[1] // 3
    pairs = width // 128
    spec = lambda off: pl.BlockSpec((n, 128), lambda p, off=off: (0, off + p))
    o = jax.ShapeDtypeStruct((n, width), jnp.bfloat16)
    return pl.pallas_call(
        functools.partial(bwd_kernel, bq, bk),
        grid=(pairs,),
        out_shape=(o, o, o),
        in_specs=[spec(0), spec(pairs), spec(2 * pairs), spec(0), spec(0), pl.BlockSpec((1, 8, n), lambda p: (p, 0, 0))],
        out_specs=(spec(0),) * 3,
        scratch_shapes=[pltpu.VMEM((2, n, 128), jnp.bfloat16)] * 3 + [pltpu.VMEM((8, n), jnp.float32), pltpu.VMEM((n, 128), jnp.float32)],
        compiler_params=pltpu.CompilerParams(vmem_limit_bytes=48 << 20),
        cost_estimate=pl.CostEstimate(flops=10 * n * n * width, bytes_accessed=16 * n * width, transcendentals=n * n * width // 128),
        name="attend_bwd",
    )(mixed, mixed, mixed, grad, attended, lse)


BF = jnp.bfloat16
F32 = jnp.float32
CHUNKS = 4
VMEM_SPEC = pl.BlockSpec(memory_space=pltpu.VMEM)
SMEM_SPEC = pl.BlockSpec(memory_space=pltpu.SMEM)


def remote(src, dst, send_sem, recv_sem, axis, index):
    return pltpu.make_async_remote_copy(
        src_ref=src,
        dst_ref=dst,
        send_sem=send_sem,
        recv_sem=recv_sem,
        device_id={axis: index},
        device_id_type=pl.DeviceIdType.MESH,
    )


class Group:
    def __init__(self, size):
        self.size = size
        self.chips = size // 2
        self.me = lax.axis_index("tensor")
        self.chip = self.me // 2
        self.core = self.me % 2
        self.sibling = self.chip * 2 + 1 - self.core

    def same(self, off):
        return (self.chip + off) % self.chips * 2 + self.core

    def other(self, off):
        return (self.chip + off) % self.chips * 2 + 1 - self.core

    def greet(self, barrier):
        peers = [self.sibling] + [self.same(off) for off in range(1, self.chips)]
        for peer in peers:
            pl.semaphore_signal(
                barrier, inc=1, device_id={"tensor": peer}, device_id_type=pl.DeviceIdType.MESH
            )
        return len(peers)


def loop(count, body):
    def step(k, carry):
        body(k)
        return carry

    lax.fori_loop(0, count, step, 0)


def loop_range(low, high, body):
    def step(k, carry):
        body(k)
        return carry

    lax.fori_loop(low, high, step, 0)


class Gather:
    def __init__(self, group, buf, sem):
        self.g, self.buf, self.sem = group, buf, sem

    def own(self, off, k):
        g, sem = self.g, self.sem
        here = self.buf.at[g.me, k]
        if off == 0:
            return remote(here, here, sem.at[0, 0, k], sem.at[3, 0, k], "tensor", g.sibling)
        return remote(
            here, here, sem.at[0, off, k], sem.at[2, g.chips - off, k], "tensor", g.same(off)
        )

    def passed(self, off, k):
        here = self.buf.at[self.g.same(off), k]
        sem = self.sem
        return remote(here, here, sem.at[1, off, k], sem.at[3, off, k], "tensor", self.g.sibling)

    def send(self, k):
        for off in list(range(1, self.g.chips)) + [0]:
            self.own(off, k).start()

    def forward(self, k):
        g, sem = self.g, self.sem
        for off in range(1, g.chips):
            here = self.buf.at[g.same(off), k]
            remote(
                here, here, sem.at[0, off, k], sem.at[2, off, k], "tensor", g.same(off)
            ).wait_recv()
            self.passed(off, k).start()

    def wait(self, k):
        g, sem = self.g, self.sem
        for off in range(g.chips):
            here = self.buf.at[g.other(off), k]
            remote(
                here, here, sem.at[0, 0, k], sem.at[3, off, k], "tensor", g.sibling
            ).wait_recv()

    def drain(self, k):
        for off in range(self.g.chips):
            self.own(off, k).wait_send()
            if off:
                self.passed(off, k).wait_send()


class Scatter:
    def __init__(self, group, part, in_near, out_far, in_far, sem):
        self.g, self.part, self.sem = group, part, sem
        self.in_near, self.out_far, self.in_far = in_near, out_far, in_far

    def near(self, off, k):
        sem = self.sem
        return remote(
            self.part.at[self.g.other(off), k], self.in_near.at[off, k], sem.at[0, off, k],
            sem.at[1, off, k], "tensor", self.g.sibling,
        )

    def far(self, off, k):
        g, sem = self.g, self.sem
        back = g.chips - off
        return remote(
            self.out_far.at[off - 1, k], self.in_far.at[back - 1, k], sem.at[2, off, k],
            sem.at[3, back, k], "tensor", g.same(off),
        )

    def send(self, k):
        for off in list(range(1, self.g.chips)) + [0]:
            self.near(off, k).start()

    def combine(self, k):
        g = self.g
        for off in range(1, g.chips):
            self.near(off, k).wait_recv()
            total = self.part[g.same(off), k].astype(F32) + self.in_near[off, k].astype(F32)
            self.out_far[off - 1, k] = total.astype(BF)
            self.far(off, k).start()

    def final(self, k):
        g, sem = self.g, self.sem
        self.near(0, k).wait_recv()
        total = self.part[g.me, k].astype(F32) + self.in_near[0, k].astype(F32)
        for off in range(1, g.chips):
            remote(
                self.out_far.at[off - 1, k], self.in_far.at[off - 1, k], sem.at[2, off, k],
                sem.at[3, off, k], "tensor", g.same(off),
            ).wait_recv()
            total = total + self.in_far[off - 1, k].astype(F32)
        return total

    def drain(self, k):
        for off in range(self.g.chips):
            self.near(off, k).wait_send()
            if off:
                self.far(off, k).wait_send()


def scatter_scratch(size, rows, d):
    chips = size // 2
    block = lambda c: pltpu.VMEM((c, CHUNKS, rows, d), BF)
    return [pltpu.VMEM((size, CHUNKS, rows, d), BF), block(chips), block(chips - 1), block(chips - 1)]


def sems(group):
    return pltpu.SemaphoreType.DMA((4, group // 2, CHUNKS))


class Place:
    def __init__(self, count):
        self.count = count
        self.line = count // 2
        self.me = lax.axis_index("dp")
        self.row = self.me // 2
        self.side = self.me % 2
        self.partner = self.row * 2 + 1 - self.side
        self.next = self.row + 1 - self.row % 2 * 2
        self.inner = self.next % 3 == 0

    def at(self, row):
        return row * 2 + self.side

    def peer(self, off):
        return self.at((self.row + off) % self.line)

    def greet(self, barrier):
        peers = [self.partner] + [self.peer(off) for off in range(1, self.line)]
        for peer in peers:
            pl.semaphore_signal(
                barrier, inc=1, device_id={"dp": peer}, device_id_type=pl.DeviceIdType.MESH
            )
        return len(peers)


class Total:
    def __init__(self, place, src, near, far, sem):
        self.p, self.src, self.near, self.far, self.sem = place, src, near, far, sem

    def pair(self):
        p, sem = self.p, self.sem
        return remote(
            self.src.at[1 - p.side], self.near, sem.at[0, 0], sem.at[1, 0], "dp", p.partner
        )

    def outward(self):
        p, sem = self.p, self.sem
        return remote(
            self.near.at[pl.ds(1 - p.row // 3, 3)], self.far.at[pl.ds(0, 3)], sem.at[0, 1],
            sem.at[1, 1], "dp", p.at(p.next),
        )

    def inward(self):
        p, sem = self.p, self.sem
        return remote(
            self.near.at[p.next], self.far.at[0], sem.at[0, 1], sem.at[1, 1], "dp", p.at(p.next)
        )

    def summed(self, i):
        p, sem = self.p, self.sem
        target = (3 - p.row, 3 - p.next)[i]
        return remote(
            self.near.at[target], self.far.at[3], sem.at[0, 2 + i], sem.at[1, 2], "dp", p.at(target)
        )

    def start(self):
        self.pair().start()

    def add(self):
        self.pair().wait_recv()
        for j in range(self.p.line):
            total = self.src[self.p.side, j].astype(F32) + self.near[j].astype(F32)
            self.near[j] = total.astype(BF)

    def scatter(self):
        @pl.when(self.p.inner)
        def _():
            self.inward().start()

        @pl.when(jnp.logical_not(self.p.inner))
        def _():
            self.outward().start()

    def halve(self):
        self.add()
        self.scatter()

    def relay(self):
        p = self.p

        @pl.when(p.inner)
        def _():
            self.outward().wait_recv()
            skip = 2 - p.row
            for i, target in enumerate((3 - p.row, 3 - p.next)):
                total = self.near[target].astype(F32) + self.far[target - skip].astype(F32)
                self.near[target] = total.astype(BF)
                self.summed(i).start()
            total = self.near[p.row].astype(F32) + self.far[p.row - skip].astype(F32)
            self.near[p.row] = total.astype(BF)

        @pl.when(jnp.logical_not(p.inner))
        def _():
            self.inward().wait_recv()
            total = self.near[p.row].astype(F32) + self.far[0].astype(F32)
            self.near[p.row] = total.astype(BF)

    def settle(self):
        self.summed(0).wait_recv()
        return (self.near[self.p.row].astype(F32) + self.far[3].astype(F32)).astype(BF)

    def drain(self, pair=True, pieces=True):
        if pair:
            self.pair().wait_send()
        if not pieces:
            return

        @pl.when(self.p.inner)
        def _():
            self.inward().wait_send()
            self.summed(0).wait_send()
            self.summed(1).wait_send()

        @pl.when(jnp.logical_not(self.p.inner))
        def _():
            self.outward().wait_send()


class Share:
    def __init__(self, place, piece, half, sem):
        self.p, self.piece_at, self.half_at, self.sem = place, piece, half, sem

    def piece(self, i, owner, target):
        p, sem = self.p, self.sem
        here = self.piece_at(p.side, owner)
        return remote(here, here, sem.at[0, i], sem.at[1, owner], "dp", p.at(target))

    def first(self):
        p = self.p
        second = jnp.where(p.inner, 3 - p.row, 3 - p.next)
        return self.piece(0, p.row, p.next), self.piece(1, p.row, second)

    def passed(self):
        p = self.p
        return self.piece(2, 3 - p.row, p.next), self.piece(3, 3 - p.next, p.next)

    def half(self):
        p, sem = self.p, self.sem
        here = self.half_at(p.side)
        return remote(here, here, sem.at[0, 4], sem.at[1, 4], "dp", p.partner)

    def start(self, piece):
        self.piece_at(self.p.side, self.p.row)[...] = piece
        for one in self.first():
            one.start()

    def relay(self):
        p = self.p

        @pl.when(p.inner)
        def _():
            for i, owner in ((2, 3 - p.row), (3, 3 - p.next)):
                self.piece(i, owner, p.next).wait_recv()
                self.piece(i, owner, p.next).start()

    def gathered(self):
        p = self.p
        self.piece(0, p.next, p.next).wait_recv()

        @pl.when(jnp.logical_not(p.inner))
        def _():
            self.piece(0, 3 - p.row, p.next).wait_recv()
            self.piece(0, 3 - p.next, p.next).wait_recv()

    def spread(self):
        self.gathered()
        self.half().start()

    def sent(self):
        p = self.p
        for one in self.first():
            one.wait_send()

        @pl.when(p.inner)
        def _():
            for one in self.passed():
                one.wait_send()

    def finish(self, pieces=True):
        p, sem = self.p, self.sem
        there = self.half_at(1 - p.side)
        remote(there, there, sem.at[0, 4], sem.at[1, 4], "dp", p.partner).wait_recv()
        if pieces:
            self.sent()
        self.half().wait_send()


def total_scratch(line, block):
    return [pltpu.VMEM((line,) + block, BF)] * 2 + [pltpu.SemaphoreType.DMA((2, line))]


ANY_SPEC = pl.BlockSpec(memory_space=pl.ANY)


class Move:
    def __init__(self, src, dst, sem):
        self.copy = pltpu.make_async_copy(src, dst, sem)

    def start(self):
        self.copy.start()
        return self

    def wait(self):
        self.copy.wait()


def norm_stats(x):
    centred = x - jnp.mean(x, axis=-1, keepdims=True)
    inverse = lax.rsqrt(jnp.mean(centred * centred, axis=-1, keepdims=True) + EPS)
    return centred * inverse, inverse


def norm_pull(grad, unit, inverse, gain):
    g = grad * gain
    g = g - jnp.mean(g, axis=-1, keepdims=True) - unit * jnp.mean(g * unit, axis=-1, keepdims=True)
    return g * inverse


def rows_of(ref, k, cols=slice(None)):
    x = ref[:, k, :, cols]
    return x.reshape(x.shape[0] * x.shape[1], x.shape[2])


def col_sum(x):
    return jnp.sum(x, axis=0, keepdims=True)


def enter_kernel(group):
    barrier = pltpu.get_barrier_semaphore()
    pl.semaphore_wait(barrier, group.greet(barrier))


def fold(x, op):
    r = x[:, :128]
    for c in range(1, x.shape[1] // 128):
        r = op(r, x[:, c * 128:(c + 1) * 128])
    return r


class Attend:
    def __init__(self, size, units, length, mixed, out, lse, scores, values):
        self.size, self.units, self.length = size, units, length
        self.mixed, self.out, self.lse, self.scores, self.values = mixed, out, lse, scores, values
        self.width = out.shape[-1]
        self.pairs = self.width // 128
        self.block = mixed.shape[0] // size
        self.rows = self.block // units
        lane = lax.broadcasted_iota(jnp.int32, (1, 128), 1)
        self.heads = [lane < HD, lane >= HD]

    def prepare(self):
        for x in range(self.pairs):
            for h in range(2):
                v = self.mixed[:, 2 * self.width + x * 128:2 * self.width + (x + 1) * 128]
                self.values[2 * x + h] = jnp.where(self.heads[h], v, jnp.zeros_like(v))

    def run(self, u, event=None):
        def body(i):
            self.unit(u, i // self.pairs, i % self.pairs)
            if event is not None:
                pl.when(i == (self.size - 1) * self.pairs - 1)(event)

        loop(self.size * self.pairs, body)

    def unit(self, u, s, x):
        bq, bk = self.rows, self.block
        lanes = pl.ds(pl.multiple_of(x * 128, 128), 128)
        k_lanes = pl.ds(pl.multiple_of(self.width + x * 128, 128), 128)
        k0 = pl.multiple_of(s * bk, bk)
        q0 = pl.multiple_of(s * bk + u * bq, bq)
        qb = self.mixed[pl.ds(q0, bq), lanes]
        qh = [jnp.where(self.heads[h], qb, jnp.zeros_like(qb)) for h in range(2)]
        edge = (u + 1) * bq
        row = lax.broadcasted_iota(jnp.int32, (bq, edge), 0) + u * bq
        mask = lax.broadcasted_iota(jnp.int32, (bq, edge), 1) <= row
        zero = jnp.zeros((bq, 128), F32)

        def first(j, most):
            kb = self.mixed[pl.ds(pl.multiple_of(j * bk, bk), bk), k_lanes]
            new = []
            for h in range(2):
                sc = mm(qh[h], kb, NT)
                self.scores[h, j] = sc
                new.append(jnp.maximum(most[h], fold(jnp.abs(sc), jnp.maximum)))
            return tuple(new)

        most = lax.fori_loop(0, s, first, (zero, zero))
        kb = self.mixed[pl.ds(k0, edge), k_lanes]
        top, state = [], []
        for h in range(2):
            sc = jnp.where(mask, mm(qh[h], kb, NT), 0.0)
            m = jnp.maximum(most[h], fold(jnp.abs(sc), jnp.maximum))
            top.append(jnp.max(m, axis=1, keepdims=True) * SC)
            e = jnp.where(mask, jnp.exp2(jnp.abs(sc) * SC - top[h]), 0.0)
            w = (sgn_of(sc) * e).astype(BF)
            state.append((mm(w, self.values[2 * x + h, pl.ds(k0, edge), :], NN), fold(e, jnp.add)))

        def second(j, carry):
            new = []
            for h in range(2):
                acc, total = carry[h]
                sc = self.scores[h, j]
                e = jnp.exp2(jnp.abs(sc) * SC - top[h])
                w = (sgn_of(sc) * e).astype(BF)
                rows = pl.ds(pl.multiple_of(j * bk, bk), bk)
                acc = acc + mm(w, self.values[2 * x + h, rows, :], NN)
                new.append((acc, total + fold(e, jnp.add)))
            return tuple(new)

        state = lax.fori_loop(0, s, second, tuple(state))
        result = 0.0
        for h in range(2):
            total = jnp.sum(state[h][1], axis=1, keepdims=True)
            result = result + state[h][0] / total
            log_total = jnp.broadcast_to(top[h] + jnp.log(total) * LOG2E, (bq, 128))
            self.lse[x, h:h + 1, pl.ds(q0, bq)] = jnp.transpose(log_total)[0:1, :]
        live = (lax.broadcasted_iota(jnp.int32, (bq, 1), 0) + q0) < self.length[0]
        self.out[pl.ds(q0, bq), lanes] = jnp.where(live, result, 0.0).astype(BF)


def core_kernel(
    size, count, length, gain1, shift1, tb, mb, gain, shift, ub,
    w_hbm, tok_hbm, cot_hbm, mw_hbm, up_hbm, down_hbm,
    full_hbm, mixed_hbm, att, lse, gatt, gres_hbm, resid_hbm, pout_hbm, g_merge, small, bias, *rest,
):
    if count:
        (pieces, held, raw, rest) = (rest[:2], rest[2], rest[3], rest[4:])
    else:
        (g_up, g_down, rest) = (rest[0], rest[1], rest[2:])
    (
        w, mixed, tok, cot, mw, up, down, scores, values, resid, gres, pout, part, in_near, out_far, in_far,
        full, hid, gb, sem0, sem1, sem2, sem3, sem4, sem5, load_sem, cot_sem, out_sem, free,
    ) = rest[:29]
    rest = rest[29:]
    g = Group(size)
    rows, d = tok.shape[0] // CHUNKS, tok.shape[1]
    width, units = mw.shape[0], up.shape[1]
    step = min(512, units)
    p = Place(count) if count else None
    span = lambda k: pl.ds(pl.multiple_of(k * rows, rows), rows)
    loads = [
        Move(src, dst, load_sem.at[i]).start()
        for i, (src, dst) in enumerate(
            ((tok_hbm, tok), (w_hbm, w), (mw_hbm, mw), (up_hbm, up), (down_hbm, down))
        )
    ]
    own = lambda k: Move(cot_hbm.at[k], cot.at[g.me, k], cot_sem.at[k])
    loop(CHUNKS, lambda k: own(k).start())
    begin = Gather(g, full, sem0)
    barrier = pltpu.get_barrier_semaphore()
    pl.semaphore_wait(barrier, g.greet(barrier) + (p.greet(barrier) if count else 0))
    tops = Gather(g, cot, sem5)
    first = Scatter(g, part, in_near, out_far, in_far, sem1)
    spread = Gather(g, full, sem2)
    second = Scatter(g, part, in_near, out_far, in_far, sem3)
    if units == d:
        gfull = hid
    else:
        gfull, rest = rest[0], rest[1:]
    back = Gather(g, gfull, sem4)
    sums = []
    if count:
        g_up, g_down, rest = rest[0], rest[1], rest[2:]
        for ref in (g_down.at[0], g_down.at[1], g_up.at[0]):
            near, far, sem = rest[:3]
            rest = rest[3:]
            sums.append(Total(p, ref, near, far, sem))

    def at(s, k):
        return pl.ds(pl.multiple_of((s * CHUNKS + k) * rows, rows), rows)

    def enter(k):
        unit, _ = norm_stats(tok[span(k), :].astype(F32))
        full[g.me, k] = (unit * gain1[...] + shift1[...]).astype(BF)
        begin.send(k)

    loads[0].wait()
    loop(CHUNKS, enter)

    def mask(k):
        own(k).wait()
        row = lax.broadcasted_iota(jnp.int32, (rows, 1), 0) + (g.me * CHUNKS + k) * rows
        cot[g.me, k] = jnp.where(row < length[0], cot[g.me, k].astype(F32), 0.0).astype(BF)
        tops.send(k)

    loop(CHUNKS, mask)
    loads[1].wait()

    def full_store(k):
        return Move(full.at[:, k], full_hbm.at[:, k], out_sem.at[3, k])

    def project(k):
        begin.wait(k)
        full_store(k).start()
        x = rows_of(full, k)
        for j in range(3):
            cols = slice(j * width, (j + 1) * width)
            y = (mm(x, w[j], NN) + tb[j:j + 1, :]).astype(BF)
            for s in range(size):
                mixed[at(s, k), cols] = y[s * rows:(s + 1) * rows]

    def begin_step(k):
        begin.forward(k)

        @pl.when(k > 0)
        def _():
            project(k - 1)

    loop(CHUNKS, begin_step)
    project(CHUNKS - 1)
    mixed_store = Move(mixed, mixed_hbm, load_sem.at[5]).start()
    attend = Attend(size, 2, length, mixed, att, lse, scores, values)
    attend.prepare()

    def merge(k):
        x = jnp.concatenate([att[at(s, k), :] for s in range(size)], axis=0)
        y = mm(x, mw[...], NN).astype(BF)
        for s in range(size):
            part[s, k] = y[s * rows:(s + 1) * rows]
        first.send(k)

    def resid_store(k):
        return Move(resid.at[span(k)], resid_hbm.at[span(k)], out_sem.at[0, k])

    def norm(k):
        x = tok[span(k), :].astype(F32) + first.final(k) + mb[...]
        resid[span(k), :] = x
        resid_store(k).start()
        unit, _ = norm_stats(x)
        full[g.me, k] = (unit * gain[...] + shift[...]).astype(BF)
        spread.send(k)

    def inner(k):
        spread.forward(k)
        spread.wait(k)
        x = rows_of(full, k)
        top = rows_of(cot, k)

        def tile(j):
            cols = pl.ds(pl.multiple_of(j * step, step), step)
            v = mm(x, up[:, cols], NN) + ub[:, cols]
            gh = mm(top, down[cols, :], NT)
            c0, c1 = 0.7978845608, 0.044715
            v2 = v * v
            th = jnp.tanh(c0 * (v + c1 * v2 * v))
            half = 0.5 * (1.0 + th)
            h = (v * half).astype(BF)
            slope = half + 0.5 * v * (1.0 - th * th) * (c0 * (1.0 + 3.0 * c1 * v2))
            gv = (gh * slope).astype(BF)
            bias[0:1, cols] += col_sum(gv.astype(F32))
            for s in range(size):
                hid[s, k, :, cols] = h[s * rows:(s + 1) * rows]
                gb[s, k, :, cols] = gv[s * rows:(s + 1) * rows]

        loop(units // step, tile)

    def pout_store(k):
        return Move(pout.at[k % 2], pout_hbm.at[:, k], out_sem.at[1, k])

    def leave(k):
        h, gv = rows_of(hid, k), rows_of(gb, k)

        @pl.when(k >= 2)
        def _():
            pout_store(k - 2).wait()

        def tile(j):
            cols = pl.ds(pl.multiple_of(j * 512, 512), 512)
            y = mm(h, down[:, cols], NN).astype(BF)
            z = mm(gv, up[cols, :], NT).astype(BF)
            for s in range(size):
                pout[k % 2, s, :, cols] = y[s * rows:(s + 1) * rows]
                part[s, k, :, cols] = z[s * rows:(s + 1) * rows]

        loop(d // 512, tile)
        pout_store(k).start()
        second.send(k)

    def flat(ref, cols):
        x = ref[:, :, :, cols]
        return x.reshape(size * CHUNKS * rows, x.shape[3])

    def products(ref, left, right, extent):
        tall = min(256, extent)

        def block(i):
            cols = pl.ds(pl.multiple_of(i * tall, tall), tall)
            y = mm(flat(left, cols), flat(right, slice(None)), TN).astype(BF)
            if not count:
                ref[cols, :] = y
            else:
                deep = ref.shape[3]
                for e in range(tall // deep):
                    f = i * (tall // deep) + e
                    ref[f // (2 * p.line), f // p.line % 2, f % p.line] = y[e * deep:(e + 1) * deep]

        return block, extent // tall

    def weights(ref, left, right, extent, event=None):
        block, blocks = products(ref, left, right, extent)
        after(0, blocks, block, {blocks // 2 - 1: event})

    def after(low, high, body, events):
        def step(k):
            body(k)
            for at_k, event in events.items():
                if count and event is not None:
                    pl.when(k == at_k)(event)

        loop_range(low, high, step)

    def gres_store(k):
        return Move(gres.at[k % 2], gres_hbm.at[span(k)], out_sem.at[2, k])

    def pull(k):
        gs = second.final(k)
        unit, inverse = norm_stats(resid[span(k), :])
        top = cot[g.me, k].astype(F32)
        gr = top + norm_pull(gs, unit, inverse, gain[...])

        @pl.when(k >= 2)
        def _():
            gres_store(k - 2).wait()

        gres[k % 2] = gr
        gres_store(k).start()
        gfull[g.me, k] = gr.astype(BF)
        back.send(k)
        small[2:3, :] += col_sum(gr)
        small[3:4, :] += col_sum(gs * unit)
        small[4:5, :] += col_sum(gs)
        small[5:6, :] += col_sum(top)

    def last(k):
        back.forward(k)
        back.wait(k)
        y = mm(rows_of(gfull, k), mw[...], NT)
        for s in range(size):
            row = lax.broadcasted_iota(jnp.int32, (rows, 1), 0) + (s * CHUNKS + k) * rows
            gatt[s, k] = jnp.where(row < length[0], y[s * rows:(s + 1) * rows], 0.0).astype(BF)

    def later(*steps):
        if count:
            for one in steps:
                one()

    bias[...] = jnp.zeros_like(bias)
    small[...] = jnp.zeros_like(small)
    attend.run(0)
    for load in loads[2:]:
        load.wait()
    loop(CHUNKS, begin.drain)
    loop(CHUNKS, lambda k: full_store(k).wait())
    loop(2, merge)
    loop(2, first.combine)
    loop(2, tops.forward)

    def between():
        loop_range(2, CHUNKS, tops.forward)
        loop(2, norm)

    attend.run(1, between)
    loop_range(2, CHUNKS, merge)
    loop_range(2, CHUNKS, first.combine)
    loop(CHUNKS, tops.wait)
    loop(2, inner)
    loop(2, first.drain)
    loop(2, leave)
    loop_range(2, CHUNKS, norm)
    loop(2, second.combine)
    loop_range(2, CHUNKS, first.drain)
    loop_range(2, CHUNKS, inner)
    weights(g_down, hid, cot, units, sums[0].start if count else None)
    pl.semaphore_wait(free, g.greet(free))
    loop(2, pull)
    after(2, CHUNKS, leave, {2: sums[1].start if count else None})
    loop_range(2, CHUNKS, second.combine)
    later(lambda: sums[0].halve())
    weights(g_up, full, gb, d)
    later(lambda: sums[2].start())
    loop(CHUNKS, tops.drain)
    loop(CHUNKS, spread.drain)

    def turn():
        sums[0].relay()
        sums[1].halve()

    after(2, CHUNKS, pull, {2: turn})
    after(0, CHUNKS, last, {0: lambda: sums[1].relay()})
    y = mm(att[...], flat(gfull, slice(None)), TN).astype(BF)
    if count:
        deep = g_merge.shape[2]
        for f in range(2 * p.line):
            g_merge[f // p.line, f % p.line] = y[f * deep:(f + 1) * deep]
        raw[...] = g_up[1]
        sums[2].add()
        held[...] = sums[2].near[...]
        pieces[0][...] = sums[0].settle()
        pieces[1][...] = sums[1].settle()
        for h in range(3):
            sums[h].drain(True, h < 2)
    else:
        g_merge[...] = y
    loop(CHUNKS, second.drain)
    loop(CHUNKS, back.drain)
    loop(CHUNKS, lambda k: resid_store(k).wait())
    mixed_store.wait()
    loop_range(2, CHUNKS, lambda k: pout_store(k).wait())
    loop_range(2, CHUNKS, lambda k: gres_store(k).wait())


def core(size, count, lengths, gain1, shift1, tb, mb, gain, shift, ub, w, tokens, cotangent, mw,
         up, down):
    rows, d = tokens.shape
    r = rows // CHUNKS
    n = rows * size
    width, units = mw.shape[0], up.shape[1]
    pairs = width // 128
    shape = jax.ShapeDtypeStruct
    dma = pltpu.SemaphoreType.DMA
    vm = pltpu.VMEM
    wide = lambda c: vm((size, CHUNKS, r, c), BF)
    line = count // 2
    if count:
        blocks = ((2, 2, line, d // (4 * line), units), (2, 2, line, units // (4 * line), d))
        merge = shape((2, line, width // (2 * line), d), BF)
        piece = [shape(b[3:], BF) for b in blocks[::-1]]
        extra = (piece[0], piece[0], shape((line,) + blocks[0][3:], BF), shape(blocks[0][1:], BF))
        scratch = [vm(b, BF) for b in blocks]
        scratch += total_scratch(line, blocks[1][3:]) * 2 + total_scratch(line, blocks[0][3:])
    else:
        merge = shape((width, d), BF)
        extra = (shape((d, units), BF), shape((units, d), BF))
        scratch = []
    if units != d:
        scratch = [wide(d)] + scratch
    outs = (
        (shape((size, CHUNKS, r, d), BF), ANY_SPEC),
        (shape((n, 3 * width), BF), ANY_SPEC),
        (shape((n, width), BF), VMEM_SPEC),
        (shape((pairs, 8, n), F32), VMEM_SPEC),
        (shape((size, CHUNKS, r, width), BF), VMEM_SPEC),
        (shape((rows, d), F32), ANY_SPEC),
        (shape((rows, d), F32), ANY_SPEC),
        (shape((size, CHUNKS, r, d), BF), ANY_SPEC),
        (merge, VMEM_SPEC),
        (shape((8, d), F32), VMEM_SPEC),
        (shape((8, units), F32), VMEM_SPEC),
        *((x, VMEM_SPEC) for x in extra),
    )
    return pl.pallas_call(
        functools.partial(core_kernel, size, count),
        out_shape=tuple(x for x, _ in outs),
        in_specs=[SMEM_SPEC] + [VMEM_SPEC] * 7 + [ANY_SPEC] * 6,
        out_specs=tuple(x for _, x in outs),
        scratch_shapes=[
            vm(w.shape, BF), vm((n, 3 * width), BF), vm((rows, d), BF), wide(d), vm((width, d), BF), vm((d, units), BF), vm((units, d), BF),
            vm((2, size, rows // 2, rows), F32), vm((2 * pairs, n, 128), BF), vm((rows, d), F32),
            vm((2, r, d), F32), vm((2, size, r, d), BF),
        ]
        + scatter_scratch(size, r, d)
        + [wide(d), wide(units), wide(units)]
        + [sems(size)] * 6
        + [dma((6,)), dma((CHUNKS,)), dma((4, CHUNKS)), pltpu.SemaphoreType.REGULAR]
        + scratch,
        compiler_params=pltpu.CompilerParams(
            collective_id=1, has_side_effects=True, vmem_limit_bytes=64 << 20
        ),
        name="core",
    )(lengths, gain1, shift1, tb, mb, gain, shift, ub, w, tokens, cotangent.reshape(CHUNKS, r, d), mw,
      up, down)


def tail_kernel(
    size, dq, dk, dv, full, w, tok, gres, gain,
    gtok, g_triple, small, bias,
    part, in_near, out_far, in_far, sem,
):
    g = Group(size)
    rows, d = tok.shape[0] // CHUNKS, tok.shape[1]
    width = dq.shape[3]
    enter_kernel(g)
    scatter = Scatter(g, part, in_near, out_far, in_far, sem)
    span = lambda k: pl.ds(pl.multiple_of(k * rows, rows), rows)
    grads = (dq, dk, dv)

    def back(k):
        def tile(j):
            cols = pl.ds(pl.multiple_of(j * 256, 256), 256)
            z = sum(
                mm(rows_of(x, k), w[c, cols, :], NT)
                for c, x in enumerate(grads)
            )
            for s in range(size):
                part[s, k, :, cols] = z[s * rows:(s + 1) * rows].astype(BF)

        loop(d // 256, tile)
        scatter.send(k)

    loop(CHUNKS, back)
    loop(CHUNKS, scatter.combine)

    def flat(ref, cols):
        x = ref[:, :, :, cols]
        return x.reshape(size * CHUNKS * rows, x.shape[3])

    bias[...] = jnp.zeros_like(bias)
    for c, x in enumerate(grads):
        y = flat(x, slice(None))
        bias[0:1, c * width:(c + 1) * width] = col_sum(y.astype(F32))

        def tile(i):
            more = pl.ds(pl.multiple_of(i * 256, 256), 256)
            g_triple[c, more, :] = mm(flat(full, more), y, TN).astype(BF)

        loop(d // 256, tile)
    small[...] = jnp.zeros_like(small)

    def pull(k):
        gf = scatter.final(k)
        unit, inverse = norm_stats(tok[span(k), :].astype(F32))
        gtok[span(k), :] = gres[span(k), :] + norm_pull(gf, unit, inverse, gain[...])
        small[0:1, :] += col_sum(gf * unit)
        small[1:2, :] += col_sum(gf)

    loop(CHUNKS, pull)
    loop(CHUNKS, scatter.drain)


def tail(size, dq, dk, dv, full, w, tokens, gres, gain):
    rows, d = tokens.shape
    r = rows // CHUNKS
    width = dq.shape[-1]
    shape = jax.ShapeDtypeStruct
    return pl.pallas_call(
        functools.partial(tail_kernel, size),
        out_shape=(
            shape((rows, d), F32),
            shape((3, d, width), BF),
            shape((8, d), F32),
            shape((8, 3 * width), F32),
        ),
        in_specs=[VMEM_SPEC] * 8,
        out_specs=(VMEM_SPEC,) * 4,
        scratch_shapes=scatter_scratch(size, r, d) + [sems(size)],
        compiler_params=pltpu.CompilerParams(
            collective_id=2, has_side_effects=True, vmem_limit_bytes=56 << 20
        ),
        name="tail",
    )(dq, dk, dv, full, w, tokens, gres, gain)


class Everyone:
    def __init__(self, axis, count, buf, sem):
        self.axis, self.count, self.buf, self.sem = axis, count, buf, sem
        self.me = lax.axis_index(axis)

    def copy(self, owner, off, back):
        here = self.buf.at[owner]
        return remote(
            here, here, self.sem.at[0, off], self.sem.at[1, back], self.axis,
            (self.me + off) % self.count,
        )

    def start(self, value):
        self.buf[self.me] = value
        for off in range(1, self.count):
            self.copy(self.me, off, self.count - off).start()

    def finish(self):
        for off in range(1, self.count):
            self.copy((self.me + off) % self.count, off, off).wait_recv()
        total = self.buf[0]
        for j in range(1, self.count):
            total = total + self.buf[j]
        for off in range(1, self.count):
            self.copy(self.me, off, self.count - off).wait_send()
        return total


def late_kernel(
    size, count, bk, gain, db, p_down0, p_down1, u_held, u_raw, g_merge, small_in, bias_in,
    mixed_hbm, att_hbm, gatt_hbm, lse_hbm, full_hbm, w_hbm, tok_hbm, gres_hbm, resid_hbm, pout_hbm,
    out_hbm, gtok_hbm, down_hbm, up_hbm, merge_hbm, o_triple, small,
    mixed, att, gatt, lse, full, w, tok, gres, resid, pout, load_sem,
    qm, km, dom, dsc, dq_acc, gm, g_triple, part, in_near, out_far, in_far,
    in_near2, out_far2, in_far2, sem, sem2, u_far, u_sem, v_near, v_far, v_sem,
    m_near, m_far, m_sem, t_near, t_far, t_sem, s_sem, t_buf, t_sems, d_buf, d_sems, g_sem,
    t_buf2, t_sems2, d_buf2, d_sems2, o_down, o_up, o_merge, o_sem, out_sem,
):
    loads = [
        Move(src, dst, load_sem.at[i]).start()
        for i, (src, dst) in enumerate(
            (
                (mixed_hbm, mixed), (gatt_hbm, gatt), (att_hbm, att), (lse_hbm, lse),
                (pout_hbm, pout), (resid_hbm, resid), (full_hbm, full), (w_hbm, w),
                (tok_hbm, tok), (gres_hbm, gres),
            )
        )
    ]
    g, p = Group(size), Place(count)
    n = mixed.shape[0]
    rows, d = tok.shape[0] // CHUNKS, tok.shape[1]
    width = att.shape[1]
    pairs = width // 128
    barrier = pltpu.get_barrier_semaphore()
    for axis, extent in (("tensor", size), ("dp", count)):
        for off in range(1, extent):
            pl.semaphore_signal(
                barrier,
                inc=1,
                device_id={axis: (lax.axis_index(axis) + off) % extent},
                device_id_type=pl.DeviceIdType.MESH,
            )
    pl.semaphore_wait(barrier, size + count - 2)

    def share(ref, sem):
        return Share(p, lambda side, line: ref.at[side, line], lambda side: ref.at[side], sem)

    deep = g_triple.shape[5]

    def triple_share(x, h):
        lanes, part_rows = pl.ds(x * 128, 128), pl.ds(h * deep, deep)
        return Share(
            p,
            lambda side, line: o_triple.at[:, side, line, part_rows, lanes],
            lambda side: o_triple.at[:, side, :, part_rows, lanes],
            s_sem.at[5 + 2 * x + h],
        )

    def triple_total(x, h):
        return Total(p, g_triple.at[x, h], t_near.at[x, h], t_far.at[x, h], t_sem.at[x, h])

    shares = [
        share(ref.at[h], s_sem.at[2 * a + h])
        for a, ref in enumerate((o_down, o_up))
        for h in range(2)
    ]
    merge_total = Total(p, g_merge, m_near, m_far, m_sem)
    merge_share = share(o_merge, s_sem.at[4])
    totals = [triple_total(x, h) for x in range(pairs) for h in range(2)]
    triples = [triple_share(x, h) for x in range(pairs) for h in range(2)]
    branch = Scatter(g, pout, in_near2, out_far2, in_far2, sem2)
    up_total = Total(p, None, u_held, u_far, u_sem)
    raw_total = Total(p, u_raw, v_near, v_far, v_sem)
    raw_total.start()
    shares[0].start(p_down0[...])
    group_early = Everyone("tensor", size, t_buf, t_sems)
    all_early = Everyone("dp", count, d_buf, d_sems)
    group_early.start(small_in[...])

    def early():
        small[...] = group_early.finish()
    for load in loads[:4]:
        load.wait()

    lane = lax.broadcasted_iota(jnp.int32, (1, 128), 1)
    heads = [lane < HD, lane >= HD]
    row = lax.broadcasted_iota(jnp.int32, (bk, bk), 0)
    col = lax.broadcasted_iota(jnp.int32, (bk, bk), 1)

    def attention(x, events):
        def lanes(c):
            return pl.ds(pl.multiple_of(c * width + x * 128, 128), 128)

        def prepare(i):
            sl = pl.ds(pl.multiple_of(i * bk, bk), bk)
            z = jnp.zeros((bk, 128), BF)
            for h in range(2):
                qm[h, sl, :] = jnp.where(heads[h], mixed[sl, lanes(0)], z)
                km[h, sl, :] = jnp.where(heads[h], mixed[sl, lanes(1)], z)
                do = jnp.where(heads[h], gatt[sl, lanes(0)], z)
                dom[h, sl, :] = do
                prod = do.astype(F32) * att[sl, lanes(0)].astype(F32)
                dd = jnp.broadcast_to(jnp.sum(prod, axis=1, keepdims=True), (bk, 128))
                dsc[h:h + 1, sl] = jnp.transpose(dd)[0:1, :]
            dq_acc[sl, :] = jnp.zeros((bk, 128), F32)

        loop(n // bk, prepare)

        def tile(j, i, dk, dv, diag):
            ks, qs = pl.ds(pl.multiple_of(j * bk, bk), bk), pl.ds(pl.multiple_of(i * bk, bk), bk)
            kb, vb = mixed[ks, lanes(1)], mixed[ks, lanes(2)]
            dq = None
            for h in range(2):
                qh, doh = qm[h, qs, :], dom[h, qs, :]
                s = mm(kb, qh, NT)
                dp = mm(vb, doh, NT)
                e = jnp.exp2(jnp.abs(s) * SC - lse[x, h:h + 1, qs])
                if diag:
                    e = jnp.where(row <= col, e, 0.0)
                sg = sgn_of(s)
                a = sg * e
                ds = (a * (sg * dp - dsc[h:h + 1, qs])).astype(BF)
                dv = dv + mm(a.astype(BF), doh, NN)
                dk = dk + mm(ds, qh, NN)
                t = mm(ds, km[h, ks, :], TN)
                dq = t if dq is None else dq + t
            dq_acc[qs, :] += dq
            return dk, dv

        def serve(j, i):
            for at_x, at_j, at_i, event in events:
                pl.when((x == at_x) & (j == at_j) & (i == at_i))(event)

        def block(j):
            serve(j, j)
            z = jnp.zeros((bk, 128), F32)
            dk, dv = tile(j, j, z, z, True)

            def more(i, c):
                serve(j, i)
                return tile(j, i, c[0], c[1], False)

            dk, dv = lax.fori_loop(j + 1, n // bk, more, (dk, dv))
            ks = pl.ds(pl.multiple_of(j * bk, bk), bk)
            gm[1, ks, lanes(0)] = (dk * HD ** (-0.5)).astype(BF)
            gm[2, ks, lanes(0)] = dv.astype(BF)

        loop(n // bk, block)
        gm[0, :, lanes(0)] = (dq_acc[...] * HD ** (-0.5)).astype(BF)

    def flat(ref, cols):
        y = ref[:, :, :, cols]
        return y.reshape(n, y.shape[3])

    def weights(x):
        mine = pl.ds(pl.multiple_of(x * 128, 128), 128)
        y = jnp.concatenate([gm[c, :, mine] for c in range(3)], axis=1)

        def tile(i):
            z = mm(flat(full, pl.ds(pl.multiple_of(i * 256, 256), 256)), y, TN).astype(BF)
            for e in range(128 // deep):
                f = i * (128 // deep) + e
                for h in range(2):
                    at = (2 * e + h) * deep
                    for c in range(3):
                        g_triple[x, h, f // p.line, f % p.line, c] = z[
                            at:at + deep, c * 128:(c + 1) * 128
                        ]

        loop(d // 256, tile)
        triple_total(x, 0).start()

    span = lambda k: pl.ds(pl.multiple_of(k * rows, rows), rows)

    def branch_start():
        loads[4].wait()
        loop(CHUNKS, branch.send)

    def out_store(k):
        return Move(pout.at[g.me, k], out_hbm.at[span(k)], out_sem.at[k])

    def branch_end():
        loads[5].wait()

        def one(k):
            pout[g.me, k] = (resid[span(k), :] + branch.final(k) + db[...]).astype(BF)
            out_store(k).start()

        loop(CHUNKS, one)

    span = lambda k: pl.ds(pl.multiple_of(k * rows, rows), rows)

    def branch_start():
        loads[4].wait()
        loop(CHUNKS, branch.send)

    def out_store(k):
        return Move(pout.at[g.me, k], out_hbm.at[span(k)], out_sem.at[k])

    def branch_end():
        loads[5].wait()

        def one(k):
            pout[g.me, k] = (resid[span(k), :] + branch.final(k) + db[...]).astype(BF)
            out_store(k).start()

        loop(CHUNKS, one)

    schedule = [[] for _ in range(pairs)]
    end = pairs - 1
    events = [
        (0, 0, 0, branch_start),
        (0, 0, 2, up_total.scatter),
        (0, 1, 1, shares[0].relay),
        (0, 1, 1, lambda: loop(CHUNKS, branch.combine)),
        (0, 1, 1, early),
        (0, 1, 2, lambda: shares[1].start(p_down1[...])),
        (0, 1, 3, shares[0].spread),
        (0, 1, 3, raw_total.halve),
        (0, 2, 2, up_total.relay),
        (0, 3, 3, shares[1].relay),
        (0, 3, 3, merge_total.start),
        (end, 0, 0, raw_total.relay),
        (end, 0, 1, lambda: shares[2].start(up_total.settle())),
        (end, 0, 1, shares[1].spread),
        (end, 0, 2, totals[1].start),
        (end, 0, 3, lambda: shares[3].start(raw_total.settle())),
        (end, 0, 3, shares[2].relay),
        (end, 1, 1, branch_end),
        (end, 1, 1, totals[0].halve),
        (end, 1, 2, merge_total.halve),
        (end, 1, 3, shares[2].spread),
        (end, 2, 2, shares[3].relay),
        (end, 2, 3, totals[1].halve),
        (end, 2, 3, totals[0].relay),
        (end, 3, 3, merge_total.relay),
        (end, 3, 3, shares[3].spread),
    ]

    def pair(x):
        attention(x, events)

        @pl.when(x < end)
        def _():
            pl.when(x == 0)(lambda: [load.wait() for load in loads[6:]] and None)
            weights(x)

    loop(pairs, pair)

    scatter = Scatter(g, part, in_near, out_far, in_far, sem)

    def back(k):
        def tile(j):
            cols = pl.ds(pl.multiple_of(j * 256, 256), 256)
            z = 0.0
            for c in range(3):
                y = jnp.concatenate(
                    [
                        gm[c, pl.ds(pl.multiple_of((s * CHUNKS + k) * rows, rows), rows), :]
                        for s in range(size)
                    ],
                    axis=0,
                )
                z = z + mm(y, w[c, cols, :], NT)
            for s in range(size):
                part[s, k, :, cols] = z[s * rows:(s + 1) * rows].astype(BF)

        loop(d // 256, tile)
        scatter.send(k)

    near_end, far_end = totals[-2:]
    loop(2, back)
    scatter.combine(0)
    triples[0].start(totals[0].settle())
    scatter.combine(1)
    totals[1].relay()
    weights(end)
    merge_share.start(merge_total.settle())

    def back_step(k):
        back(k)

        @pl.when(k == 2)
        def _():
            far_end.start()
            triples[1].start(totals[1].settle())

    loop_range(2, CHUNKS, back_step)
    scatter.combine(2)
    scatter.combine(3)
    merge_share.relay()
    units = bias_in.shape[1]
    small[6:7, :units] = bias_in[0:1, :]
    for c in range(3):
        small[7:8, c * width:(c + 1) * width] = col_sum(gm[c].astype(F32))
    all_early.start(small[...])
    small[0:2, :] = jnp.zeros((2, d), F32)

    def gtok_store(k):
        return Move(tok.at[span(k)], gtok_hbm.at[span(k)], g_sem.at[k])

    def pull(k):
        gf = scatter.final(k)
        unit, inverse = norm_stats(tok[span(k), :].astype(F32))
        total = gres[span(k), :] + norm_pull(gf, unit, inverse, gain[...])
        tok[span(k), :] = total.astype(BF)
        gtok_store(k).start()
        small[0:1, :] += col_sum(gf * unit)
        small[1:2, :] += col_sum(gf)

    near_end.halve()
    triples[0].relay()
    merge_share.spread()
    far_end.halve()
    near_end.relay()
    triples[1].relay()
    triples[0].spread()

    def pull_step(k):
        pull(k)

        @pl.when(k == 1)
        def _():
            triples[-2].start(near_end.settle())
            far_end.relay()
            triples[1].spread()
            triples[-2].relay()
            triples[-1].start(far_end.settle())

        @pl.when(k == 2)
        def _():
            triples[-2].spread()
            triples[-1].relay()

    loop(CHUNKS, pull_step)
    quarter = d // 4
    group_sum = Everyone("tensor", size, t_buf2, t_sems2)
    all_sum = Everyone("dp", count, d_buf2, d_sems2)
    group_sum.start(
        jnp.concatenate(
            [small[r:r + 1, c * quarter:(c + 1) * quarter] for r in range(2) for c in range(4)],
            axis=0,
        )
    )
    triples[-1].spread()
    all_sum.start(group_sum.finish())
    stores = [
        Move(ref, hbm, o_sem.at[i])
        for i, (ref, hbm) in enumerate(((o_down, down_hbm), (o_up, up_hbm), (o_merge, merge_hbm)))
    ]
    for one, store in ((shares[:2], stores[0]), (shares[2:], stores[1]), ([merge_share], stores[2])):
        for x in one:
            x.finish()
        store.start()
    small[...] = all_early.finish()
    total = all_sum.finish()
    for r in range(2):
        for c in range(4):
            i = 4 * r + c
            small[r:r + 1, c * quarter:(c + 1) * quarter] = total[i:i + 1, :]
    for one in triples:
        one.finish()
    for store in stores:
        store.wait()
    merge_total.drain()
    up_total.drain(False)
    raw_total.drain()
    for t in totals:
        t.drain()
    loop(CHUNKS, scatter.drain)
    loop(CHUNKS, branch.drain)
    loop(CHUNKS, lambda k: gtok_store(k).wait())
    loop(CHUNKS, lambda k: out_store(k).wait())


def late(size, count, gain, db, p_down0, p_down1, u_held, u_raw, g_merge, small_in, bias_in,
         mixed, att, gatt, lse, full, w, tokens, gres, resid, pout):
    rows, d = tokens.shape
    n, width = att.shape
    r = rows // CHUNKS
    line = count // 2
    pairs = width // 128
    bk = min(512, n)
    shape = jax.ShapeDtypeStruct
    piece = d // count
    vm = pltpu.VMEM
    dma = pltpu.SemaphoreType.DMA
    deep = g_merge.shape[2]
    scatter = scatter_scratch(size, r, d)
    loads = (mixed, att, gatt, lse, full, w, tokens, gres, resid, pout)
    return pl.pallas_call(
        functools.partial(late_kernel, size, count, bk),
        out_shape=(
            shape((rows, d), BF),
            shape((rows, d), BF),
            shape((2, 2, line) + p_down1.shape, BF),
            shape((2, 2, line) + u_raw.shape[2:], BF),
            shape(g_merge.shape, BF),
            shape((3, 2, line, piece, width), BF),
            shape((8, d), F32),
        ),
        in_specs=[VMEM_SPEC] * 9 + [ANY_SPEC] * len(loads),
        out_specs=(ANY_SPEC,) * 5 + (VMEM_SPEC,) * 2,
        scratch_shapes=[vm(x.shape, x.dtype) for x in loads]
        + [dma((len(loads),))]
        + [vm((2, n, 128), BF)] * 3
        + [vm((8, n), F32), vm((n, 128), F32), vm((3, n, width), BF)]
        + [vm((pairs, 2, 2, line, 3, piece // 2, 128), BF)]
        + scatter
        + scatter[1:]
        + [sems(size)] * 2
        + total_scratch(line, u_raw.shape[2:])[1:] + total_scratch(line, u_raw.shape[2:])
        + total_scratch(line, (deep, d))
        + [vm((pairs, 2, line, 3, piece // 2, 128), BF)] * 2
        + [dma((pairs, 2, 2, line)), dma((5 + 2 * pairs, 2, line + 1))]
        + [vm((size, 8, d), F32), dma((2, size)), vm((count, 8, d), F32), dma((2, count)), dma((CHUNKS,))]
        + [vm((size, 8, d // 4), F32), dma((2, size)), vm((count, 8, d // 4), F32), dma((2, count))]
        + [vm((2, 2, line) + p_down1.shape, BF), vm((2, 2, line) + u_raw.shape[2:], BF)]
        + [vm(g_merge.shape, BF), dma((3,)), dma((CHUNKS,))],
        compiler_params=pltpu.CompilerParams(
            collective_id=3, has_side_effects=True, vmem_limit_bytes=64 << 20
        ),
        name="late",
    )(gain, db, p_down0, p_down1, u_held, u_raw, g_merge, small_in, bias_in, *loads)


def widen_kernel(down, up, merge, triple, small, out, tok, o_down, o_up, o_merge, o_triple, o_out, o_tok, *o_small):
    for src, dst in ((down, o_down), (up, o_up), (merge, o_merge), (triple, o_triple)):
        dst[...] = src[...].astype(F32)
    o_out[...] = out[...]
    o_tok[...] = tok[...].astype(F32)

    @pl.when(pl.program_id(0) == 0)
    def _():
        for i, dst in enumerate(o_small[:7]):
            dst[...] = small[i:i + 1, :dst.shape[1]]
        width = o_small[7].shape[1]
        for c in range(3):
            o_small[7][c:c + 1, :] = small[7:8, c * width:(c + 1) * width]


def widen(down, up, merge, triple, small, out, tok):
    steps = 2
    d, units, width = small.shape[1], up.shape[1], triple.shape[2]

    def spec(x):
        axis = x.ndim - 2
        block = x.shape[:axis] + (x.shape[axis] // steps, x.shape[-1])
        return pl.BlockSpec(block, lambda i: (0,) * axis + (i, 0))

    def whole(shape):
        return pl.BlockSpec(shape, lambda i: (0, 0))

    arrays = (down, up, merge, triple)
    lines = [(1, d)] * 6 + [(1, units), (3, width)]
    outs = [(x.shape, F32, spec(x)) for x in arrays] + [(out.shape, out.dtype, spec(out)), (tok.shape, F32, spec(tok))]
    outs += [(x, F32, whole(x)) for x in lines]
    return pl.pallas_call(
        widen_kernel,
        grid=(steps,),
        out_shape=tuple(jax.ShapeDtypeStruct(x, t) for x, t, _ in outs),
        in_specs=[spec(x) for x in arrays] + [whole(small.shape), spec(out), spec(tok)],
        out_specs=tuple(x for _, _, x in outs),
        compiler_params=pltpu.CompilerParams(vmem_limit_bytes=60 << 20),
        name="widen",
    )(down, up, merge, triple, small, out, tok)


def on_device(
    tokens,
    first_gain,
    first_shift,
    triple_weight,
    triple_bias,
    merge_weight,
    merge_bias,
    second_gain,
    second_shift,
    up_weight,
    up_bias,
    down_weight,
    down_bias,
    lengths,
    cotangent,
):
    size = lax.axis_size("tensor")
    count = lax.axis_size("dp")
    row_count, d = tokens.shape
    rows = row_count // CHUNKS
    width = triple_weight.shape[2]
    units = up_weight.shape[1]
    n = row_count * size
    fused = (
        count == 8 and units % 512 == 0 and width % 256 == 0 and 3 * width <= d and units <= d
    )
    count = count if fused else 0
    line = lambda v: v.reshape(1, -1)
    w = jnp.transpose(triple_weight, (1, 0, 2))
    full, mixed, attended, log_total, gatt, gres, resid, pout, g_merge, small_b, bias_b, *rest = core(
        size, count, lengths, line(first_gain), line(first_shift), triple_bias, line(merge_bias),
        line(second_gain), line(second_shift), line(up_bias), w, tokens, cotangent, merge_weight,
        up_weight, down_weight,
    )
    gatt = gatt.reshape(n, width)
    if fused:
        output, gtok, down, up, merge, triple, small = late(
            size, count, line(first_gain), line(down_bias), *rest, g_merge, small_b, bias_b,
            mixed, attended, gatt, log_total, full, w, tokens, gres, resid, pout,
        )
        down, up, merge, triple, output, gtok, *small, up_b, triple_b = widen(
            down.reshape(units, d), up.reshape(d, units), merge.reshape(width, d),
            triple.reshape(3, d, width), small, output, gtok,
        )
        triple = jnp.transpose(triple, (1, 0, 2))
        small = [x.reshape(d) for x in small]
        up_b = up_b.reshape(units)
    else:
        branch = lax.psum_scatter(pout.reshape(n, d), "tensor", scatter_dimension=0, tiled=True)
        g_up, g_down = rest
        blocks = lambda x: x.reshape(size, CHUNKS, rows, x.shape[-1])
        dq, dk, dv = attend_bwd(mixed, attended, log_total, gatt)
        gtok, g_triple, small_c, bias_c = tail(
            size, blocks(dq), blocks(dk), blocks(dv), full, w, tokens, gres, line(first_gain)
        )
        merge, up, down, triple = lax.psum((g_merge, g_up, g_down, g_triple), "dp")
        triple_b, up_b = lax.psum((bias_c[0], bias_b[0]), "dp")
        small = lax.psum(small_b + small_c, ("dp", "tensor"))
        triple = jnp.transpose(triple, (1, 0, 2)).astype(F32)
        triple_b = triple_b.reshape(3, width)
        merge, up, down = merge.astype(F32), up.astype(F32), down.astype(F32)
        output = (resid + branch.astype(F32) + down_bias).astype(BF)
    return (
        output,
        gtok,
        small[0],
        small[1],
        triple,
        triple_b,
        merge,
        small[2],
        small[3],
        small[4],
        up,
        up_b,
        down,
        small[5],
    )


def solution(mesh):
    in_specs = (
        P(("dp", "tensor"), None),
        P(),
        P(),
        P(None, None, "tensor"),
        P(None, "tensor"),
        P("tensor", None),
        P(),
        P(),
        P(),
        P(None, "tensor"),
        P("tensor"),
        P("tensor", None),
        P(),
        P("dp"),
        P(("dp", "tensor"), None),
    )
    out_specs = (
        P(("dp", "tensor"), None),
        P(("dp", "tensor"), None),
        P(),
        P(),
        P(None, None, "tensor"),
        P(None, "tensor"),
        P("tensor", None),
        P(),
        P(),
        P(),
        P(None, "tensor"),
        P("tensor"),
        P("tensor", None),
        P(),
    )
    return jax.shard_map(
        on_device, mesh=mesh, in_specs=in_specs, out_specs=out_specs, check_vma=False
    )
```
